512 devices in a mesh: gx: 32 (over z_hi, y, core), gy: 16 (over x, z_lo).
Axes of the slice: x: 4, y: 4, z: 16 (z_hi: 4, z_lo: 4; z = z_hi * 4 + z_lo), core: 2. Of those that a mesh axis runs over, the one named last changes fastest.
Arguments:
- particles: float32 [7, 8388608], P(None, ('gx', 'gy')), may hold values from -3 to 3, as said below
- mig_count: int32 [512, 4], P(('gx', 'gy')), may hold values from 1 to 512, as said below
- mig_rows: int32 [512, 4, 512], P(('gx', 'gy')), may hold values from 0 to 16383, as said below
- active_ids: int32 [512, 2, 8], P(('gx', 'gy')), may hold values from 0 to 127, as said below
- active_count: int32 [512, 2], P(('gx', 'gy')), may hold values from 1 to 8, as said below
- local_nbrs: int32 [512, 2, 8, 3], P(('gx', 'gy')), may hold values from 0 to 127
- ghost_slots: int32 [512, 2, 8, 4], P(('gx', 'gy')), may hold values from 0 to 127
- export_blocks: int32 [512, 16, 8], P(('gx', 'gy')), may hold values from 0 to 127
Outputs:
- density: float32 [8388608], P(('gx', 'gy'))
- accel: float32 [3, 8388608], P(None, ('gx', 'gy'))
The draws below stay inside these ranges and needn't reach their ends.
Inputs may be any that keep to these rules, and one draw needn't show every extreme that they name: `mig_count`: each level's count is the same for both devices of a pair, and device 0 and its partners exchange exactly 512 at every level. `mig_rows`: the slots of one device at one level are distinct. `active_ids`: the 16 ids of one device are distinct. `active_count`: the two bins of one device hold at most 12 blocks together; device 0 holds 8 in bin 0 and 12 in all. `particles`: Rows: positions first, then mass, smoothing length, internal energy and previous density, these four positive.
All inputs are finite; a program needn't handle non-finite values.
Results may differ from the reference program's by a relative error of at most 0.00002.
Values sent between devices are 32-bit elements; how exact they have to be, the bound alone decides.
A program may use at most 128 MiB of HBM per device.

```python
import math
import jax
import jax.numpy as jnp
from jax import lax

BLK = 128
NB = 128
MIG = 512
NACT = 8
TOTACT = 12
NLOC = 3
NGH = 4
SLOTS = 8
PEERS = 16
PER_DEV = 16384
PARTICLES = 8388608
DEVICES = 512


def log_draw(subkey, low_end, high_end):
    unit = jax.random.uniform(subkey, (1, PARTICLES), jnp.float32)
    return low_end * jnp.exp(unit * jnp.log(high_end / low_end))


def draw_particles(key, part):
    subkeys = jax.random.split(key, 5)
    places = jnp.clip(0.5 * jax.random.normal(subkeys[0], (3, PARTICLES), jnp.float32), -3.0, 3.0)
    masses = log_draw(subkeys[1], 0.004, 0.016)
    smooth = log_draw(subkeys[2], 0.5, 1.0)
    energy = log_draw(subkeys[3], 0.5, 2.0)
    previous = log_draw(subkeys[4], 0.2, 2.0)
    return jnp.concatenate([places, masses, smooth, energy, previous], axis=0)


def draw_mig_count(key, part):
    raw_counts = jax.random.randint(key, (DEVICES, 4), 1, MIG + 1)
    raw_counts = raw_counts.at[0].set(MIG)
    device = jnp.arange(DEVICES, dtype=jnp.int32)
    partners = jnp.stack([device ^ 2 * PEERS, device ^ PEERS, device ^ 2, device ^ 1], axis=1)
    mirrored = raw_counts[partners, jnp.arange(4, dtype=jnp.int32)[None, :]]
    return jnp.maximum(raw_counts, mirrored)


def draw_mig_rows(key, part):
    subkeys = jax.random.split(key, DEVICES * 4)
    chosen = jax.vmap(lambda one_key: jax.random.permutation(one_key, PER_DEV)[:MIG])(subkeys)
    return chosen.reshape(DEVICES, 4, MIG).astype(jnp.int32)


def draw_active_ids(key, part):
    subkeys = jax.random.split(key, DEVICES)
    chosen = jax.vmap(lambda one_key: jax.random.permutation(one_key, NB)[:2 * NACT])(subkeys)
    return chosen.reshape(DEVICES, 2, NACT).astype(jnp.int32)


def draw_active_count(key, part):
    subkeys = jax.random.split(key, 2)
    first_bin = jax.random.randint(subkeys[0], (DEVICES,), 1, NACT + 1)
    second_bin = jax.random.randint(subkeys[1], (DEVICES,), 1, NACT + 1)
    second_bin = jnp.minimum(second_bin, TOTACT - first_bin)
    first_bin = first_bin.at[0].set(NACT)
    second_bin = second_bin.at[0].set(TOTACT - NACT)
    return jnp.stack([first_bin, second_bin], axis=1).astype(jnp.int32)


def touch_ends(entries, key, smallest, top_value):
    place = [jax.random.randint(jax.random.fold_in(key, axis), (), 0, length) for axis, length in enumerate(entries.shape)]
    widest = entries.shape.index(max(entries.shape))
    next_to = place[:widest] + [(place[widest] + 1) % entries.shape[widest]] + place[widest + 1:]
    return entries.at[tuple(place)].set(smallest).at[tuple(next_to)].set(top_value)


def setup_inputs(seed: int = 0) -> dict:
    arg_keys = jax.random.split(jax.random.key(seed), 9)
    return {
        "particles": draw_particles(jax.random.fold_in(arg_keys[8], 71), 0),
        "mig_count": draw_mig_count(jax.random.fold_in(arg_keys[8], 71), 0),
        "mig_rows": draw_mig_rows(jax.random.fold_in(arg_keys[8], 71), 0),
        "active_ids": draw_active_ids(jax.random.fold_in(arg_keys[8], 71), 0),
        "active_count": draw_active_count(jax.random.fold_in(arg_keys[8], 71), 0),
        "local_nbrs": touch_ends(jax.random.randint(arg_keys[5], (DEVICES, 2, NACT, NLOC), 0, NB), jax.random.fold_in(arg_keys[5], 1), 0, NB - 1).astype(jnp.int32),
        "ghost_slots": touch_ends(jax.random.randint(arg_keys[6], (DEVICES, 2, NACT, NGH), 0, PEERS * SLOTS), jax.random.fold_in(arg_keys[6], 1), 0, (PEERS * SLOTS) - 1).astype(jnp.int32),
        "export_blocks": touch_ends(jax.random.randint(arg_keys[7], (DEVICES, PEERS, SLOTS), 0, NB), jax.random.fold_in(arg_keys[7], 1), 0, NB - 1).astype(jnp.int32),
    }


KERNEL_NORM = 21.0 / (16.0 * math.pi)
GAMMA_LESS = 2.0 / 3.0

def density_tile(centre_pos, smooth, others):
    offset = centre_pos[:, :, None] - others[0:3, None, :]
    distance = jnp.sqrt(lax.optimization_barrier(jnp.sum(offset * offset, axis=0)))
    scaled = distance / smooth[:, None]
    falloff = jnp.maximum(1.0 - 0.5 * scaled, 0.0)
    square = falloff * falloff
    kernel = KERNEL_NORM / (smooth * smooth * smooth)[:, None] * (square * square) * (1.0 + 2.0 * scaled)
    return lax.optimization_barrier(jnp.sum(kernel * others[3][None, :], axis=1))

def pair_force(centre, others):
    offset = centre[0:3, :, None] - others[0:3, None, :]
    distance = jnp.sqrt(lax.optimization_barrier(jnp.sum(offset * offset, axis=0)))
    pair_smooth = 0.5 * (centre[4][:, None] + others[4][None, :])
    scaled = distance / pair_smooth
    falloff = jnp.maximum(1.0 - 0.5 * scaled, 0.0)
    inverse = 1.0 / pair_smooth
    inv_square = inverse * inverse
    gradient = -5.0 * KERNEL_NORM * (falloff * falloff * falloff) * (inv_square * inv_square * inverse)
    pressure = GAMMA_LESS * (centre[5] / centre[6])[:, None] + GAMMA_LESS * (others[5] / others[6])[None, :]
    weight = -(centre[3][:, None] * others[3][None, :]) * pressure * gradient
    pushes = weight[None] * offset
    return (lax.optimization_barrier(jnp.sum(pushes, axis=2)), -lax.optimization_barrier(jnp.sum(pushes, axis=1)))

def slot_densities(own_blocks, ghosts, slot_ids, near_ids, far_ids):

    def per_slot(inputs):
        active, near, far = inputs
        centre = own_blocks[active]
        neighbours = jnp.concatenate([centre[None, 0:4], own_blocks[near][:, 0:4], ghosts[far][:, 0:4]], axis=0)
        tile_sums = jax.vmap(lambda block_row: density_tile(centre[0:3], centre[4], block_row))(neighbours)
        return lax.optimization_barrier(jnp.sum(tile_sums, axis=0))
    return lax.map(per_slot, (slot_ids, near_ids, far_ids))

def slot_forces(own_blocks, ghosts, slot_ids, near_ids, far_ids, live_slot):

    def per_slot(inputs):
        active, near, far, alive = inputs
        centre = own_blocks[active]
        neighbours = jnp.concatenate([own_blocks[near], ghosts[far]], axis=0)
        self_push = pair_force(centre, centre)[0]
        on_centre, on_others = jax.vmap(lambda block_row: pair_force(centre, block_row))(neighbours)
        factor = jnp.where(alive, 1.0, 0.0).astype(jnp.float32)
        count_near = near.shape[0]
        centre_sum = (self_push + lax.optimization_barrier(jnp.sum(on_centre, axis=0))) * factor
        return (centre_sum, on_others[:count_near] * factor, on_others[count_near:] * factor)
    return lax.map(per_slot, (slot_ids, near_ids, far_ids, live_slot))

def migrate(current, mig_count, mig_rows):
    device = jnp.arange(DEVICES, dtype=jnp.int32)
    partners = (device ^ 2 * PEERS, device ^ PEERS, device ^ 2, device ^ 1)
    lane_ids = jnp.arange(MIG, dtype=jnp.int32)
    for section_num in range(4):
        moving_rows = mig_rows[:, section_num, :]
        outgoing = jnp.take_along_axis(current, moving_rows[None], axis=2)
        arrived = outgoing[:, partners[section_num], :]
        staying = lane_ids[None, :] < mig_count[:, section_num][:, None]
        settled = jnp.where(staying[None], arrived, outgoing)
        current = current.at[:, device[:, None], moving_rows].set(settled)
    return current

def reference(particles, mig_count, mig_rows, active_ids, active_count, local_nbrs, ghost_slots, export_blocks):
    current = migrate(particles.reshape(7, DEVICES, PER_DEV), mig_count, mig_rows)
    blocks = current.reshape(7, DEVICES, NB, BLK).transpose(1, 2, 0, 3)
    device = jnp.arange(DEVICES, dtype=jnp.int32)
    owners = (device // PEERS)[:, None] * PEERS + jnp.arange(PEERS, dtype=jnp.int32)[None, :]
    exported = export_blocks[owners[:, :, None], (device % PEERS)[:, None, None], jnp.arange(SLOTS, dtype=jnp.int32)[None, None, :]]
    slot_ids = active_ids.reshape(DEVICES, 2 * NACT)
    live_slot = (jnp.arange(NACT, dtype=jnp.int32)[None, None, :] < active_count[:, :, None]).reshape(DEVICES, 2 * NACT)
    near_ids = local_nbrs.reshape(DEVICES, 2 * NACT, NLOC)
    far_ids = ghost_slots.reshape(DEVICES, 2 * NACT, NGH)

    def fetch_ghosts(source, device_id):
        return source[owners[device_id][:, None], exported[device_id]].reshape(PEERS * SLOTS, 7, BLK)

    def densities(device_id):
        ghosts = fetch_ghosts(blocks, device_id)
        own_blocks = blocks[device_id]
        fresh = slot_densities(own_blocks, ghosts, slot_ids[device_id], near_ids[device_id], far_ids[device_id])
        previous = own_blocks[:, 6]
        chosen = slot_ids[device_id]
        return previous.at[chosen].set(jnp.where(live_slot[device_id][:, None], fresh, previous[chosen]))
    density_all = lax.map(densities, device)
    blocks = blocks.at[:, :, 6].set(density_all)

    def forces(device_id):
        ghosts = fetch_ghosts(blocks, device_id)
        own_blocks = blocks[device_id]
        on_centre, on_near, on_far = slot_forces(own_blocks, ghosts, slot_ids[device_id], near_ids[device_id], far_ids[device_id], live_slot[device_id])
        totals = jnp.zeros((NB, 3, BLK), dtype=jnp.float32).at[slot_ids[device_id]].add(on_centre)
        totals = totals.at[near_ids[device_id].reshape(-1)].add(on_near.reshape(-1, 3, BLK))
        returned = jnp.zeros((PEERS * SLOTS, 3, BLK), dtype=jnp.float32).at[far_ids[device_id].reshape(-1)].add(on_far.reshape(-1, 3, BLK))
        return (totals, returned)
    totals, returned = lax.map(forces, device)
    totals = totals.at[owners[:, :, None], exported].add(returned.reshape(DEVICES, PEERS, SLOTS, 3, BLK))
    accel = totals / blocks[:, :, 3][:, :, None, :]
    return (blocks[:, :, 6].reshape(-1), accel.transpose(2, 0, 1, 3).reshape(3, -1))
```

```python
import functools
import math

import jax
import jax.numpy as jnp
from jax import lax
from jax.experimental import pallas as pl
from jax.experimental.pallas import tpu as pltpu
from jax.sharding import PartitionSpec as P

BLK = 128
TOTACT = 12
LEVELS = 4
CHAN = 8
SENT = 6

KERNEL_NORM = 21.0 / (16.0 * math.pi)
GAMMA_LESS = 2.0 / 3.0
TINY = 1e-37
MESH = pl.DeviceIdType.MESH
VMEM = pltpu.VMEM
SMEM = pltpu.SMEM
F32 = jnp.float32
I32 = jnp.int32


def lanes(shape):
    return lax.broadcasted_iota(I32, shape, len(shape) - 1)


def spec(space):
    return pl.BlockSpec(memory_space=space)


def flipped(index, bit):
    return index + bit - 2 * bit * (lax.div(index, bit) % 2)


def gather_kernel(rows_ref, x_ref, out_ref):
    lane = lanes((7, BLK))
    chunks = out_ref.shape[2] // BLK

    def chunk(n, _):
        level, base = n // chunks, (n % chunks) * BLK

        def step(k8, held):
            for k in range(8):
                slot = k8 * 8 + k
                row = rows_ref[0, level, base + slot]
                start = pl.multiple_of((row >> 7) * BLK, BLK)
                tile = x_ref[:, pl.ds(start, BLK)]
                tile = pltpu.roll(tile, (slot - (row & 127)) & 127, 1)
                held = jnp.where(lane == slot, tile, held)
            return held

        held = lax.fori_loop(0, BLK // 8, step, jnp.zeros((7, BLK), F32))
        out_ref[level, 0:7, pl.ds(pl.multiple_of(base, BLK), BLK)] = held
        out_ref[level, 7:8, pl.ds(pl.multiple_of(base, BLK), BLK)] = jnp.zeros((1, BLK), F32)
        return 0

    lax.fori_loop(0, LEVELS * chunks, chunk, 0)


def pieces(value):
    first = value.astype(jnp.bfloat16).astype(F32)
    rest = value - first
    second = rest.astype(jnp.bfloat16).astype(F32)
    return first, second, rest - second


def migrate_kernel(count_ref, rows_ref, first_ref, out_ref, leaving, landed, match, ssem, rsem):
    gx, gy = lax.axis_index("gx"), lax.axis_index("gy")
    partners = [(flipped(gx, 2), gy), (flipped(gx, 1), gy), (gx, flipped(gy, 2)), (gx, flipped(gy, 1))]
    barrier = pltpu.get_barrier_semaphore()
    for partner in partners:
        pl.semaphore_signal(barrier, inc=1, device_id=partner, device_id_type=MESH)
    pl.semaphore_wait(barrier, LEVELS)

    def copy(level):
        return pltpu.make_async_remote_copy(
            src_ref=(first_ref if level == 0 else leaving).at[level],
            dst_ref=landed.at[level],
            send_sem=ssem.at[level],
            recv_sem=rsem.at[level],
            device_id=partners[level],
            device_id_type=MESH,
        )

    width = rows_ref.shape[2]
    first = copy(0)
    first.start()
    rows = [rows_ref[0, level : level + 1, :] for level in range(LEVELS)]
    pair = {}
    for early in range(LEVELS - 1):
        used = lanes((1, width)) < count_ref[0, early]
        keys = jnp.where(used, rows[early], -1).astype(F32)
        for late in range(early + 1, LEVELS):
            pair[late, early] = len(pair)
        for part in range(width // BLK):
            across = jnp.broadcast_to(keys[:, part * BLK : (part + 1) * BLK], (BLK, BLK))
            down = jnp.transpose(across)
            down = jnp.concatenate([down] * (width // BLK), axis=1)
            for late in range(early + 1, LEVELS):
                same = down == rows[late].astype(F32)
                match[pair[late, early], part * BLK : (part + 1) * BLK, :] = jnp.where(same, 1.0, 0.0).astype(
                    jnp.bfloat16
                )
    first.wait()
    factors = []
    for level in range(1, LEVELS):
        hi, mid, lo = pieces(landed[level - 1])
        factors.append(
            jnp.concatenate([hi, mid, lo, jnp.ones((8, width), F32)], axis=0).astype(jnp.bfloat16)
        )
        out = first_ref[level]
        for early in range(level):
            found = jnp.dot(factors[early], match[pair[level, early]], preferred_element_type=F32)
            value = (found[0:8] + found[8:16]) + found[16:24]
            out = jnp.where(found[24:32] > 0.5, value, out)
        leaving[level] = out
        moving = copy(level)
        moving.start()
        moving.wait()
    out_ref[...] = landed[...]


def place_kernel(
    rows_ref, count_ref, ids_ref, live_ref, near_ref, far_ref, exp_ref, x_ref, landed_ref,
    tiles_ref, stage_ref, prev_ref, expcol_ref, table_ref, centres_ref, act_out, near_out, far_out,
):
    blocks = x_ref.shape[1] // BLK
    peers = exp_ref.shape[1]
    slots = exp_ref.shape[2]
    lane = lanes((CHAN, BLK))

    def load(b8, _):
        for k in range(8):
            b = b8 * 8 + k
            tiles_ref[pl.ds(b * CHAN, 7), :] = x_ref[:, pl.ds(pl.multiple_of(b * BLK, BLK), BLK)]
        return 0

    lax.fori_loop(0, blocks // 8, load, 0)
    tiles_ref[pl.ds(7, blocks, stride=CHAN), :] = jnp.zeros((blocks, BLK), F32)
    chunks = landed_ref.shape[2] // BLK

    def chunk(n, _):
        level, base = n // chunks, (n % chunks) * BLK
        held = landed_ref[level, :, pl.ds(pl.multiple_of(base, BLK), BLK)]
        count = count_ref[0, level] - base

        def step(k8, _):
            for k in range(8):
                slot = k8 * 8 + k
                row = rows_ref[0, level, base + slot]
                spot = row & 127
                turned = pltpu.roll(held, (spot - slot) & 127, 1)
                spot = jnp.where(slot < count, spot, -1)
                pltpu.store(
                    tiles_ref.at[pl.ds(pl.multiple_of((row >> 7) * CHAN, CHAN), CHAN), :],
                    turned,
                    mask=lane == spot,
                )
            return 0

        lax.fori_loop(0, BLK // 8, step, 0)
        return 0

    lax.fori_loop(0, LEVELS * chunks, chunk, 0)

    wide = lanes((1, BLK))

    def pack(p, ids):
        for t in range(slots):
            block = exp_ref[0, p, t]
            tile = tiles_ref[pl.ds(pl.multiple_of(block * CHAN, CHAN), CHAN), :]
            stage_ref[pl.ds(p * (SENT * slots) + t, SENT, stride=slots), :] = tile[0:SENT]
            prev_ref[pl.ds(p * slots + t, 1), :] = tile[6:7]
            expcol_ref[pl.ds(p * slots + t, 1), :] = jnp.full((1, BLK), block, I32)
            ids = jnp.where(wide == p * slots + t, block, ids)
        return ids

    export_ids = lax.fori_loop(0, peers, pack, jnp.full((1, BLK), -1, I32))
    in_first = live_ref[0, 0]
    in_all = in_first + live_ref[0, 1]
    near_count = near_ref.shape[3]
    far_count = far_ref.shape[3]

    def compact(p, carry):
        centre, far = carry
        n = jnp.where(p < in_first, 0, 1)
        i = jnp.minimum(jnp.where(p < in_first, p, p - in_first), ids_ref.shape[2] - 1)
        alive = p < in_all
        block = ids_ref[0, n, i]
        act_out[2 * p] = block
        tile = tiles_ref[pl.ds(pl.multiple_of(block * CHAN, CHAN), CHAN), :]
        centres_ref[pl.ds(pl.multiple_of(p * CHAN, CHAN), 7), :] = tile[0:7]
        centres_ref[pl.ds(p * CHAN + 7, 1), :] = 0.5 / tile[4:5]
        act_out[2 * p + 1] = jnp.where(alive, block, -1)
        centre = jnp.where(wide == p, jnp.where(alive, block, -1), centre)
        for k in range(near_count):
            other = near_ref[0, n, i, k]
            near_out[p * near_count + k] = other
            centre = jnp.where(wide == TOTACT + p * near_count + k, jnp.where(alive, other, -1), centre)
        for k in range(far_count):
            other = far_ref[0, n, i, k]
            far_out[2 * (p * far_count + k)] = other
            far_out[2 * (p * far_count + k) + 1] = (other // slots) * (SENT * slots) + other % slots
            far = jnp.where(wide == p * far_count + k, jnp.where(alive, other, -1), far)
        return centre, far

    centres_ref[TOTACT * CHAN :, :] = jnp.zeros((BLK - TOTACT * CHAN, BLK), F32)
    empty = jnp.full((1, BLK), -1, I32)
    centre_ids, far_ids = lax.fori_loop(0, TOTACT, compact, (empty, empty))
    table_ref[0:1, :] = centre_ids
    table_ref[1:2, :] = far_ids
    table_ref[2:3, :] = export_ids
    table_ref[3:8, :] = jnp.full((5, BLK), -1, I32)


def picked(chunk, lane_number):
    return jnp.take_along_axis(chunk, jnp.full(chunk.shape, lane_number, I32), axis=1)


def abreast(ref):
    return jnp.concatenate([ref[0], ref[1], ref[2]], axis=1)


def exact_dot(left, right):
    return lax.dot_general(
        left, right, (((1,), (0,)), ((), ())), precision=lax.Precision.HIGHEST, preferred_element_type=F32
    )


def pairs_kernel(
    act_ref, near_ref, far_ref, tiles_ref, stage_ref, prev_ref, expcol_ref, table_ref, centres_in,
    dens_out, adds_out, back_out,
    ghosts, ghost_dens, dens_stage, back_stage, back_land, centres, cols, sums, dist, rhos, pj, pg, adds, fars, forces,
    ssem, rsem,
):
    gx, me = lax.axis_index("gx"), lax.axis_index("gy")
    peers = lax.axis_size("gy")
    slots = stage_ref.shape[0] // (peers * SENT)
    block_count = dens_out.shape[0]
    near_count = near_ref.shape[0] // TOTACT
    far_count = far_ref.shape[0] // (2 * TOTACT)
    lane8 = lanes((8, BLK))

    barrier = pltpu.get_barrier_semaphore()
    for apart in range(1, peers):
        pl.semaphore_signal(barrier, inc=1, device_id=(gx, lax.rem(me + apart, peers)), device_id_type=MESH)
    pl.semaphore_wait(barrier, peers - 1)

    def exchange(phase, source, target, rows):
        copies = []
        for apart in range(1, peers):
            peer = lax.rem(me + apart, peers)
            copies.append(
                pltpu.make_async_remote_copy(
                    src_ref=source.at[pl.ds(peer * rows, rows), :],
                    dst_ref=target.at[pl.ds(me * rows, rows), :],
                    send_sem=ssem.at[phase, apart - 1],
                    recv_sem=rsem.at[phase, apart - 1],
                    device_id=(gx, peer),
                    device_id_type=MESH,
                )
            )
        for moving in copies:
            moving.start()
        return copies

    def finish(copies, source, target, rows):
        here = pl.ds(me * rows, rows)
        target[here, :] = source[here, :]
        for moving in copies:
            moving.wait()

    sent_blocks = exchange(0, stage_ref, ghosts, SENT * slots)

    centres[...] = centres_in[...]
    cols[...] = jnp.transpose(centres[...])

    def local_row(block, channel):
        return jnp.broadcast_to(tiles_ref[pl.ds(block * CHAN + channel, 1), :], (8, BLK))

    def ghost_row(base, channel):
        return jnp.broadcast_to(ghosts[pl.ds(base + channel * slots, 1), :], (8, BLK))

    def density_phase(p, first, rows, then):
        def chunk(q, _):
            part = cols[pl.ds(pl.multiple_of(q * 8, 8), 8), :]
            cx, cy, cz = (picked(part, p * CHAN + c) for c in range(3))
            inverse = picked(part, p * CHAN + 7)
            total = None
            for n, (x, y, z, mass) in enumerate(rows):
                dx, dy, dz = cx - x, cy - y, cz - z
                square = dx * dx + dy * dy + dz * dz
                r = square * lax.rsqrt(jnp.maximum(square, TINY))
                dist[p, first + n, pl.ds(pl.multiple_of(q * 8, 8), 8), :] = r
                half = r * inverse
                fall = jnp.maximum(1.0 - half, 0.0)
                fall = fall * fall
                term = (fall * fall) * (1.0 + 4.0 * half) * mass
                total = term if total is None else total + term
            then(q, part, total)
            return 0

        lax.fori_loop(0, BLK // 8, chunk, 0)

    def local_density(p, _):
        blocks = [act_ref[2 * p]] + [near_ref[p * near_count + k] for k in range(near_count)]

        def then(q, part, total):
            sums[p, pl.ds(pl.multiple_of(q * 8, 8), 8), :] = total

        density_phase(p, 0, [[local_row(b, c) for c in range(4)] for b in blocks], then)
        return 0

    lax.fori_loop(0, TOTACT, local_density, 0)
    finish(sent_blocks, stage_ref, ghosts, SENT * slots)
    rhos[...] = jnp.zeros_like(rhos)

    def ghost_density(p, _):
        others = [far_ref[2 * (p * far_count + k) + 1] for k in range(far_count)]

        def then(q, part, total):
            here = pl.ds(pl.multiple_of(q * 8, 8), 8)
            smooth = picked(part, p * CHAN + 4)
            total = jnp.sum(total + sums[p, here, :], axis=1, keepdims=True)
            rho = KERNEL_NORM / (smooth * smooth * smooth) * total
            rhos[here, :] = jnp.where(lane8 == p, rho, rhos[here, :])

        density_phase(p, 1 + near_count, [[ghost_row(g, c) for c in range(4)] for g in others], then)
        return 0

    lax.fori_loop(0, TOTACT, ghost_density, 0)
    fresh = jnp.transpose(rhos[...])
    rhos[...] = fresh
    block_number = lax.broadcasted_iota(I32, (block_count, BLK), 0)
    dens = tiles_ref[pl.ds(6, block_count, stride=CHAN), :]
    exported = prev_ref[...]
    export_block = expcol_ref[...]
    for p in range(TOTACT):
        block = act_ref[2 * p + 1]
        exported = jnp.where(export_block == block, fresh[p : p + 1, :], exported)
    dens_stage[...] = exported
    sent_dens = exchange(1, dens_stage, ghost_dens, slots)
    for p in range(TOTACT):
        block = act_ref[2 * p + 1]
        dens = jnp.where(block_number == block, fresh[p : p + 1, :], dens)
    dens_out[...] = dens
    pj[...] = GAMMA_LESS * (tiles_ref[pl.ds(5, block_count, stride=CHAN), :] / dens)
    for p in range(TOTACT):
        centres[p * CHAN + 6 : p * CHAN + 7, :] = (
            GAMMA_LESS * 32.0 * 5.0 * KERNEL_NORM * (centres[p * CHAN + 5 : p * CHAN + 6, :] / fresh[p : p + 1, :])
        )
    pj[...] = (32.0 * 5.0 * KERNEL_NORM) * pj[...]
    cols[...] = jnp.transpose(centres[...])
    forces[...] = jnp.zeros_like(forces)

    def force_phase(p, first, rows, skip):
        kept = len(rows) - skip

        def chunk(q, carry):
            here = pl.ds(pl.multiple_of(q * 8, 8), 8)
            part = cols[here, :]
            cx, cy, cz, cm, ch, _, cp = (picked(part, p * CHAN + c) for c in range(7))
            total = [None] * 3
            carry = list(carry)
            for n, (x, y, z, mass, smooth, pressure) in enumerate(rows):
                inverse = 1.0 / (ch + smooth)
                fall = jnp.maximum(1.0 - dist[p, first + n, here, :] * inverse, 0.0) * inverse
                scale = (fall * fall) * fall * (inverse * inverse)
                weight = scale * ((cm * mass) * (cp + pressure))
                for c, (mine, theirs) in enumerate(((cx, x), (cy, y), (cz, z))):
                    push = weight * (mine - theirs)
                    total[c] = push if total[c] is None else total[c] + push
                    if n >= skip:
                        carry[(n - skip) * 3 + c] = carry[(n - skip) * 3 + c] + push
            held = forces[here, :]
            for c in range(3):
                whole = jnp.sum(total[c], axis=1, keepdims=True)
                held = jnp.where(lane8 == 3 * p + c, held + whole, held)
            forces[here, :] = held
            return tuple(carry)

        done = lax.fori_loop(0, BLK // 8, chunk, (jnp.zeros((8, BLK), F32),) * (3 * kept))
        return [[-jnp.sum(done[n * 3 + c], axis=0, keepdims=True) for c in range(3)] for n in range(kept)]

    adds[...] = jnp.zeros_like(adds)
    fars[...] = jnp.zeros_like(fars)

    def local_force(p, _):
        blocks = [act_ref[2 * p]] + [near_ref[p * near_count + k] for k in range(near_count)]
        rows = [
            [local_row(b, c) for c in range(5)] + [jnp.broadcast_to(pj[pl.ds(b, 1), :], (8, BLK))] for b in blocks
        ]
        found = force_phase(p, 0, rows, 1)
        for n in range(near_count):
            for c in range(3):
                adds[c, pl.ds(TOTACT + p * near_count + n, 1), :] = found[n][c]
        return 0

    lax.fori_loop(0, TOTACT, local_force, 0)
    finish(sent_dens, dens_stage, ghost_dens, slots)
    for s in range(peers):
        energy = ghosts[s * SENT * slots + 5 * slots : s * SENT * slots + 6 * slots, :]
        pg[s * slots : (s + 1) * slots, :] = (GAMMA_LESS * 32.0 * 5.0 * KERNEL_NORM) * (
            energy / ghost_dens[s * slots : (s + 1) * slots, :]
        )

    def ghost_force(p, _):
        others = [[far_ref[2 * (p * far_count + k) + i] for i in range(2)] for k in range(far_count)]
        rows = [
            [ghost_row(base, c) for c in range(5)] + [jnp.broadcast_to(pg[pl.ds(g, 1), :], (8, BLK))]
            for g, base in others
        ]
        found = force_phase(p, 1 + near_count, rows, 0)
        for n in range(far_count):
            for c in range(3):
                fars[c, pl.ds(p * far_count + n, 1), :] = found[n][c]
        return 0

    lax.fori_loop(0, TOTACT, ghost_force, 0)
    ghost_number = lax.broadcasted_iota(I32, (peers * slots, BLK), 0)
    chosen = jnp.where(ghost_number == table_ref[1:2, :], 1.0, 0.0)
    back_stage[...] = exact_dot(chosen, abreast(fars))
    sent_back = exchange(2, back_stage, back_land, slots)
    turned = jnp.transpose(forces[...])
    for p in range(TOTACT):
        for c in range(3):
            adds[c, p : p + 1, :] = turned[3 * p + c : 3 * p + c + 1, :]
    adds_out[...] = adds[...]
    finish(sent_back, back_stage, back_land, slots)
    back_out[...] = back_land[...]


def finish_kernel(table_ref, tiles_ref, dens_ref, adds_ref, back_ref, dens_out, accel_out, held):
    block_count = dens_ref.shape[0]
    block_number = lax.broadcasted_iota(I32, (block_count, BLK), 0)
    own = jnp.where(block_number == table_ref[0:1, :], 1.0, 0.0)
    sent = jnp.where(block_number == table_ref[2:3, :], 1.0, 0.0)
    totals = exact_dot(own, abreast(adds_ref)) + exact_dot(sent, back_ref[...])
    mass = tiles_ref[pl.ds(3, block_count, stride=CHAN), :]
    for c in range(3):
        held[c] = totals[:, c * BLK : (c + 1) * BLK] / mass
    dens_out[...] = dens_ref[...]

    def put(b8, _):
        for k in range(8):
            b = b8 * 8 + k
            for c in range(3):
                accel_out[c : c + 1, pl.ds(pl.multiple_of(b * BLK, BLK), BLK)] = held[c, pl.ds(b, 1), :]
        return 0

    lax.fori_loop(0, block_count // 8, put, 0)


def shards(
    particles, mig_count, mig_rows, active_ids, active_count, local_nbrs, ghost_slots, export_blocks
):
    count = particles.shape[1]
    blocks = count // BLK
    width = mig_rows.shape[2]
    peers, slots = export_blocks.shape[1:]
    near_count, far_count = local_nbrs.shape[3], ghost_slots.shape[3]
    limit = 60 * 1024 * 1024
    struct = jax.ShapeDtypeStruct
    outgoing = pl.pallas_call(
        gather_kernel,
        name="gather_rows",
        out_shape=struct((LEVELS, CHAN, width), F32),
        in_specs=[spec(SMEM), spec(VMEM)],
        out_specs=spec(VMEM),
        compiler_params=pltpu.CompilerParams(vmem_limit_bytes=limit),
    )(mig_rows, particles)
    landed = pl.pallas_call(
        migrate_kernel,
        name="migrate",
        out_shape=struct((LEVELS, CHAN, width), F32),
        in_specs=[spec(SMEM), spec(VMEM), spec(VMEM)],
        out_specs=spec(VMEM),
        scratch_shapes=[
            VMEM((LEVELS, CHAN, width), F32),
            VMEM((LEVELS, CHAN, width), F32),
            VMEM((6, width, width), jnp.bfloat16),
            pltpu.SemaphoreType.DMA((LEVELS,)),
            pltpu.SemaphoreType.DMA((LEVELS,)),
        ],
        compiler_params=pltpu.CompilerParams(collective_id=0, has_side_effects=True, vmem_limit_bytes=limit),
    )(mig_count, mig_rows, outgoing)
    tiles, stage, prev, expcol, table, centres, act, near, far = pl.pallas_call(
        place_kernel,
        name="place",
        out_shape=(
            struct((blocks * CHAN, BLK), F32),
            struct((peers * SENT * slots, BLK), F32),
            struct((peers * slots, BLK), F32),
            struct((peers * slots, BLK), I32),
            struct((8, BLK), I32),
            struct((BLK, BLK), F32),
            struct((2 * TOTACT,), I32),
            struct((TOTACT * near_count,), I32),
            struct((2 * TOTACT * far_count,), I32),
        ),
        in_specs=[spec(SMEM)] * 7 + [spec(VMEM)] * 2,
        out_specs=(spec(VMEM),) * 6 + (spec(SMEM),) * 3,
        compiler_params=pltpu.CompilerParams(vmem_limit_bytes=limit),
    )(
        mig_rows, mig_count, active_ids, active_count, local_nbrs, ghost_slots, export_blocks,
        particles, landed,
    )
    ghost_count = peers * slots
    dens, adds, back = pl.pallas_call(
        pairs_kernel,
        name="pairs",
        out_shape=(
            struct((blocks, BLK), F32),
            struct((3, BLK, BLK), F32),
            struct((ghost_count, 3 * BLK), F32),
        ),
        in_specs=[spec(SMEM)] * 3 + [spec(VMEM)] * 6,
        out_specs=(spec(VMEM),) * 3,
        scratch_shapes=[
            VMEM((ghost_count * SENT, BLK), F32),
            VMEM((ghost_count, BLK), F32),
            VMEM((ghost_count, BLK), F32),
            VMEM((ghost_count, 3 * BLK), F32),
            VMEM((ghost_count, 3 * BLK), F32),
            VMEM((BLK, BLK), F32),
            VMEM((BLK, BLK), F32),
            VMEM((TOTACT, BLK, BLK), F32),
            VMEM((TOTACT, 1 + near_count + far_count, BLK, BLK), F32),
            VMEM((BLK, BLK), F32),
            VMEM((blocks, BLK), F32),
            VMEM((ghost_count, BLK), F32),
            VMEM((3, BLK, BLK), F32),
            VMEM((3, BLK, BLK), F32),
            VMEM((BLK, BLK), F32),
            pltpu.SemaphoreType.DMA((3, peers - 1)),
            pltpu.SemaphoreType.DMA((3, peers - 1)),
        ],
        compiler_params=pltpu.CompilerParams(collective_id=1, has_side_effects=True, vmem_limit_bytes=limit),
    )(act, near, far, tiles, stage, prev, expcol, table, centres)
    density, accel = pl.pallas_call(
        finish_kernel,
        name="finish",
        out_shape=(struct((blocks, BLK), F32), struct((3, count), F32)),
        in_specs=[spec(VMEM)] * 5,
        out_specs=(spec(VMEM),) * 2,
        scratch_shapes=[VMEM((3, blocks, BLK), F32)],
        compiler_params=pltpu.CompilerParams(vmem_limit_bytes=limit),
    )(table, tiles, dens, adds, back)
    return density.reshape(-1), accel


def solution(mesh):
    placed = (
        P(None, ("gx", "gy")),
        P(("gx", "gy"), None),
        P(("gx", "gy"), None, None),
        P(("gx", "gy"), None, None),
        P(("gx", "gy"), None),
        P(("gx", "gy"), None, None, None),
        P(("gx", "gy"), None, None, None),
        P(("gx", "gy"), None, None),
    )
    return jax.shard_map(
        shards,
        mesh=mesh,
        in_specs=placed,
        out_specs=(P(("gx", "gy")), P(None, ("gx", "gy"))),
        check_vma=False,
    )
```

```python
import functools
import math

import jax
import jax.numpy as jnp
from jax import lax
from jax.experimental import pallas as pl
from jax.experimental.pallas import tpu as pltpu
from jax.sharding import PartitionSpec as P

BLK = 128
TOTACT = 12
LEVELS = 4
CHAN = 8
SENT = 6

KERNEL_NORM = 21.0 / (16.0 * math.pi)
GAMMA_LESS = 2.0 / 3.0
FORCE_NORM = GAMMA_LESS * 32.0 * 5.0 * KERNEL_NORM
TINY = 1e-37
PART = 32
MESH = pl.DeviceIdType.MESH
VMEM = pltpu.VMEM
SMEM = pltpu.SMEM
F32 = jnp.float32
I32 = jnp.int32


def lanes(shape):
    return lax.broadcasted_iota(I32, shape, len(shape) - 1)


def spec(space):
    return pl.BlockSpec(memory_space=space)


def flipped(index, bit):
    return index + bit - 2 * bit * (lax.div(index, bit) % 2)


def picked(chunk, lane_number):
    return jnp.take_along_axis(
        chunk, jnp.full(chunk.shape, lane_number, I32), axis=1, mode="promise_in_bounds"
    )


def gather(tiles, rows):
    parts = []
    for part in range(rows.shape[1] // BLK):
        here = rows[:, part * BLK : (part + 1) * BLK]
        block = jnp.broadcast_to(here >> 7, (CHAN, BLK))
        spot = jnp.broadcast_to(here & 127, (CHAN, BLK))

        def step(n, held):
            held = list(held)
            for k in range(16):
                b = n * 16 + k
                tile = tiles[pl.ds(pl.multiple_of(b * CHAN, CHAN), CHAN), :]
                turned = jnp.take_along_axis(tile, spot, axis=1, mode="promise_in_bounds")
                held[k % 4] = jnp.where(block == b, turned, held[k % 4])
            return tuple(held)

        zero = jnp.zeros((CHAN, BLK), F32)
        held = lax.fori_loop(0, tiles.shape[0] // (16 * CHAN), step, (zero,) * 4)
        parts.append((held[0] + held[1]) + (held[2] + held[3]))
    return jnp.concatenate(parts, axis=1)


def pieces(value):
    first = value.astype(jnp.bfloat16).astype(F32)
    rest = value - first
    second = rest.astype(jnp.bfloat16).astype(F32)
    return first, second, rest - second


def migrate_kernel(
    count_ref, rows_ref, x_ref, out_ref, start_ref, spot_ref, tiles, leaving, landed, match, ssem, rsem
):
    gx, gy = lax.axis_index("gx"), lax.axis_index("gy")
    partners = [(flipped(gx, 2), gy), (flipped(gx, 1), gy), (gx, flipped(gy, 2)), (gx, flipped(gy, 1))]
    barrier = pltpu.get_barrier_semaphore()
    for partner in partners:
        pl.semaphore_signal(barrier, inc=1, device_id=partner, device_id_type=MESH)
    width = rows_ref.shape[2]
    blocks = x_ref.shape[1] // BLK

    def load(b8, _):
        for k in range(8):
            b = b8 * 8 + k
            tiles[pl.ds(b * CHAN, 7), :] = x_ref[:, pl.ds(pl.multiple_of(b * BLK, BLK), BLK)]
        return 0

    tiles[pl.ds(7, blocks, stride=CHAN), :] = jnp.zeros((blocks, BLK), F32)
    lax.fori_loop(0, blocks // 8, load, 0)
    rows = [rows_ref[0, level : level + 1, :] for level in range(LEVELS)]
    leaving[0] = gather(tiles, rows[0])
    pl.semaphore_wait(barrier, LEVELS)

    def copy(level):
        return pltpu.make_async_remote_copy(
            src_ref=leaving.at[level],
            dst_ref=landed.at[level],
            send_sem=ssem.at[level],
            recv_sem=rsem.at[level],
            device_id=partners[level],
            device_id_type=MESH,
        )

    first = copy(0)
    first.start()
    pair = {}
    for early in range(LEVELS - 1):
        used = lanes((1, width)) < count_ref[0, early]
        keys = jnp.where(used, rows[early], -1).astype(F32)
        for late in range(early + 1, LEVELS):
            pair[late, early] = len(pair)
        for part in range(width // BLK):
            across = jnp.broadcast_to(keys[:, part * BLK : (part + 1) * BLK], (BLK, BLK))
            down = jnp.transpose(across)
            down = jnp.concatenate([down] * (width // BLK), axis=1)
            for late in range(early + 1, LEVELS):
                same = down == rows[late].astype(F32)
                match[pair[late, early], part * BLK : (part + 1) * BLK, :] = jnp.where(same, 1.0, 0.0).astype(
                    jnp.bfloat16
                )
    kept = {1: gather(tiles, rows[1])}
    first.wait()
    factors = []
    for level in range(1, LEVELS):
        hi, mid, lo = pieces(landed[level - 1])
        factors.append(
            jnp.concatenate([hi, mid, lo, jnp.ones((8, width), F32)], axis=0).astype(jnp.bfloat16)
        )
        out = kept[level]
        for early in range(level):
            found = jnp.dot(factors[early], match[pair[level, early]], preferred_element_type=F32)
            value = (found[0:8] + found[8:16]) + found[16:24]
            out = jnp.where(found[24:32] > 0.5, value, out)
        leaving[level] = out
        moving = copy(level)
        moving.start()
        if level + 1 < LEVELS:
            kept[level + 1] = gather(tiles, rows[level + 1])
        else:
            for each in range(LEVELS):
                used = lanes((1, width)) < count_ref[0, each]
                start = (rows[each] >> 7) * CHAN
                spot = jnp.where(used, rows[each] & 127, -1)
                for part in range(width // BLK):
                    n = each * (width // BLK) + part
                    start_ref[n : n + 1, :] = start[:, part * BLK : (part + 1) * BLK]
                    spot_ref[n : n + 1, :] = spot[:, part * BLK : (part + 1) * BLK]
        moving.wait()
    out_ref[...] = landed[...]


def place_kernel(
    start_ref, spot_ref, ids_ref, live_ref, near_ref, far_ref, exp_ref, x_ref, landed_ref,
    tiles_ref, stage_ref, prev_ref, expcol_ref, table_ref, centres_ref, act_out, near_out, far_out,
):
    blocks = x_ref.shape[1] // BLK
    slots, peers = exp_ref.shape[1:]
    lane = lanes((CHAN, BLK))

    def load(b8, _):
        for k in range(8):
            b = b8 * 8 + k
            tiles_ref[pl.ds(b * CHAN, 7), :] = x_ref[:, pl.ds(pl.multiple_of(b * BLK, BLK), BLK)]
        return 0

    lax.fori_loop(0, blocks // 8, load, 0)
    tiles_ref[pl.ds(7, blocks, stride=CHAN), :] = jnp.zeros((blocks, BLK), F32)
    chunks = landed_ref.shape[2] // BLK

    def chunk(n, _):
        level, base = n // chunks, (n % chunks) * BLK
        held = landed_ref[level, :, pl.ds(pl.multiple_of(base, BLK), BLK)]
        for k in range(BLK):
            pltpu.store(
                tiles_ref.at[pl.ds(pl.multiple_of(start_ref[n, k], CHAN), CHAN), :],
                picked(held, k),
                mask=lane == spot_ref[n, k],
            )
        return 0

    lax.fori_loop(0, LEVELS * chunks, chunk, 0)

    wide = lanes((1, BLK))

    def pack(p, ids):
        for t in range(slots):
            block = exp_ref[0, t, p]
            tile = tiles_ref[pl.ds(pl.multiple_of(block * CHAN, CHAN), CHAN), :]
            stage_ref[pl.ds(p * (SENT * slots) + t, SENT, stride=slots), :] = tile[0:SENT]
            prev_ref[pl.ds(p * slots + t, 1), :] = tile[6:7]
            expcol_ref[pl.ds(p * slots + t, 1), :] = jnp.full((1, BLK), block, I32)
            ids = jnp.where(wide == p * slots + t, block, ids)
        return ids

    export_ids = lax.fori_loop(0, peers, pack, jnp.full((1, BLK), -1, I32))
    in_first = live_ref[0, 0]
    in_all = in_first + live_ref[0, 1]
    near_count = near_ref.shape[1]
    far_count = far_ref.shape[2]

    def compact(p, carry):
        centre, far = carry
        n = jnp.where(p < in_first, 0, 1)
        i = jnp.minimum(jnp.where(p < in_first, p, p - in_first), ids_ref.shape[2] - 1)
        alive = p < in_all
        block = ids_ref[0, n, i]
        act_out[2 * p] = block
        tile = tiles_ref[pl.ds(pl.multiple_of(block * CHAN, CHAN), CHAN), :]
        centres_ref[pl.ds(pl.multiple_of(p * CHAN, CHAN), 7), :] = tile[0:7]
        centres_ref[pl.ds(p * CHAN + 7, 1), :] = 0.5 / tile[4:5]
        act_out[2 * p + 1] = jnp.where(alive, block, -1)
        centre = jnp.where(wide == p, jnp.where(alive, block, -1), centre)
        for k in range(near_count):
            other = near_ref[0, k, n, i]
            near_out[p * near_count + k] = other
            centre = jnp.where(wide == TOTACT + p * near_count + k, jnp.where(alive, other, -1), centre)
        for k in range(far_count):
            other = far_ref[0, n, k, i]
            far_out[2 * (p * far_count + k)] = other
            far_out[2 * (p * far_count + k) + 1] = (other // slots) * (SENT * slots) + other % slots
            far = jnp.where(wide == p * far_count + k, jnp.where(alive, other, -1), far)
        return centre, far

    centres_ref[TOTACT * CHAN :, :] = jnp.zeros((BLK - TOTACT * CHAN, BLK), F32)
    empty = jnp.full((1, BLK), -1, I32)
    centre_ids, far_ids = lax.fori_loop(0, TOTACT, compact, (empty, empty))
    table_ref[0:1, :] = centre_ids
    table_ref[1:2, :] = far_ids
    table_ref[2:3, :] = export_ids
    table_ref[3:8, :] = jnp.full((5, BLK), -1, I32)


def abreast(ref):
    return jnp.concatenate([ref[0], ref[1], ref[2]], axis=1)


def exact_dot(left, right):
    return lax.dot_general(
        left, right, (((1,), (0,)), ((), ())), precision=lax.Precision.HIGHEST, preferred_element_type=F32
    )


def pairs_kernel(
    act_ref, near_ref, far_ref, tiles_ref, stage_ref, prev_ref, expcol_ref, table_ref, centres_in,
    dens_out, adds_out, back_out,
    ghosts, ghost_dens, dens_stage, back_stage, back_land, centres, cols, wide, sums, weights, rhos, pj, pg, adds, fars,
    forces, ssem, rsem,
):
    gx, me = lax.axis_index("gx"), lax.axis_index("gy")
    peers = lax.axis_size("gy")
    slots = stage_ref.shape[0] // (peers * SENT)
    block_count = dens_out.shape[0]
    near_count = near_ref.shape[0] // TOTACT
    far_count = far_ref.shape[0] // (2 * TOTACT)
    lane_part = lanes((PART, BLK))

    barrier = pltpu.get_barrier_semaphore()
    for apart in range(1, peers):
        pl.semaphore_signal(barrier, inc=1, device_id=(gx, lax.rem(me + apart, peers)), device_id_type=MESH)
    cols[...] = jnp.transpose(centres_in[...])
    pl.semaphore_wait(barrier, peers - 1)

    def exchange(phase, source, target, rows):
        copies = []
        for apart in range(1, peers):
            peer = lax.rem(me + apart, peers)
            copies.append(
                pltpu.make_async_remote_copy(
                    src_ref=source.at[pl.ds(peer * rows, rows), :],
                    dst_ref=target.at[pl.ds(me * rows, rows), :],
                    send_sem=ssem.at[phase, apart - 1],
                    recv_sem=rsem.at[phase, apart - 1],
                    device_id=(gx, peer),
                    device_id_type=MESH,
                )
            )
        for moving in copies:
            moving.start()
        return copies

    def finish(copies, source, target, rows):
        here = pl.ds(me * rows, rows)
        target[here, :] = source[here, :]
        for moving in copies:
            moving.wait()

    def sliced(q):
        return pl.ds(pl.multiple_of(q * PART, PART), PART)

    def local_row(block, channel):
        return tiles_ref[pl.ds(block * CHAN + channel, 1), :]

    def ghost_row(base, channel):
        return ghosts[pl.ds(base + channel * slots, 1), :]

    def separation(mine, theirs):
        dx, dy, dz = (a - b for a, b in zip(mine, theirs))
        square = dx * dx + dy * dy + dz * dz
        return square * lax.rsqrt(jnp.maximum(square, TINY))

    def density_term(r, inverse, mass5, mass4):
        fall = jnp.maximum(1.0 - r * inverse, 0.0)
        fall2 = fall * fall
        return (fall2 * fall2) * (mass5 - mass4 * fall)

    def pair_weight(r, smooth, mass, other_smooth, other_mass):
        inverse = 1.0 / (smooth + other_smooth)
        fall = jnp.maximum(1.0 - r * inverse, 0.0) * inverse
        return ((fall * fall) * fall * (inverse * inverse)) * (mass * other_mass)

    sent_blocks = exchange(0, stage_ref, ghosts, SENT * slots)

    def local_first(p, _):
        blocks = [act_ref[2 * p]] + [near_ref[p * near_count + k] for k in range(near_count)]
        rows = [[local_row(b, c) for c in range(5)] for b in blocks]
        masses = [(5.0 * row[3], 4.0 * row[3]) for row in rows]

        def part(q, _):
            here = sliced(q)
            chunk = cols[here, :]
            mine = [picked(chunk, p * CHAN + c) for c in (0, 1, 2, 3, 4, 7)]
            for c in range(6):
                wide[p, c, here, :] = mine[c]
            total = None
            for n, row in enumerate(rows):
                r = separation(mine[0:3], row[0:3])
                term = density_term(r, mine[5], *masses[n])
                total = term if total is None else total + term
                weights[p, n, here, :] = pair_weight(r, mine[4], mine[3], row[4], row[3])
            sums[p, here, :] = total
            return 0

        lax.fori_loop(0, BLK // PART, part, 0)
        return 0

    lax.fori_loop(0, TOTACT, local_first, 0)
    finish(sent_blocks, stage_ref, ghosts, SENT * slots)
    rhos[...] = jnp.zeros_like(rhos)

    def ghost_first(p, _):
        others = [far_ref[2 * (p * far_count + k) + 1] for k in range(far_count)]
        rows = [[ghost_row(g, c) for c in range(4)] for g in others]
        masses = [(5.0 * row[3], 4.0 * row[3]) for row in rows]

        def part(q, _):
            here = sliced(q)
            mine = [wide[p, c, here, :] for c in (0, 1, 2)]
            inverse = wide[p, 5, here, :]
            smooth = wide[p, 4, here, 0:1]
            total = sums[p, here, :]
            for n, row in enumerate(rows):
                r = separation(mine, row[0:3])
                weights[p, 1 + near_count + n, here, :] = r
                total = total + density_term(r, inverse, *masses[n])
            rho = KERNEL_NORM / (smooth * smooth * smooth) * jnp.sum(total, axis=1, keepdims=True)
            rhos[here, :] = jnp.where(lane_part == p, rho, rhos[here, :])
            return 0

        lax.fori_loop(0, BLK // PART, part, 0)
        return 0

    lax.fori_loop(0, TOTACT, ghost_first, 0)
    fresh = jnp.transpose(rhos[...])
    exported = prev_ref[...]
    export_block = expcol_ref[...]
    for p in range(TOTACT):
        exported = jnp.where(export_block == act_ref[2 * p + 1], fresh[p : p + 1, :], exported)
    dens_stage[...] = exported
    sent_dens = exchange(1, dens_stage, ghost_dens, slots)

    block_number = lax.broadcasted_iota(I32, (block_count, BLK), 0)
    dens = tiles_ref[pl.ds(6, block_count, stride=CHAN), :]
    for p in range(TOTACT):
        dens = jnp.where(block_number == act_ref[2 * p + 1], fresh[p : p + 1, :], dens)
    dens_out[...] = dens
    pj[...] = FORCE_NORM * (tiles_ref[pl.ds(5, block_count, stride=CHAN), :] / dens)
    centres[...] = jnp.zeros_like(centres)
    for p in range(TOTACT):
        energy = centres_in[p * CHAN + 5 : p * CHAN + 6, :]
        centres[p : p + 1, :] = FORCE_NORM * (energy / fresh[p : p + 1, :])
    cols[...] = jnp.transpose(centres[...])
    forces[...] = jnp.zeros_like(forces)
    adds[...] = jnp.zeros_like(adds)
    fars[...] = jnp.zeros_like(fars)

    def ghost_second(p, _):
        others = [far_ref[2 * (p * far_count + k) + 1] for k in range(far_count)]
        rows = [[ghost_row(g, c) for c in (3, 4)] for g in others]

        def part(q, _):
            here = sliced(q)
            mass, smooth = wide[p, 3, here, :], wide[p, 4, here, :]
            for n, row in enumerate(rows):
                r = weights[p, 1 + near_count + n, here, :]
                weights[p, 1 + near_count + n, here, :] = pair_weight(r, smooth, mass, row[1], row[0])
            wide[p, 5, here, :] = picked(cols[here, :], p)
            return 0

        lax.fori_loop(0, BLK // PART, part, 0)
        return 0

    lax.fori_loop(0, TOTACT, ghost_second, 0)

    def force_phase(p, first, rows, skip):
        kept = len(rows) - skip

        def part(q, carry):
            here = sliced(q)
            mine = [wide[p, c, here, :] for c in (0, 1, 2)]
            pressure = wide[p, 5, here, :]
            total = [None] * 3
            carry = list(carry)
            for n, row in enumerate(rows):
                weight = weights[p, first + n, here, :] * (pressure + row[3])
                for c in range(3):
                    push = weight * (mine[c] - row[c])
                    total[c] = push if total[c] is None else total[c] + push
                    if n >= skip:
                        at = (n - skip) * 3 + c
                        down = [push[8 * i : 8 * i + 8] for i in range(PART // 8)]
                        while len(down) > 1:
                            down = [down[i] + down[i + 1] for i in range(0, len(down), 2)]
                        carry[at] = carry[at] + down[0]
            held = forces[here, :]
            for c in range(3):
                whole = jnp.sum(total[c], axis=1, keepdims=True)
                held = jnp.where(lane_part == 3 * p + c, held + whole, held)
            forces[here, :] = held
            return tuple(carry)

        done = lax.fori_loop(0, BLK // PART, part, (jnp.zeros((8, BLK), F32),) * (3 * kept))
        return [[-jnp.sum(done[n * 3 + c], axis=0, keepdims=True) for c in range(3)] for n in range(kept)]

    finish(sent_dens, dens_stage, ghost_dens, slots)
    for s in range(peers):
        energy = ghosts[s * SENT * slots + 5 * slots : s * SENT * slots + 6 * slots, :]
        pg[s * slots : (s + 1) * slots, :] = FORCE_NORM * (energy / ghost_dens[s * slots : (s + 1) * slots, :])

    def ghost_force(p, _):
        others = [[far_ref[2 * (p * far_count + k) + i] for i in range(2)] for k in range(far_count)]
        rows = [[ghost_row(base, c) for c in range(3)] + [pg[pl.ds(g, 1), :]] for g, base in others]
        found = force_phase(p, 1 + near_count, rows, 0)
        for n in range(far_count):
            for c in range(3):
                fars[c, pl.ds(p * far_count + n, 1), :] = found[n][c]
        return 0

    lax.fori_loop(0, TOTACT, ghost_force, 0)
    ghost_number = lax.broadcasted_iota(I32, (peers * slots, BLK), 0)
    chosen = jnp.where(ghost_number == table_ref[1:2, :], 1.0, 0.0)
    back_stage[...] = exact_dot(chosen, abreast(fars))
    sent_back = exchange(2, back_stage, back_land, slots)

    def local_force(p, _):
        blocks = [act_ref[2 * p]] + [near_ref[p * near_count + k] for k in range(near_count)]
        rows = [[local_row(b, c) for c in range(3)] + [pj[pl.ds(b, 1), :]] for b in blocks]
        found = force_phase(p, 0, rows, 1)
        for n in range(near_count):
            for c in range(3):
                adds[c, pl.ds(TOTACT + p * near_count + n, 1), :] = found[n][c]
        return 0

    lax.fori_loop(0, TOTACT, local_force, 0)
    turned = jnp.transpose(forces[...])
    for p in range(TOTACT):
        for c in range(3):
            adds[c, p : p + 1, :] = turned[3 * p + c : 3 * p + c + 1, :]
    adds_out[...] = adds[...]
    finish(sent_back, back_stage, back_land, slots)
    back_out[...] = back_land[...]


def finish_kernel(table_ref, tiles_ref, dens_ref, adds_ref, back_ref, dens_out, accel_out, held):
    block_count = dens_ref.shape[0]
    block_number = lax.broadcasted_iota(I32, (block_count, BLK), 0)
    own = jnp.where(block_number == table_ref[0:1, :], 1.0, 0.0)
    sent = jnp.where(block_number == table_ref[2:3, :], 1.0, 0.0)
    totals = exact_dot(own, abreast(adds_ref)) + exact_dot(sent, back_ref[...])
    mass = tiles_ref[pl.ds(3, block_count, stride=CHAN), :]
    for c in range(3):
        held[c] = totals[:, c * BLK : (c + 1) * BLK] / mass
    dens_out[...] = dens_ref[...]

    def put(b8, _):
        for k in range(8):
            b = b8 * 8 + k
            for c in range(3):
                accel_out[c : c + 1, pl.ds(pl.multiple_of(b * BLK, BLK), BLK)] = held[c, pl.ds(b, 1), :]
        return 0

    lax.fori_loop(0, block_count // 8, put, 0)


def shards(
    particles, mig_count, mig_rows, active_ids, active_count, local_nbrs, ghost_slots, export_blocks
):
    count = particles.shape[1]
    blocks = count // BLK
    width = mig_rows.shape[2]
    peers, slots = export_blocks.shape[1:]
    near_count, far_count = local_nbrs.shape[3], ghost_slots.shape[3]
    limit = 60 * 1024 * 1024
    struct = jax.ShapeDtypeStruct
    parts = LEVELS * width // BLK
    landed, start, spot = pl.pallas_call(
        migrate_kernel,
        name="migrate",
        out_shape=(
            struct((LEVELS, CHAN, width), F32),
            struct((parts, BLK), I32),
            struct((parts, BLK), I32),
        ),
        in_specs=[spec(SMEM), spec(VMEM), spec(VMEM)],
        out_specs=(spec(VMEM),) * 3,
        scratch_shapes=[
            VMEM((blocks * CHAN, BLK), F32),
            VMEM((LEVELS, CHAN, width), F32),
            VMEM((LEVELS, CHAN, width), F32),
            VMEM((6, width, width), jnp.bfloat16),
            pltpu.SemaphoreType.DMA((LEVELS,)),
            pltpu.SemaphoreType.DMA((LEVELS,)),
        ],
        compiler_params=pltpu.CompilerParams(collective_id=0, has_side_effects=True, vmem_limit_bytes=limit),
    )(mig_count, mig_rows, particles)
    tiles, stage, prev, expcol, table, centres, act, near, far = pl.pallas_call(
        place_kernel,
        name="place",
        out_shape=(
            struct((blocks * CHAN, BLK), F32),
            struct((peers * SENT * slots, BLK), F32),
            struct((peers * slots, BLK), F32),
            struct((peers * slots, BLK), I32),
            struct((8, BLK), I32),
            struct((BLK, BLK), F32),
            struct((2 * TOTACT,), I32),
            struct((TOTACT * near_count,), I32),
            struct((2 * TOTACT * far_count,), I32),
        ),
        in_specs=[spec(SMEM)] * 7 + [spec(VMEM)] * 2,
        out_specs=(spec(VMEM),) * 6 + (spec(SMEM),) * 3,
        compiler_params=pltpu.CompilerParams(vmem_limit_bytes=limit),
    )(
        start, spot, active_ids, active_count,
        local_nbrs.transpose(0, 3, 1, 2), ghost_slots.transpose(0, 1, 3, 2), export_blocks.transpose(0, 2, 1),
        particles, landed,
    )
    ghost_count = peers * slots
    dens, adds, back = pl.pallas_call(
        pairs_kernel,
        name="pairs",
        out_shape=(
            struct((blocks, BLK), F32),
            struct((3, BLK, BLK), F32),
            struct((ghost_count, 3 * BLK), F32),
        ),
        in_specs=[spec(SMEM)] * 3 + [spec(VMEM)] * 6,
        out_specs=(spec(VMEM),) * 3,
        scratch_shapes=[
            VMEM((ghost_count * SENT, BLK), F32),
            VMEM((ghost_count, BLK), F32),
            VMEM((ghost_count, BLK), F32),
            VMEM((ghost_count, 3 * BLK), F32),
            VMEM((ghost_count, 3 * BLK), F32),
            VMEM((BLK, BLK), F32),
            VMEM((BLK, BLK), F32),
            VMEM((TOTACT, 6, BLK, BLK), F32),
            VMEM((TOTACT, BLK, BLK), F32),
            VMEM((TOTACT, 1 + near_count + far_count, BLK, BLK), F32),
            VMEM((BLK, BLK), F32),
            VMEM((blocks, BLK), F32),
            VMEM((ghost_count, BLK), F32),
            VMEM((3, BLK, BLK), F32),
            VMEM((3, BLK, BLK), F32),
            VMEM((BLK, BLK), F32),
            pltpu.SemaphoreType.DMA((3, peers - 1)),
            pltpu.SemaphoreType.DMA((3, peers - 1)),
        ],
        compiler_params=pltpu.CompilerParams(collective_id=1, has_side_effects=True, vmem_limit_bytes=limit),
    )(act, near, far, tiles, stage, prev, expcol, table, centres)
    density, accel = pl.pallas_call(
        finish_kernel,
        name="finish",
        out_shape=(struct((blocks, BLK), F32), struct((3, count), F32)),
        in_specs=[spec(VMEM)] * 5,
        out_specs=(spec(VMEM),) * 2,
        scratch_shapes=[VMEM((3, blocks, BLK), F32)],
        compiler_params=pltpu.CompilerParams(vmem_limit_bytes=limit),
    )(table, tiles, dens, adds, back)
    return density.reshape(-1), accel


def solution(mesh):
    placed = (
        P(None, ("gx", "gy")),
        P(("gx", "gy"), None),
        P(("gx", "gy"), None, None),
        P(("gx", "gy"), None, None),
        P(("gx", "gy"), None),
        P(("gx", "gy"), None, None, None),
        P(("gx", "gy"), None, None, None),
        P(("gx", "gy"), None, None),
    )
    return jax.shard_map(
        shards,
        mesh=mesh,
        in_specs=placed,
        out_specs=(P(("gx", "gy")), P(None, ("gx", "gy"))),
        check_vma=False,
    )
```

```python
import functools
import math

import jax
import jax.numpy as jnp
from jax import lax
from jax.experimental import pallas as pl
from jax.experimental.pallas import tpu as pltpu
from jax.sharding import PartitionSpec as P

BLK = 128
TOTACT = 12
LEVELS = 4
CHAN = 8
SENT = 4
SLOT_BITS = 3

KERNEL_NORM = 21.0 / (16.0 * math.pi)
GAMMA_LESS = 2.0 / 3.0
FORCE_NORM = GAMMA_LESS * 32.0 * 5.0 * KERNEL_NORM
TINY = 1e-37
PART = 32
MESH = pl.DeviceIdType.MESH
VMEM = pltpu.VMEM
SMEM = pltpu.SMEM
F32 = jnp.float32
I32 = jnp.int32


def lanes(shape):
    return lax.broadcasted_iota(I32, shape, len(shape) - 1)


def spec(space):
    return pl.BlockSpec(memory_space=space)


def flipped(index, bit):
    return index + bit - 2 * bit * (lax.div(index, bit) % 2)


def picked(chunk, lane_number):
    return jnp.take_along_axis(
        chunk, jnp.full(chunk.shape, lane_number, I32), axis=1, mode="promise_in_bounds"
    )


def gather(tiles, rows):
    parts = []
    for part in range(rows.shape[1] // BLK):
        here = rows[:, part * BLK : (part + 1) * BLK]
        block = jnp.broadcast_to(here >> 7, (CHAN, BLK))
        spot = jnp.broadcast_to(here & 127, (CHAN, BLK))

        def step(n, held):
            held = list(held)
            for k in range(16):
                b = n * 16 + k
                tile = tiles[b]
                turned = jnp.take_along_axis(tile, spot, axis=1, mode="promise_in_bounds")
                held[k % 4] = jnp.where(block == b, turned, held[k % 4])
            return tuple(held)

        zero = jnp.zeros((CHAN, BLK), F32)
        held = lax.fori_loop(0, tiles.shape[0] // 16, step, (zero,) * 4)
        parts.append((held[0] + held[1]) + (held[2] + held[3]))
    return jnp.concatenate(parts, axis=1)


def pieces(value):
    first = value.astype(jnp.bfloat16).astype(F32)
    rest = value - first
    second = rest.astype(jnp.bfloat16).astype(F32)
    return first, second, rest - second


def abreast(ref):
    return jnp.concatenate([ref[0], ref[1], ref[2]], axis=1)


def exact_dot(left, right):
    return lax.dot_general(
        left, right, (((1,), (0,)), ((), ())), precision=lax.Precision.HIGHEST, preferred_element_type=F32
    )


def row_sums(value):
    parts = jnp.concatenate(pieces(value), axis=1).astype(jnp.bfloat16)
    ones = jnp.ones((8, parts.shape[1]), jnp.bfloat16)
    return lax.dot_general(ones, parts, (((1,), (1,)), ((), ())), preferred_element_type=F32)[0:1]


def substep_kernel(
    count_ref, ids_ref, live_ref, near_ref, far_ref, exp_ref, rows_ref, x_ref,
    dens_out, mass_out, table_out, adds_out, back_out,
    tiles, leaving, landed, match, map_lane, map_part, act, near, far,
    stage, stage_h, stage_p, energies, expcol, ghosts, ghost_h, ghost_p, back_stage, back_land,
    centres, cols, wide, sums, weights, rhos, pj, adds, fars, forces,
    mig_ssem, mig_rsem, ssem, rsem,
):
    gx, me = lax.axis_index("gx"), lax.axis_index("gy")
    peers = lax.axis_size("gy")
    slots = exp_ref.shape[1]
    width = rows_ref.shape[2]
    parts = width // BLK
    blocks = x_ref.shape[1] // BLK
    near_count, far_count = near_ref.shape[1], far_ref.shape[2]
    partners = [(flipped(gx, 2), me), (flipped(gx, 1), me), (gx, flipped(me, 2)), (gx, flipped(me, 1))]
    around = [(gx, lax.rem(me + apart, peers)) for apart in range(1, peers)]

    barrier = pltpu.get_barrier_semaphore()
    for other in partners[0:2] + around:
        pl.semaphore_signal(barrier, inc=1, device_id=other, device_id_type=MESH)

    def load(b8, _):
        for k in range(8):
            b = b8 * 8 + k
            tiles[b, 0:7, :] = x_ref[:, pl.ds(pl.multiple_of(b * BLK, BLK), BLK)]
            tiles[b, 7:8, :] = jnp.zeros((1, BLK), F32)
        return 0

    lax.fori_loop(0, blocks // 8, load, 0)
    rows = [rows_ref[0, level : level + 1, :] for level in range(LEVELS)]
    leaving[0] = gather(tiles, rows[0])
    pl.semaphore_wait(barrier, peers + 1)

    def copy(level):
        return pltpu.make_async_remote_copy(
            src_ref=leaving.at[level],
            dst_ref=landed.at[level],
            send_sem=mig_ssem.at[level],
            recv_sem=mig_rsem.at[level],
            device_id=partners[level],
            device_id_type=MESH,
        )

    pair = {}
    for early in range(LEVELS - 1):
        for late in range(early + 1, LEVELS):
            pair[late, early] = len(pair)

    def relate(early):
        keys = jnp.where(lanes((1, width)) < count_ref[0, early], rows[early], -1)
        lane = lanes((BLK, BLK))
        slot = lax.broadcasted_iota(I32, (BLK, BLK), 0)
        owner = lax.broadcasted_iota(I32, (blocks, width), 0)
        spots = []
        for part in range(parts):
            down = jnp.transpose(jnp.broadcast_to(keys[:, part * BLK : (part + 1) * BLK], (BLK, BLK)))
            hit = (down & 127) == lane
            spots.append(
                jnp.concatenate(
                    [jnp.where(hit, (slot + 1).astype(F32), 0.0), jnp.where(hit, float(part), 0.0)], axis=1
                ).astype(jnp.bfloat16)
            )
            down = jnp.concatenate([down] * parts, axis=1)
            for late in range(early + 1, LEVELS):
                match[pair[late, early], part * BLK : (part + 1) * BLK, :] = jnp.where(
                    down == rows[late], 1.0, 0.0
                ).astype(jnp.bfloat16)
        held = jnp.where(owner == (keys >> 7), 1.0, 0.0).astype(jnp.bfloat16)
        found = jnp.dot(held, jnp.concatenate(spots, axis=0), preferred_element_type=F32).astype(I32)
        map_lane[early] = jnp.maximum(found[:, 0:BLK] - 1, 0)
        map_part[early] = jnp.where(found[:, 0:BLK] > 0, found[:, BLK:], -1)

    def settle(level):
        arrived = [landed[level, :, part * BLK : (part + 1) * BLK] for part in range(parts)]

        def step(b8, _):
            for k in range(8):
                b = b8 * 8 + k
                spot = jnp.broadcast_to(map_lane[level, pl.ds(b, 1), :], (CHAN, BLK))
                which = jnp.broadcast_to(map_part[level, pl.ds(b, 1), :], (CHAN, BLK))
                tile = tiles[b]
                for part in range(parts):
                    turned = jnp.take_along_axis(arrived[part], spot, axis=1, mode="promise_in_bounds")
                    tile = jnp.where(which == part, turned, tile)
                tiles[b] = tile
            return 0

        lax.fori_loop(0, blocks // 8, step, 0)

    wide_lane = lanes((1, BLK))

    def compact():
        in_first = live_ref[0, 0]
        in_all = in_first + live_ref[0, 1]
        centre = jnp.full((1, BLK), -1, I32)
        distant = jnp.full((1, BLK), -1, I32)
        for p in range(TOTACT):
            n = jnp.where(p < in_first, 0, 1)
            i = jnp.minimum(jnp.where(p < in_first, p, p - in_first), ids_ref.shape[2] - 1)
            alive = p < in_all
            block = ids_ref[0, n, i]
            act[2 * p] = block
            act[2 * p + 1] = jnp.where(alive, block, -1)
            centre = jnp.where(wide_lane == p, jnp.where(alive, block, -1), centre)
            for k in range(near_count):
                other = near_ref[0, k, n, i]
                near[p * near_count + k] = other
                centre = jnp.where(
                    wide_lane == TOTACT + p * near_count + k, jnp.where(alive, other, -1), centre
                )
            for k in range(far_count):
                other = far_ref[0, n, k, i]
                far[p * far_count + k] = other
                distant = jnp.where(wide_lane == p * far_count + k, jnp.where(alive, other, -1), distant)
        table_out[0:1, :] = centre
        table_out[1:2, :] = distant
        table_out[3:8, :] = jnp.full((5, BLK), -1, I32)

    first = copy(0)
    first.start()
    relate(0)
    kept = {1: gather(tiles, rows[1])}
    first.wait()
    factors = []
    for level in range(1, LEVELS):
        factors.append(
            jnp.concatenate([*pieces(landed[level - 1]), jnp.ones((8, width), F32)], axis=0).astype(jnp.bfloat16)
        )
        out = kept[level]
        for early in range(level):
            found = jnp.dot(factors[early], match[pair[level, early]], preferred_element_type=F32)
            value = (found[0:8] + found[8:16]) + found[16:24]
            out = jnp.where(found[24:32] > 0.5, value, out)
        leaving[level] = out
        moving = copy(level)
        moving.start()
        if level + 1 < LEVELS:
            relate(level)
            kept[level + 1] = gather(tiles, rows[level + 1])
        if level == LEVELS - 2:
            settle(0)
        if level == LEVELS - 1:
            relate(level)
            for each in range(1, level):
                settle(each)
            compact()
        moving.wait()
    settle(LEVELS - 1)

    def pack(p, _):
        for t in range(slots):
            tile = tiles[exp_ref[0, t, p]]
            stage[pl.ds(p * (SENT * slots) + t, SENT, stride=slots), :] = tile[0:SENT]
        return 0

    lax.fori_loop(0, peers, pack, 0)

    def exchange(phase, source, target, count):
        copies = []
        for apart in range(1, peers):
            peer = lax.rem(me + apart, peers)
            copies.append(
                pltpu.make_async_remote_copy(
                    src_ref=source.at[pl.ds(peer * count, count), :],
                    dst_ref=target.at[pl.ds(me * count, count), :],
                    send_sem=ssem.at[phase, apart - 1],
                    recv_sem=rsem.at[phase, apart - 1],
                    device_id=(gx, peer),
                    device_id_type=MESH,
                )
            )
        for moving in copies:
            moving.start()
        return copies

    def finish(copies, source, target, count):
        here = pl.ds(me * count, count)
        target[here, :] = source[here, :]
        for moving in copies:
            moving.wait()

    sent_blocks = exchange(0, stage, ghosts, SENT * slots)

    def pack_rest(p, ids):
        for t in range(slots):
            block = exp_ref[0, t, p]
            tile = tiles[block]
            row = pl.ds(p * slots + t, 1)
            stage_h[row, :] = tile[4:5]
            energies[row, :] = tile[5:6]
            stage_p[row, :] = tile[6:7]
            expcol[row, :] = jnp.full((1, BLK), block, I32)
            ids = jnp.where(wide_lane == p * slots + t, block, ids)
        return ids

    table_out[2:3, :] = lax.fori_loop(0, peers, pack_rest, jnp.full((1, BLK), -1, I32))
    centres[...] = jnp.zeros_like(centres)
    for p in range(TOTACT):
        tile = tiles[act[2 * p]]
        centres[p * CHAN : p * CHAN + 7, :] = tile[0:7]
        centres[p * CHAN + 7 : p * CHAN + 8, :] = 0.5 / tile[4:5]
    cols[...] = jnp.transpose(centres[...])

    def sliced(q):
        return slice(q * PART, (q + 1) * PART)

    def local_row(block, channel):
        return tiles[block, channel : channel + 1, :]

    def ghost_base(ghost):
        return (ghost >> SLOT_BITS) * (SENT * slots) + (ghost & (slots - 1))

    def ghost_row(base, channel):
        return ghosts[pl.ds(base + channel * slots, 1), :]

    def separation(mine, theirs):
        dx, dy, dz = (a - b for a, b in zip(mine, theirs))
        square = dx * dx + dy * dy + dz * dz
        return square * lax.rsqrt(jnp.maximum(square, TINY))

    def density_term(r, inverse, mass5, mass4):
        fall = jnp.maximum(1.0 - r * inverse, 0.0)
        fall2 = fall * fall
        return (fall2 * fall2) * (mass5 - mass4 * fall)

    def pair_weight(r, smooth, mass, other_smooth, other_mass):
        inverse = 1.0 / (smooth + other_smooth)
        fall = jnp.maximum(1.0 - r * inverse, 0.0) * inverse
        return ((fall * fall) * fall * (inverse * inverse)) * (mass * other_mass)

    def local_first(p, _):
        others = [act[2 * p]] + [near[p * near_count + k] for k in range(near_count)]
        rows = [[local_row(b, c) for c in range(5)] for b in others]
        masses = [(5.0 * row[3], 4.0 * row[3]) for row in rows]
        for q in range(BLK // PART):
            here = sliced(q)
            chunk = cols[here, :]
            mine = [picked(chunk, p * CHAN + c) for c in (0, 1, 2, 3, 4, 7)]
            for c in range(6):
                wide[p, c, here, :] = mine[c]
            total = None
            for n, row in enumerate(rows):
                r = separation(mine[0:3], row[0:3])
                term = density_term(r, mine[5], *masses[n])
                total = term if total is None else total + term
                weights[p, n, here, :] = pair_weight(r, mine[4], mine[3], row[4], row[3])
            sums[p, here, :] = total
        return 0

    lax.fori_loop(0, TOTACT, local_first, 0)
    finish(sent_blocks, stage, ghosts, SENT * slots)
    sent_h = exchange(1, stage_h, ghost_h, slots)

    def ghost_first(p, _):
        others = [ghost_base(far[p * far_count + k]) for k in range(far_count)]
        rows = [[ghost_row(g, c) for c in range(4)] for g in others]
        masses = [(5.0 * row[3], 4.0 * row[3]) for row in rows]
        for q in range(BLK // PART):
            here = sliced(q)
            mine = [wide[p, c, here, :] for c in (0, 1, 2)]
            inverse = wide[p, 5, here, :]
            total = sums[p, here, :]
            for n, row in enumerate(rows):
                r = separation(mine, row[0:3])
                weights[p, 1 + near_count + n, here, :] = r
                total = total + density_term(r, inverse, *masses[n])
            sums[p, here, :] = total
        return 0

    lax.fori_loop(0, TOTACT, ghost_first, 0)
    fresh = []
    for p in range(TOTACT):
        smooth = centres[p * CHAN + 4 : p * CHAN + 5, :]
        fresh.append(KERNEL_NORM / (smooth * smooth * smooth) * row_sums(sums[p]))
    exported = stage_p[...]
    export_block = expcol[...]
    for p in range(TOTACT):
        exported = jnp.where(export_block == act[2 * p + 1], fresh[p], exported)
    stage_p[...] = FORCE_NORM * (energies[...] / exported)
    finish(sent_h, stage_h, ghost_h, slots)
    sent_p = exchange(2, stage_p, ghost_p, slots)

    block_number = lax.broadcasted_iota(I32, (blocks, BLK), 0)
    dens = tiles[:, 6, :]
    for p in range(TOTACT):
        dens = jnp.where(block_number == act[2 * p + 1], fresh[p], dens)
    dens_out[...] = dens
    mass_out[...] = tiles[:, 3, :]
    pj[...] = FORCE_NORM * (tiles[:, 5, :] / dens)
    rhos[...] = jnp.zeros_like(rhos)
    for p in range(TOTACT):
        rhos[p : p + 1, :] = FORCE_NORM * (centres[p * CHAN + 5 : p * CHAN + 6, :] / fresh[p])
    cols[...] = jnp.transpose(rhos[...])
    adds[...] = jnp.zeros_like(adds)
    fars[...] = jnp.zeros_like(fars)

    def ghost_second(p, _):
        others = [far[p * far_count + k] for k in range(far_count)]
        rows = [[ghost_row(ghost_base(g), 3), ghost_h[pl.ds(g, 1), :]] for g in others]
        for q in range(BLK // PART):
            here = sliced(q)
            mass, smooth = wide[p, 3, here, :], wide[p, 4, here, :]
            for n, row in enumerate(rows):
                r = weights[p, 1 + near_count + n, here, :]
                weights[p, 1 + near_count + n, here, :] = pair_weight(r, smooth, mass, row[1], row[0])
            wide[p, 5, here, :] = picked(cols[here, :], p)
        return 0

    lax.fori_loop(0, TOTACT, ghost_second, 0)

    def force_phase(p, first, rows, skip, again):
        kept = len(rows) - skip
        carry = [None] * (3 * kept)
        for q in range(BLK // PART):
            here = sliced(q)
            mine = [wide[p, c, here, :] for c in (0, 1, 2)]
            pressure = wide[p, 5, here, :]
            total = [forces[c, p, here, :] for c in range(3)] if again else [None] * 3
            for n, row in enumerate(rows):
                weight = weights[p, first + n, here, :] * (pressure + row[3])
                for c in range(3):
                    push = weight * (mine[c] - row[c])
                    total[c] = push if total[c] is None else total[c] + push
                    if n >= skip:
                        at = (n - skip) * 3 + c
                        down = [push[8 * i : 8 * i + 8] for i in range(PART // 8)]
                        if carry[at] is not None:
                            down.append(carry[at])
                        while len(down) > 1:
                            down = down[2:] + [down[0] + down[1]]
                        carry[at] = down[0]
            for c in range(3):
                forces[c, p, here, :] = total[c]
        return [[-jnp.sum(carry[n * 3 + c], axis=0, keepdims=True) for c in range(3)] for n in range(kept)]

    finish(sent_p, stage_p, ghost_p, slots)

    def ghost_force(p, _):
        others = [far[p * far_count + k] for k in range(far_count)]
        rows = [[ghost_row(ghost_base(g), c) for c in range(3)] + [ghost_p[pl.ds(g, 1), :]] for g in others]
        found = force_phase(p, 1 + near_count, rows, 0, False)
        for n in range(far_count):
            for c in range(3):
                fars[c, pl.ds(p * far_count + n, 1), :] = found[n][c]
        return 0

    lax.fori_loop(0, TOTACT, ghost_force, 0)
    ghost_number = lax.broadcasted_iota(I32, (peers * slots, BLK), 0)
    chosen = jnp.where(ghost_number == table_out[1:2, :], 1.0, 0.0)
    back_stage[...] = exact_dot(chosen, abreast(fars))
    sent_back = exchange(3, back_stage, back_land, slots)

    def local_force(p, _):
        others = [act[2 * p]] + [near[p * near_count + k] for k in range(near_count)]
        rows = [[local_row(b, c) for c in range(3)] + [pj[pl.ds(b, 1), :]] for b in others]
        found = force_phase(p, 0, rows, 1, True)
        for n in range(near_count):
            for c in range(3):
                adds[c, pl.ds(TOTACT + p * near_count + n, 1), :] = found[n][c]
        return 0

    lax.fori_loop(0, TOTACT, local_force, 0)

    def centre_force(p, _):
        for c in range(3):
            adds[c, pl.ds(p, 1), :] = row_sums(forces[c, p])
        return 0

    lax.fori_loop(0, TOTACT, centre_force, 0)
    adds_out[...] = adds[...]
    finish(sent_back, back_stage, back_land, slots)
    back_out[...] = back_land[...]


def finish_kernel(table_ref, mass_ref, dens_ref, adds_ref, back_ref, dens_out, accel_out, held):
    block_count = dens_ref.shape[0]
    block_number = lax.broadcasted_iota(I32, (block_count, BLK), 0)
    own = jnp.where(block_number == table_ref[0:1, :], 1.0, 0.0)
    sent = jnp.where(block_number == table_ref[2:3, :], 1.0, 0.0)
    totals = exact_dot(own, abreast(adds_ref)) + exact_dot(sent, back_ref[...])
    mass = mass_ref[...]
    for c in range(3):
        held[c] = totals[:, c * BLK : (c + 1) * BLK] / mass
    dens_out[...] = dens_ref[...]

    def put(b8, _):
        for k in range(8):
            b = b8 * 8 + k
            for c in range(3):
                accel_out[c : c + 1, pl.ds(pl.multiple_of(b * BLK, BLK), BLK)] = held[c, pl.ds(b, 1), :]
        return 0

    lax.fori_loop(0, block_count // 8, put, 0)


def shards(
    particles, mig_count, mig_rows, active_ids, active_count, local_nbrs, ghost_slots, export_blocks
):
    count = particles.shape[1]
    blocks = count // BLK
    width = mig_rows.shape[2]
    peers, slots = export_blocks.shape[1:]
    near_count, far_count = local_nbrs.shape[3], ghost_slots.shape[3]
    limit = 60 * 1024 * 1024
    struct = jax.ShapeDtypeStruct
    ghost_count = peers * slots
    square = VMEM((BLK, BLK), F32)
    each = VMEM((ghost_count, BLK), F32)
    dens, mass, table, adds, back = pl.pallas_call(
        substep_kernel,
        name="substep",
        out_shape=(
            struct((blocks, BLK), F32),
            struct((blocks, BLK), F32),
            struct((8, BLK), I32),
            struct((3, BLK, BLK), F32),
            struct((ghost_count, 3 * BLK), F32),
        ),
        in_specs=[spec(SMEM)] * 6 + [spec(VMEM)] * 2,
        out_specs=(spec(VMEM),) * 5,
        scratch_shapes=[
            VMEM((blocks, CHAN, BLK), F32),
            VMEM((LEVELS, CHAN, width), F32),
            VMEM((LEVELS, CHAN, width), F32),
            VMEM((6, width, width), jnp.bfloat16),
            VMEM((LEVELS, blocks, BLK), I32),
            VMEM((LEVELS, blocks, BLK), I32),
            SMEM((2 * TOTACT,), I32),
            SMEM((TOTACT * near_count,), I32),
            SMEM((TOTACT * far_count,), I32),
            VMEM((ghost_count * SENT, BLK), F32),
            each,
            each,
            each,
            VMEM((ghost_count, BLK), I32),
            VMEM((ghost_count * SENT, BLK), F32),
            each,
            each,
            VMEM((ghost_count, 3 * BLK), F32),
            VMEM((ghost_count, 3 * BLK), F32),
            square,
            square,
            VMEM((TOTACT, 6, BLK, BLK), F32),
            VMEM((TOTACT, BLK, BLK), F32),
            VMEM((TOTACT, 1 + near_count + far_count, BLK, BLK), F32),
            square,
            VMEM((blocks, BLK), F32),
            VMEM((3, BLK, BLK), F32),
            VMEM((3, BLK, BLK), F32),
            VMEM((3, TOTACT, BLK, BLK), F32),
            pltpu.SemaphoreType.DMA((LEVELS,)),
            pltpu.SemaphoreType.DMA((LEVELS,)),
            pltpu.SemaphoreType.DMA((4, peers - 1)),
            pltpu.SemaphoreType.DMA((4, peers - 1)),
        ],
        compiler_params=pltpu.CompilerParams(collective_id=0, has_side_effects=True, vmem_limit_bytes=limit),
    )(
        mig_count, active_ids, active_count,
        local_nbrs.transpose(0, 3, 1, 2), ghost_slots.transpose(0, 1, 3, 2), export_blocks.transpose(0, 2, 1),
        mig_rows, particles,
    )
    density, accel = pl.pallas_call(
        finish_kernel,
        name="finish",
        out_shape=(struct((blocks, BLK), F32), struct((3, count), F32)),
        in_specs=[spec(VMEM)] * 5,
        out_specs=(spec(VMEM),) * 2,
        scratch_shapes=[VMEM((3, blocks, BLK), F32)],
        compiler_params=pltpu.CompilerParams(vmem_limit_bytes=limit),
    )(table, mass, dens, adds, back)
    return density.reshape(-1), accel


def solution(mesh):
    placed = (
        P(None, ("gx", "gy")),
        P(("gx", "gy"), None),
        P(("gx", "gy"), None, None),
        P(("gx", "gy"), None, None),
        P(("gx", "gy"), None),
        P(("gx", "gy"), None, None, None),
        P(("gx", "gy"), None, None, None),
        P(("gx", "gy"), None, None),
    )
    return jax.shard_map(
        shards,
        mesh=mesh,
        in_specs=placed,
        out_specs=(P(("gx", "gy")), P(None, ("gx", "gy"))),
        check_vma=False,
    )
```

```python
import functools
import math

import jax
import jax.numpy as jnp
from jax import lax
from jax.experimental import pallas as pl
from jax.experimental.pallas import tpu as pltpu
from jax.sharding import PartitionSpec as P

BLK = 128
TOTACT = 12
LEVELS = 4
CHAN = 8
SENT = 4
SLOT_BITS = 3
ADDED = 64

KERNEL_NORM = 21.0 / (16.0 * math.pi)
GAMMA_LESS = 2.0 / 3.0
FORCE_NORM = GAMMA_LESS * 32.0 * 5.0 * KERNEL_NORM
TINY = 1e-37
PART = 32
MESH = pl.DeviceIdType.MESH
VMEM = pltpu.VMEM
SMEM = pltpu.SMEM
F32 = jnp.float32
I32 = jnp.int32


def lanes(shape):
    return lax.broadcasted_iota(I32, shape, len(shape) - 1)


def spec(space):
    return pl.BlockSpec(memory_space=space)


def flipped(index, bit):
    return index + bit - 2 * bit * (lax.div(index, bit) % 2)


def picked(chunk, lane_number):
    return jnp.take_along_axis(
        chunk, jnp.full(chunk.shape, lane_number, I32), axis=1, mode="promise_in_bounds"
    )


def gather(tiles, rows):
    parts = []
    for part in range(rows.shape[1] // BLK):
        here = rows[:, part * BLK : (part + 1) * BLK]
        block = jnp.broadcast_to(here >> 7, (CHAN, BLK))
        spot = jnp.broadcast_to(here & 127, (CHAN, BLK))

        def step(n, held):
            held = list(held)
            for k in range(64):
                b = n * 64 + k
                tile = tiles[b]
                turned = jnp.take_along_axis(tile, spot, axis=1, mode="promise_in_bounds")
                held[k % 4] = jnp.where(block == b, turned, held[k % 4])
            return tuple(held)

        zero = jnp.zeros((CHAN, BLK), F32)
        held = lax.fori_loop(0, tiles.shape[0] // 64, step, (zero,) * 4)
        parts.append((held[0] + held[1]) + (held[2] + held[3]))
    return jnp.concatenate(parts, axis=1)


def pieces(value):
    first = value.astype(jnp.bfloat16).astype(F32)
    rest = value - first
    second = rest.astype(jnp.bfloat16).astype(F32)
    return first, second, rest - second


def abreast(ref):
    return jnp.concatenate([ref[0], ref[1], ref[2]], axis=1)


def row_sums(value):
    return jnp.sum(jnp.transpose(value), axis=0, keepdims=True)


def placed_sum(ids, terms, count):
    depth = terms.shape[0]
    owner = lax.broadcasted_iota(I32, (count, depth), 0)
    chosen = jnp.where(owner == ids[:, 0:depth], 1.0, 0.0)
    chosen = jnp.concatenate([chosen] * 3, axis=1).astype(jnp.bfloat16)
    split = jnp.concatenate(pieces(terms), axis=0).astype(jnp.bfloat16)
    return jnp.dot(chosen, split, preferred_element_type=F32)


def substep_kernel(
    count_ref, ids_ref, live_ref, near_ref, far_ref, exp_ref, rows_ref, x_ref,
    dens_out, accel_out,
    tiles, leaving, landed, match, map_lane, map_part, table, act, near, far,
    stage, stage_h, stage_p, energies, expcol, ghosts, ghost_h, ghost_p, back_stage, back_land,
    centres, cols, wide, sums, weights, rhos, pj, adds, fars, forces, held_force,
    mig_ssem, mig_rsem, ssem, rsem,
):
    gx, me = lax.axis_index("gx"), lax.axis_index("gy")
    peers = lax.axis_size("gy")
    slots = exp_ref.shape[1]
    width = rows_ref.shape[2]
    parts = width // BLK
    blocks = x_ref.shape[1] // BLK
    near_count, far_count = near_ref.shape[1], far_ref.shape[2]
    partners = [(flipped(gx, 2), me), (flipped(gx, 1), me), (gx, flipped(me, 2)), (gx, flipped(me, 1))]
    around = [(gx, lax.rem(me + apart, peers)) for apart in range(1, peers)]

    barrier = pltpu.get_barrier_semaphore()
    for other in partners[0:2] + around:
        pl.semaphore_signal(barrier, inc=1, device_id=other, device_id_type=MESH)

    def load(b8, _):
        for k in range(8):
            b = b8 * 8 + k
            tiles[b, 0:7, :] = x_ref[:, pl.ds(pl.multiple_of(b * BLK, BLK), BLK)]
            tiles[b, 7:8, :] = jnp.zeros((1, BLK), F32)
        return 0

    lax.fori_loop(0, blocks // 8, load, 0)
    rows = [rows_ref[0, level : level + 1, :] for level in range(LEVELS)]
    leaving[0] = gather(tiles, rows[0])
    pl.semaphore_wait(barrier, peers + 1)

    def copy(level):
        return pltpu.make_async_remote_copy(
            src_ref=leaving.at[level],
            dst_ref=landed.at[level],
            send_sem=mig_ssem.at[level],
            recv_sem=mig_rsem.at[level],
            device_id=partners[level],
            device_id_type=MESH,
        )

    pair = {}
    for early in range(LEVELS - 1):
        for late in range(early + 1, LEVELS):
            pair[late, early] = len(pair)

    def relate(early):
        keys = jnp.where(lanes((1, width)) < count_ref[0, early], rows[early], -1)
        lane = lanes((BLK, BLK))
        slot = lax.broadcasted_iota(I32, (BLK, BLK), 0)
        owner = lax.broadcasted_iota(I32, (blocks, width), 0)
        spots = []
        for part in range(parts):
            down = jnp.transpose(jnp.broadcast_to(keys[:, part * BLK : (part + 1) * BLK], (BLK, BLK)))
            hit = (down & 127) == lane
            spots.append(
                jnp.concatenate(
                    [jnp.where(hit, (slot + 1).astype(F32), 0.0), jnp.where(hit, float(part), 0.0)], axis=1
                ).astype(jnp.bfloat16)
            )
            down = jnp.concatenate([down] * parts, axis=1)
            for late in range(early + 1, LEVELS):
                match[pair[late, early], part * BLK : (part + 1) * BLK, :] = jnp.where(
                    down == rows[late], 1.0, 0.0
                ).astype(jnp.bfloat16)
        held = jnp.where(owner == (keys >> 7), 1.0, 0.0).astype(jnp.bfloat16)
        found = jnp.dot(held, jnp.concatenate(spots, axis=0), preferred_element_type=F32).astype(I32)
        arriving = found[:, 0:BLK] > 0
        spot = found[:, 0:BLK] - 1
        part = found[:, BLK:] + early * parts
        if early in (0, LEVELS - 1):
            map_lane[early // (LEVELS - 1)] = jnp.where(arriving, spot, 0)
            map_part[early // (LEVELS - 1)] = jnp.where(arriving, part, -1)
        else:
            map_lane[0] = jnp.where(arriving, spot, map_lane[0])
            map_part[0] = jnp.where(arriving, part, map_part[0])

    def settle(which_map, levels):
        numbers = [level * parts + part for level in levels for part in range(parts)]
        arrived = {n: landed[n // parts, :, n % parts * BLK : (n % parts + 1) * BLK] for n in numbers}

        def step(b8, _):
            for k in range(8):
                b = b8 * 8 + k
                spot = jnp.broadcast_to(map_lane[which_map, pl.ds(b, 1), :], (CHAN, BLK))
                which = jnp.broadcast_to(map_part[which_map, pl.ds(b, 1), :], (CHAN, BLK))
                tile = tiles[b]
                for n in numbers:
                    turned = jnp.take_along_axis(arrived[n], spot, axis=1, mode="promise_in_bounds")
                    tile = jnp.where(which == n, turned, tile)
                tiles[b] = tile
            return 0

        lax.fori_loop(0, blocks // 8, step, 0)

    wide_lane = lanes((1, BLK))

    def compact():
        in_first = live_ref[0, 0]
        in_all = in_first + live_ref[0, 1]
        centre = jnp.full((1, BLK), -1, I32)
        distant = jnp.full((1, BLK), -1, I32)
        for p in range(TOTACT):
            n = jnp.where(p < in_first, 0, 1)
            i = jnp.minimum(jnp.where(p < in_first, p, p - in_first), ids_ref.shape[2] - 1)
            alive = p < in_all
            block = ids_ref[0, n, i]
            act[2 * p] = block
            act[2 * p + 1] = jnp.where(alive, block, -1)
            centre = jnp.where(wide_lane == p, jnp.where(alive, block, -1), centre)
            for k in range(near_count):
                other = near_ref[0, k, n, i]
                near[p * near_count + k] = other
                centre = jnp.where(
                    wide_lane == TOTACT + p * near_count + k, jnp.where(alive, other, -1), centre
                )
            for k in range(far_count):
                other = far_ref[0, n, k, i]
                far[p * far_count + k] = other
                distant = jnp.where(wide_lane == p * far_count + k, jnp.where(alive, other, -1), distant)
        table[0:1, :] = centre
        table[1:2, :] = distant
        table[3:8, :] = jnp.full((5, BLK), -1, I32)

    first = copy(0)
    first.start()
    kept = {1: gather(tiles, rows[1])}
    relate(0)
    compact()
    first.wait()
    factors = []
    for level in range(1, LEVELS):
        factors.append(
            jnp.concatenate([*pieces(landed[level - 1]), jnp.ones((8, width), F32)], axis=0).astype(jnp.bfloat16)
        )
        out = kept[level]
        for early in range(level):
            found = jnp.dot(factors[early], match[pair[level, early]], preferred_element_type=F32)
            value = (found[0:8] + found[8:16]) + found[16:24]
            out = jnp.where(found[24:32] > 0.5, value, out)
        leaving[level] = out
        moving = copy(level)
        moving.start()
        if level + 1 < LEVELS:
            kept[level + 1] = gather(tiles, rows[level + 1])
        relate(level)
        if level == LEVELS - 1:
            settle(0, range(LEVELS - 1))
        moving.wait()
    settle(1, [LEVELS - 1])

    def pack(p, _):
        for t in range(slots):
            tile = tiles[exp_ref[0, t, p]]
            stage[pl.ds(p * (SENT * slots) + t, SENT, stride=slots), :] = tile[0:SENT]
        return 0

    lax.fori_loop(0, peers, pack, 0)

    def exchange(phase, source, target, count):
        for apart in range(1, peers):
            peer = lax.rem(me + apart, peers)
            pltpu.make_async_remote_copy(
                src_ref=source.at[pl.ds(peer * count, count), :],
                dst_ref=target.at[pl.ds(me * count, count), :],
                send_sem=ssem.at[phase],
                recv_sem=rsem.at[phase],
                device_id=(gx, peer),
                device_id_type=MESH,
            ).start()
        return phase

    def finish(phase, source, target, count):
        here = pl.ds(me * count, count)
        target[here, :] = source[here, :]
        whole = pl.ds(0, (peers - 1) * count)
        pltpu.make_async_remote_copy(
            src_ref=source.at[whole, :],
            dst_ref=target.at[whole, :],
            send_sem=ssem.at[phase],
            recv_sem=rsem.at[phase],
            device_id=(gx, lax.rem(me + 1, peers)),
            device_id_type=MESH,
        ).wait()

    sent_blocks = exchange(0, stage, ghosts, SENT * slots)

    def pack_rest(p, ids):
        for t in range(slots):
            block = exp_ref[0, t, p]
            tile = tiles[block]
            row = pl.ds(p * slots + t, 1)
            stage_h[row, :] = tile[4:5]
            energies[row, :] = tile[5:6]
            stage_p[row, :] = tile[6:7]
            expcol[row, :] = jnp.full((1, BLK), block, I32)
            ids = jnp.where(wide_lane == p * slots + t, block, ids)
        return ids

    table[2:3, :] = lax.fori_loop(0, peers, pack_rest, jnp.full((1, BLK), -1, I32))
    centres[...] = jnp.zeros_like(centres)
    for p in range(TOTACT):
        tile = tiles[act[2 * p]]
        centres[p * CHAN : p * CHAN + 7, :] = tile[0:7]
        centres[p * CHAN + 7 : p * CHAN + 8, :] = 0.5 / tile[4:5]
    cols[...] = jnp.transpose(centres[...])

    def sliced(q):
        return slice(q * PART, (q + 1) * PART)

    def local_row(block, channel):
        return tiles[block, channel : channel + 1, :]

    def ghost_base(ghost):
        return (ghost >> SLOT_BITS) * (SENT * slots) + (ghost & (slots - 1))

    def ghost_row(base, channel):
        return ghosts[pl.ds(base + channel * slots, 1), :]

    def separation(mine, theirs):
        dx, dy, dz = (a - b for a, b in zip(mine, theirs))
        square = dx * dx + dy * dy + dz * dz
        return square * lax.rsqrt(jnp.maximum(square, TINY))

    def density_term(r, inverse, mass5, mass4):
        fall = jnp.maximum(1.0 - r * inverse, 0.0)
        fall2 = fall * fall
        return (fall2 * fall2) * (mass5 - mass4 * fall)

    def pair_weight(r, smooth, mass, other_smooth, other_mass):
        inverse = 1.0 / (smooth + other_smooth)
        fall = jnp.maximum(1.0 - r * inverse, 0.0) * inverse
        return ((fall * fall) * fall * (inverse * inverse)) * (mass * other_mass)

    def local_first(p, _):
        others = [act[2 * p]] + [near[p * near_count + k] for k in range(near_count)]
        rows = [[local_row(b, c) for c in range(5)] for b in others]
        masses = [(5.0 * row[3], 4.0 * row[3]) for row in rows]
        for q in range(BLK // PART):
            here = sliced(q)
            chunk = cols[here, :]
            mine = [picked(chunk, p * CHAN + c) for c in (0, 1, 2, 3, 4, 7)]
            for c in range(6):
                wide[p, c, here, :] = mine[c]
            total = None
            for n, row in enumerate(rows):
                r = separation(mine[0:3], row[0:3])
                term = density_term(r, mine[5], *masses[n])
                total = term if total is None else total + term
                weights[p, n, here, :] = pair_weight(r, mine[4], mine[3], row[4], row[3])
            sums[p, here, :] = total
        return 0

    lax.fori_loop(0, TOTACT, local_first, 0)
    finish(sent_blocks, stage, ghosts, SENT * slots)
    sent_h = exchange(1, stage_h, ghost_h, slots)

    def density_of(p):
        smooth = centres[pl.ds(p * CHAN + 4, 1), :]
        rhos[pl.ds(p, 1), :] = KERNEL_NORM / (smooth * smooth * smooth) * row_sums(sums[p])

    def ghost_first(p, _):
        others = [ghost_base(far[p * far_count + k]) for k in range(far_count)]
        rows = [[ghost_row(g, c) for c in range(4)] for g in others]
        masses = [(5.0 * row[3], 4.0 * row[3]) for row in rows]
        density_of(jnp.maximum(p - 1, 0))
        for q in range(BLK // PART):
            here = sliced(q)
            mine = [wide[p, c, here, :] for c in (0, 1, 2)]
            inverse = wide[p, 5, here, :]
            total = sums[p, here, :]
            for n, row in enumerate(rows):
                r = separation(mine, row[0:3])
                weights[p, 1 + near_count + n, here, :] = r
                total = total + density_term(r, inverse, *masses[n])
            sums[p, here, :] = total
        return 0

    lax.fori_loop(0, TOTACT, ghost_first, 0)
    density_of(TOTACT - 1)
    fresh = [rhos[p : p + 1, :] for p in range(TOTACT)]
    exported = stage_p[...]
    export_block = expcol[...]
    for p in range(TOTACT):
        exported = jnp.where(export_block == act[2 * p + 1], fresh[p], exported)
    stage_p[...] = FORCE_NORM * (energies[...] / exported)
    finish(sent_h, stage_h, ghost_h, slots)
    sent_p = exchange(2, stage_p, ghost_p, slots)

    block_number = lax.broadcasted_iota(I32, (blocks, BLK), 0)
    dens = tiles[:, 6, :]
    for p in range(TOTACT):
        dens = jnp.where(block_number == act[2 * p + 1], fresh[p], dens)
    dens_out[...] = dens
    pj[...] = FORCE_NORM * (tiles[:, 5, :] / dens)
    rhos[...] = jnp.zeros_like(rhos)
    for p in range(TOTACT):
        rhos[p : p + 1, :] = FORCE_NORM * (centres[p * CHAN + 5 : p * CHAN + 6, :] / fresh[p])
    cols[...] = jnp.transpose(rhos[...])
    adds[...] = jnp.zeros_like(adds)
    fars[...] = jnp.zeros_like(fars)

    def ghost_second(p, _):
        others = [far[p * far_count + k] for k in range(far_count)]
        rows = [[ghost_row(ghost_base(g), 3), ghost_h[pl.ds(g, 1), :]] for g in others]
        for q in range(BLK // PART):
            here = sliced(q)
            mass, smooth = wide[p, 3, here, :], wide[p, 4, here, :]
            for n, row in enumerate(rows):
                r = weights[p, 1 + near_count + n, here, :]
                weights[p, 1 + near_count + n, here, :] = pair_weight(r, smooth, mass, row[1], row[0])
            wide[p, 5, here, :] = picked(cols[here, :], p)
        return 0

    lax.fori_loop(0, TOTACT, ghost_second, 0)

    def force_phase(p, first, rows, skip, again):
        kept = len(rows) - skip
        carry = [None] * (3 * kept)
        for q in range(BLK // PART):
            here = sliced(q)
            mine = [wide[p, c, here, :] for c in (0, 1, 2)]
            pressure = wide[p, 5, here, :]
            total = [forces[c, p, here, :] for c in range(3)] if again else [None] * 3
            for n, row in enumerate(rows):
                weight = weights[p, first + n, here, :] * (pressure + row[3])
                for c in range(3):
                    push = weight * (mine[c] - row[c])
                    total[c] = push if total[c] is None else total[c] + push
                    if n >= skip:
                        at = (n - skip) * 3 + c
                        down = [push[8 * i : 8 * i + 8] for i in range(PART // 8)]
                        if carry[at] is not None:
                            down.append(carry[at])
                        while len(down) > 1:
                            down = down[2:] + [down[0] + down[1]]
                        carry[at] = down[0]
            for c in range(3):
                forces[c, p, here, :] = total[c]
        return [[-jnp.sum(carry[n * 3 + c], axis=0, keepdims=True) for c in range(3)] for n in range(kept)]

    finish(sent_p, stage_p, ghost_p, slots)

    def ghost_force(p, _):
        others = [far[p * far_count + k] for k in range(far_count)]
        rows = [[ghost_row(ghost_base(g), c) for c in range(3)] + [ghost_p[pl.ds(g, 1), :]] for g in others]
        found = force_phase(p, 1 + near_count, rows, 0, False)
        for n in range(far_count):
            for c in range(3):
                fars[c, pl.ds(p * far_count + n, 1), :] = found[n][c]
        return 0

    lax.fori_loop(0, TOTACT, ghost_force, 0)
    back_stage[...] = placed_sum(table[1:2, :], abreast(fars), peers * slots)
    sent_back = exchange(3, back_stage, back_land, slots)

    def centre_force(p):
        for c in range(3):
            adds[c, pl.ds(p, 1), :] = row_sums(forces[c, p])

    def local_force(p, _):
        others = [act[2 * p]] + [near[p * near_count + k] for k in range(near_count)]
        rows = [[local_row(b, c) for c in range(3)] + [pj[pl.ds(b, 1), :]] for b in others]
        centre_force(jnp.maximum(p - 1, 0))
        found = force_phase(p, 0, rows, 1, True)
        for n in range(near_count):
            for c in range(3):
                adds[c, pl.ds(TOTACT + p * near_count + n, 1), :] = found[n][c]
        return 0

    lax.fori_loop(0, TOTACT, local_force, 0)
    centre_force(TOTACT - 1)
    totals = placed_sum(table[0:1, :], abreast(adds), blocks)
    finish(sent_back, back_stage, back_land, slots)
    totals = totals + placed_sum(table[2:3, :], back_land[...], blocks)
    mass = tiles[:, 3, :]
    for c in range(3):
        held_force[c] = totals[:, c * BLK : (c + 1) * BLK] / mass

    def put(b8, _):
        for k in range(8):
            b = b8 * 8 + k
            for c in range(3):
                accel_out[c : c + 1, pl.ds(pl.multiple_of(b * BLK, BLK), BLK)] = held_force[c, pl.ds(b, 1), :]
        return 0

    lax.fori_loop(0, blocks // 8, put, 0)


def shards(
    particles, mig_count, mig_rows, active_ids, active_count, local_nbrs, ghost_slots, export_blocks
):
    count = particles.shape[1]
    blocks = count // BLK
    width = mig_rows.shape[2]
    peers, slots = export_blocks.shape[1:]
    near_count, far_count = local_nbrs.shape[3], ghost_slots.shape[3]
    limit = 60 * 1024 * 1024
    struct = jax.ShapeDtypeStruct
    ghost_count = peers * slots
    square = VMEM((BLK, BLK), F32)
    each = VMEM((ghost_count, BLK), F32)
    density, accel = pl.pallas_call(
        substep_kernel,
        name="substep",
        out_shape=(struct((blocks, BLK), F32), struct((3, count), F32)),
        in_specs=[spec(SMEM)] * 6 + [spec(VMEM)] * 2,
        out_specs=(spec(VMEM),) * 2,
        scratch_shapes=[
            VMEM((blocks, CHAN, BLK), F32),
            VMEM((LEVELS, CHAN, width), F32),
            VMEM((LEVELS, CHAN, width), F32),
            VMEM((6, width, width), jnp.bfloat16),
            VMEM((2, blocks, BLK), I32),
            VMEM((2, blocks, BLK), I32),
            VMEM((8, BLK), I32),
            SMEM((2 * TOTACT,), I32),
            SMEM((TOTACT * near_count,), I32),
            SMEM((TOTACT * far_count,), I32),
            VMEM((ghost_count * SENT, BLK), F32),
            each,
            each,
            each,
            VMEM((ghost_count, BLK), I32),
            VMEM((ghost_count * SENT, BLK), F32),
            each,
            each,
            VMEM((ghost_count, 3 * BLK), F32),
            VMEM((ghost_count, 3 * BLK), F32),
            square,
            square,
            VMEM((TOTACT, 6, BLK, BLK), F32),
            VMEM((TOTACT, BLK, BLK), F32),
            VMEM((TOTACT, 1 + near_count + far_count, BLK, BLK), F32),
            square,
            VMEM((blocks, BLK), F32),
            VMEM((3, ADDED, BLK), F32),
            VMEM((3, ADDED, BLK), F32),
            VMEM((3, TOTACT, BLK, BLK), F32),
            VMEM((3, blocks, BLK), F32),
            pltpu.SemaphoreType.DMA((LEVELS,)),
            pltpu.SemaphoreType.DMA((LEVELS,)),
            pltpu.SemaphoreType.DMA((4,)),
            pltpu.SemaphoreType.DMA((4,)),
        ],
        compiler_params=pltpu.CompilerParams(collective_id=0, has_side_effects=True, vmem_limit_bytes=limit),
    )(
        mig_count, active_ids, active_count,
        local_nbrs.transpose(0, 3, 1, 2), ghost_slots.transpose(0, 1, 3, 2), export_blocks.transpose(0, 2, 1),
        mig_rows, particles,
    )
    return density.reshape(-1), accel


def solution(mesh):
    placed = (
        P(None, ("gx", "gy")),
        P(("gx", "gy"), None),
        P(("gx", "gy"), None, None),
        P(("gx", "gy"), None, None),
        P(("gx", "gy"), None),
        P(("gx", "gy"), None, None, None),
        P(("gx", "gy"), None, None, None),
        P(("gx", "gy"), None, None),
    )
    return jax.shard_map(
        shards,
        mesh=mesh,
        in_specs=placed,
        out_specs=(P(("gx", "gy")), P(None, ("gx", "gy"))),
        check_vma=False,
    )
```

```python
import functools
import math

import jax
import jax.numpy as jnp
from jax import lax
from jax.experimental import pallas as pl
from jax.experimental.pallas import tpu as pltpu
from jax.sharding import PartitionSpec as P

BLK = 128
TOTACT = 12
LEVELS = 4
CHAN = 8
SENT = 4
SLOT_BITS = 3
ADDED = 64
WHICH_MAP = (0, 1, 1, 2)

KERNEL_NORM = 21.0 / (16.0 * math.pi)
GAMMA_LESS = 2.0 / 3.0
FORCE_NORM = GAMMA_LESS * 32.0 * 5.0 * KERNEL_NORM
TINY = 1e-37
PART = 32
MESH = pl.DeviceIdType.MESH
VMEM = pltpu.VMEM
SMEM = pltpu.SMEM
F32 = jnp.float32
I32 = jnp.int32


def lanes(shape):
    return lax.broadcasted_iota(I32, shape, len(shape) - 1)


def spec(space):
    return pl.BlockSpec(memory_space=space)


def flipped(index, bit):
    return index + bit - 2 * bit * (lax.div(index, bit) % 2)


def picked(chunk, lane_number):
    return jnp.take_along_axis(
        chunk, jnp.full(chunk.shape, lane_number, I32), axis=1, mode="promise_in_bounds"
    )


def gather(tiles, rows):
    parts = []
    for part in range(rows.shape[1] // BLK):
        here = rows[:, part * BLK : (part + 1) * BLK]
        block = jnp.broadcast_to(here >> 7, (CHAN, BLK))
        spot = jnp.broadcast_to(here & 127, (CHAN, BLK))

        def step(n, held):
            held = list(held)
            for k in range(64):
                b = n * 64 + k
                tile = tiles[b]
                turned = jnp.take_along_axis(tile, spot, axis=1, mode="promise_in_bounds")
                held[k % 4] = jnp.where(block == b, turned, held[k % 4])
            return tuple(held)

        zero = jnp.zeros((CHAN, BLK), F32)
        held = lax.fori_loop(0, tiles.shape[0] // 64, step, (zero,) * 4)
        parts.append((held[0] + held[1]) + (held[2] + held[3]))
    return jnp.concatenate(parts, axis=1)


def pieces(value):
    first = value.astype(jnp.bfloat16).astype(F32)
    rest = value - first
    second = rest.astype(jnp.bfloat16).astype(F32)
    return first, second, rest - second


def abreast(ref):
    return jnp.concatenate([ref[0], ref[1], ref[2]], axis=1)


def row_sums(value):
    return jnp.sum(jnp.transpose(value), axis=0, keepdims=True)


def placed_sum(ids, terms, count):
    depth = terms.shape[0]
    owner = lax.broadcasted_iota(I32, (count, depth), 0)
    chosen = jnp.where(owner == ids[:, 0:depth], 1.0, 0.0)
    chosen = jnp.concatenate([chosen] * 3, axis=1).astype(jnp.bfloat16)
    split = jnp.concatenate(pieces(terms), axis=0).astype(jnp.bfloat16)
    return jnp.dot(chosen, split, preferred_element_type=F32)


def substep_kernel(
    count_ref, ids_ref, live_ref, near_ref, far_ref, exp_ref, rows_ref, x_ref,
    dens_out, force_out,
    tiles, leaving, landed, match, map_lane, map_part, table, act, near, far,
    stage, stage_h, stage_p, energies, expcol, ghosts, ghost_h, ghost_p, back_stage, back_land,
    centres, cols, wide, sums, weights, rhos, pj, adds, fars, forces,
    mig_ssem, mig_rsem, ssem, rsem,
):
    gx, me = lax.axis_index("gx"), lax.axis_index("gy")
    peers = lax.axis_size("gy")
    slots = exp_ref.shape[1]
    width = rows_ref.shape[2]
    parts = width // BLK
    blocks = x_ref.shape[1] // BLK
    near_count, far_count = near_ref.shape[1], far_ref.shape[2]
    partners = [(flipped(gx, 2), me), (flipped(gx, 1), me), (gx, flipped(me, 2)), (gx, flipped(me, 1))]
    low, high = lax.rem(me, 4), lax.div(me, 4)
    across = flipped(low, 2)
    column = (across, flipped(across, 1), flipped(low, 1), low)
    order = [lax.rem(high + apart, peers // 4) * 4 + z for z in column for apart in (2, 1, 3, 0)][: peers - 1]
    around = [(gx, peer) for peer in order]

    barrier = pltpu.get_barrier_semaphore()
    for other in partners[0:2] + around:
        pl.semaphore_signal(barrier, inc=1, device_id=other, device_id_type=MESH)

    def load(b8, _):
        for k in range(8):
            b = b8 * 8 + k
            tiles[b, 0:7, :] = x_ref[:, pl.ds(pl.multiple_of(b * BLK, BLK), BLK)]
            tiles[b, 7:8, :] = jnp.zeros((1, BLK), F32)
        return 0

    lax.fori_loop(0, blocks // 8, load, 0)
    rows = [rows_ref[0, level : level + 1, :] for level in range(LEVELS)]
    leaving[0] = gather(tiles, rows[0])
    pl.semaphore_wait(barrier, peers + 1)

    def copy(level):
        return pltpu.make_async_remote_copy(
            src_ref=leaving.at[level],
            dst_ref=landed.at[level],
            send_sem=mig_ssem.at[level],
            recv_sem=mig_rsem.at[level],
            device_id=partners[level],
            device_id_type=MESH,
        )

    pair = {}
    for early in range(LEVELS - 1):
        for late in range(early + 1, LEVELS):
            pair[late, early] = len(pair)

    def relate(early):
        keys = jnp.where(lanes((1, width)) < count_ref[0, early], rows[early], -1)
        lane = lanes((BLK, BLK))
        slot = lax.broadcasted_iota(I32, (BLK, BLK), 0)
        owner = lax.broadcasted_iota(I32, (blocks, width), 0)
        spots = []
        for part in range(parts):
            down = jnp.transpose(jnp.broadcast_to(keys[:, part * BLK : (part + 1) * BLK], (BLK, BLK)))
            hit = (down & 127) == lane
            spots.append(
                jnp.concatenate(
                    [jnp.where(hit, (slot + 1).astype(F32), 0.0), jnp.where(hit, float(part), 0.0)], axis=1
                ).astype(jnp.bfloat16)
            )
            down = jnp.concatenate([down] * parts, axis=1)
            for late in range(early + 1, LEVELS):
                match[pair[late, early], part * BLK : (part + 1) * BLK, :] = jnp.where(
                    down == rows[late], 1.0, 0.0
                ).astype(jnp.bfloat16)
        held = jnp.where(owner == (keys >> 7), 1.0, 0.0).astype(jnp.bfloat16)
        found = jnp.dot(held, jnp.concatenate(spots, axis=0), preferred_element_type=F32).astype(I32)
        arriving = found[:, 0:BLK] > 0
        spot = found[:, 0:BLK] - 1
        part = found[:, BLK:] + early * parts
        which = WHICH_MAP[early]
        if early == 2:
            spot = jnp.where(arriving, spot, map_lane[which])
            part = jnp.where(arriving, part, map_part[which])
        else:
            spot = jnp.where(arriving, spot, 0)
            part = jnp.where(arriving, part, -1)
        map_lane[which] = spot
        map_part[which] = part

    def settle(which_map, levels):
        numbers = [level * parts + part for level in levels for part in range(parts)]
        arrived = {n: landed[n // parts, :, n % parts * BLK : (n % parts + 1) * BLK] for n in numbers}

        def step(b8, _):
            for k in range(8):
                b = b8 * 8 + k
                spot = jnp.broadcast_to(map_lane[which_map, pl.ds(b, 1), :], (CHAN, BLK))
                which = jnp.broadcast_to(map_part[which_map, pl.ds(b, 1), :], (CHAN, BLK))
                tile = tiles[b]
                for n in numbers:
                    turned = jnp.take_along_axis(arrived[n], spot, axis=1, mode="promise_in_bounds")
                    tile = jnp.where(which == n, turned, tile)
                tiles[b] = tile
            return 0

        lax.fori_loop(0, blocks // 8, step, 0)

    wide_lane = lanes((1, BLK))

    def compact():
        in_first = live_ref[0, 0]
        in_all = in_first + live_ref[0, 1]
        centre = jnp.full((1, BLK), -1, I32)
        distant = jnp.full((1, BLK), -1, I32)
        for p in range(TOTACT):
            n = jnp.where(p < in_first, 0, 1)
            i = jnp.minimum(jnp.where(p < in_first, p, p - in_first), ids_ref.shape[2] - 1)
            alive = p < in_all
            block = ids_ref[0, n, i]
            act[2 * p] = block
            act[2 * p + 1] = jnp.where(alive, block, -1)
            centre = jnp.where(wide_lane == p, jnp.where(alive, block, -1), centre)
            for k in range(near_count):
                other = near_ref[0, k, n, i]
                near[p * near_count + k] = other
                centre = jnp.where(
                    wide_lane == TOTACT + p * near_count + k, jnp.where(alive, other, -1), centre
                )
            for k in range(far_count):
                other = far_ref[0, n, k, i]
                far[p * far_count + k] = other
                distant = jnp.where(wide_lane == p * far_count + k, jnp.where(alive, other, -1), distant)
        table[0:1, :] = centre
        table[1:2, :] = distant
        table[3:8, :] = jnp.full((5, BLK), -1, I32)

    first = copy(0)
    first.start()
    kept = {1: gather(tiles, rows[1])}
    relate(0)
    relate(1)
    first.wait()
    factors = []
    for level in range(1, LEVELS):
        factors.append(
            jnp.concatenate([*pieces(landed[level - 1]), jnp.ones((8, width), F32)], axis=0).astype(jnp.bfloat16)
        )
        out = kept[level]
        for early in range(level):
            found = jnp.dot(factors[early], match[pair[level, early]], preferred_element_type=F32)
            value = (found[0:8] + found[8:16]) + found[16:24]
            out = jnp.where(found[24:32] > 0.5, value, out)
        leaving[level] = out
        moving = copy(level)
        moving.start()
        if level + 1 < LEVELS:
            kept[level + 1] = gather(tiles, rows[level + 1])
        if level > 1:
            relate(level)
            settle(level - 2, [[0], [1, 2]][level - 2])
        moving.wait()

    def send(phase, source, target, count, peer):
        pltpu.make_async_remote_copy(
            src_ref=source.at[pl.ds(peer * count, count), :],
            dst_ref=target.at[pl.ds(me * count, count), :],
            send_sem=ssem.at[phase],
            recv_sem=rsem.at[phase],
            device_id=(gx, peer),
            device_id_type=MESH,
        ).start()

    def exchange(phase, source, target, count):
        for peer in order:
            send(phase, source, target, count, peer)
        return phase

    def finish(phase, source, target, count):
        here = pl.ds(me * count, count)
        target[here, :] = source[here, :]
        whole = pl.ds(0, (peers - 1) * count)
        pltpu.make_async_remote_copy(
            src_ref=source.at[whole, :],
            dst_ref=target.at[whole, :],
            send_sem=ssem.at[phase],
            recv_sem=rsem.at[phase],
            device_id=(gx, order[0]),
            device_id_type=MESH,
        ).wait()

    last = LEVELS - 1
    arrived = [landed[last, :, part * BLK : (part + 1) * BLK] for part in range(parts)]
    for peer in order + [me]:
        for t in range(slots):
            block = exp_ref[0, t, peer]
            spot = jnp.broadcast_to(map_lane[2, pl.ds(block, 1), :], (CHAN, BLK))
            which = jnp.broadcast_to(map_part[2, pl.ds(block, 1), :], (CHAN, BLK))
            tile = tiles[block]
            for part in range(parts):
                turned = jnp.take_along_axis(arrived[part], spot, axis=1, mode="promise_in_bounds")
                tile = jnp.where(which == last * parts + part, turned, tile)
            stage[pl.ds(peer * (SENT * slots) + t, SENT, stride=slots), :] = tile[0:SENT]
        if peer is not me:
            send(0, stage, ghosts, SENT * slots, peer)
    sent_blocks = 0
    settle(2, [last])
    compact()

    def pack_rest(p, ids):
        for t in range(slots):
            block = exp_ref[0, t, p]
            tile = tiles[block]
            row = pl.ds(p * slots + t, 1)
            stage_h[row, :] = tile[4:5]
            energies[row, :] = tile[5:6]
            stage_p[row, :] = tile[6:7]
            expcol[row, :] = jnp.full((1, BLK), block, I32)
            ids = jnp.where(wide_lane == p * slots + t, block, ids)
        return ids

    table[2:3, :] = lax.fori_loop(0, peers, pack_rest, jnp.full((1, BLK), -1, I32))
    centres[...] = jnp.zeros_like(centres)
    for p in range(TOTACT):
        tile = tiles[act[2 * p]]
        centres[p * CHAN : p * CHAN + 7, :] = tile[0:7]
        centres[p * CHAN + 7 : p * CHAN + 8, :] = 0.5 / tile[4:5]
    cols[...] = jnp.transpose(centres[...])

    def sliced(q):
        return slice(q * PART, (q + 1) * PART)

    def local_row(block, channel):
        return tiles[block, channel : channel + 1, :]

    def ghost_base(ghost):
        return (ghost >> SLOT_BITS) * (SENT * slots) + (ghost & (slots - 1))

    def ghost_row(base, channel):
        return ghosts[pl.ds(base + channel * slots, 1), :]

    def separation(mine, theirs):
        dx, dy, dz = (a - b for a, b in zip(mine, theirs))
        square = dx * dx + dy * dy + dz * dz
        return square * lax.rsqrt(jnp.maximum(square, TINY))

    def density_term(r, inverse, mass5, mass4):
        fall = jnp.maximum(1.0 - r * inverse, 0.0)
        fall2 = fall * fall
        return (fall2 * fall2) * (mass5 - mass4 * fall)

    def pair_weight(r, smooth, mass, other_smooth, other_mass):
        inverse = 1.0 / (smooth + other_smooth)
        fall = jnp.maximum(1.0 - r * inverse, 0.0) * inverse
        return ((fall * fall) * fall * (inverse * inverse)) * (mass * other_mass)

    def local_first(p, _):
        others = [act[2 * p]] + [near[p * near_count + k] for k in range(near_count)]
        rows = [[local_row(b, c) for c in range(5)] for b in others]
        masses = [(5.0 * row[3], 4.0 * row[3]) for row in rows]
        for q in range(BLK // PART):
            here = sliced(q)
            chunk = cols[here, :]
            mine = [picked(chunk, p * CHAN + c) for c in (0, 1, 2, 3, 4, 7)]
            for c in range(6):
                wide[p, c, here, :] = mine[c]
            total = None
            for n, row in enumerate(rows):
                r = separation(mine[0:3], row[0:3])
                term = density_term(r, mine[5], *masses[n])
                total = term if total is None else total + term
                weights[p, n, here, :] = pair_weight(r, mine[4], mine[3], row[4], row[3])
            sums[p, here, :] = total
        return 0

    lax.fori_loop(0, TOTACT, local_first, 0)
    finish(sent_blocks, stage, ghosts, SENT * slots)
    sent_h = exchange(1, stage_h, ghost_h, slots)

    def density_of(p):
        smooth = centres[pl.ds(p * CHAN + 4, 1), :]
        rhos[pl.ds(p, 1), :] = KERNEL_NORM / (smooth * smooth * smooth) * row_sums(sums[p])

    def ghost_first(p, _):
        others = [ghost_base(far[p * far_count + k]) for k in range(far_count)]
        rows = [[ghost_row(g, c) for c in range(4)] for g in others]
        masses = [(5.0 * row[3], 4.0 * row[3]) for row in rows]
        density_of(jnp.maximum(p - 1, 0))
        for q in range(BLK // PART):
            here = sliced(q)
            mine = [wide[p, c, here, :] for c in (0, 1, 2)]
            inverse = wide[p, 5, here, :]
            total = sums[p, here, :]
            for n, row in enumerate(rows):
                r = separation(mine, row[0:3])
                weights[p, 1 + near_count + n, here, :] = r
                total = total + density_term(r, inverse, *masses[n])
            sums[p, here, :] = total
        return 0

    lax.fori_loop(0, TOTACT, ghost_first, 0)
    density_of(TOTACT - 1)
    fresh = [rhos[p : p + 1, :] for p in range(TOTACT)]
    exported = stage_p[...]
    export_block = expcol[...]
    for p in range(TOTACT):
        exported = jnp.where(export_block == act[2 * p + 1], fresh[p], exported)
    stage_p[...] = FORCE_NORM * (energies[...] / exported)
    sent_p = exchange(2, stage_p, ghost_p, slots)

    block_number = lax.broadcasted_iota(I32, (blocks, BLK), 0)
    dens = tiles[:, 6, :]
    for p in range(TOTACT):
        dens = jnp.where(block_number == act[2 * p + 1], fresh[p], dens)
    dens_out[...] = dens
    pj[...] = FORCE_NORM * (tiles[:, 5, :] / dens)
    rhos[...] = jnp.zeros_like(rhos)
    for p in range(TOTACT):
        rhos[p : p + 1, :] = FORCE_NORM * (centres[p * CHAN + 5 : p * CHAN + 6, :] / fresh[p])
    cols[...] = jnp.transpose(rhos[...])
    adds[...] = jnp.zeros_like(adds)
    fars[...] = jnp.zeros_like(fars)

    def ghost_second(p, _):
        others = [far[p * far_count + k] for k in range(far_count)]
        rows = [[ghost_row(ghost_base(g), 3), ghost_h[pl.ds(g, 1), :]] for g in others]
        for q in range(BLK // PART):
            here = sliced(q)
            mass, smooth = wide[p, 3, here, :], wide[p, 4, here, :]
            for n, row in enumerate(rows):
                r = weights[p, 1 + near_count + n, here, :]
                weights[p, 1 + near_count + n, here, :] = pair_weight(r, smooth, mass, row[1], row[0])
            wide[p, 5, here, :] = picked(cols[here, :], p)
        return 0

    finish(sent_h, stage_h, ghost_h, slots)
    lax.fori_loop(0, TOTACT, ghost_second, 0)

    def force_phase(p, first, rows, skip, again):
        kept = len(rows) - skip
        carry = [None] * (3 * kept)
        for q in range(BLK // PART):
            here = sliced(q)
            mine = [wide[p, c, here, :] for c in (0, 1, 2)]
            pressure = wide[p, 5, here, :]
            total = [forces[c, p, here, :] for c in range(3)] if again else [None] * 3
            for n, row in enumerate(rows):
                weight = weights[p, first + n, here, :] * (pressure + row[3])
                for c in range(3):
                    push = weight * (mine[c] - row[c])
                    total[c] = push if total[c] is None else total[c] + push
                    if n >= skip:
                        at = (n - skip) * 3 + c
                        down = [push[8 * i : 8 * i + 8] for i in range(PART // 8)]
                        if carry[at] is not None:
                            down.append(carry[at])
                        while len(down) > 1:
                            down = down[2:] + [down[0] + down[1]]
                        carry[at] = down[0]
            for c in range(3):
                forces[c, p, here, :] = total[c]
        return [[-jnp.sum(carry[n * 3 + c], axis=0, keepdims=True) for c in range(3)] for n in range(kept)]

    finish(sent_p, stage_p, ghost_p, slots)

    def ghost_force(c):
        def body(p, _):
            others = [far[p * far_count + k] for k in range(far_count)]
            rows = [(ghost_row(ghost_base(g), c), ghost_p[pl.ds(g, 1), :] if c == 0 else None) for g in others]
            carry = [None] * far_count
            for q in range(BLK // PART):
                here = sliced(q)
                mine = wide[p, c, here, :]
                total = None
                for n, (row, pressure) in enumerate(rows):
                    weight = weights[p, 1 + near_count + n, here, :]
                    if c == 0:
                        weight = weight * (wide[p, 5, here, :] + pressure)
                        weights[p, 1 + near_count + n, here, :] = weight
                    push = weight * (mine - row)
                    total = push if total is None else total + push
                    down = [push[8 * i : 8 * i + 8] for i in range(PART // 8)]
                    if carry[n] is not None:
                        down.append(carry[n])
                    while len(down) > 1:
                        down = down[2:] + [down[0] + down[1]]
                    carry[n] = down[0]
                forces[c, p, here, :] = total
            for n in range(far_count):
                fars[c, pl.ds(p * far_count + n, 1), :] = -jnp.sum(carry[n], axis=0, keepdims=True)
            return 0

        lax.fori_loop(0, TOTACT, body, 0)

    for c in range(3):
        ghost_force(c)
        back_stage[c] = placed_sum(table[1:2, :], fars[c], peers * slots)
        exchange(3 + c, back_stage.at[c], back_land.at[c], slots)

    def centre_force(p):
        for c in range(3):
            adds[c, pl.ds(p, 1), :] = row_sums(forces[c, p])

    def local_force(p, _):
        others = [act[2 * p]] + [near[p * near_count + k] for k in range(near_count)]
        rows = [[local_row(b, c) for c in range(3)] + [pj[pl.ds(b, 1), :]] for b in others]
        centre_force(jnp.maximum(p - 1, 0))
        found = force_phase(p, 0, rows, 1, True)
        for n in range(near_count):
            for c in range(3):
                adds[c, pl.ds(TOTACT + p * near_count + n, 1), :] = found[n][c]
        return 0

    lax.fori_loop(0, TOTACT, local_force, 0)
    centre_force(TOTACT - 1)
    totals = placed_sum(table[0:1, :], abreast(adds), blocks)
    for c in range(3):
        finish(3 + c, back_stage.at[c], back_land.at[c], slots)
    totals = totals + placed_sum(table[2:3, :], abreast(back_land), blocks)
    mass = tiles[:, 3, :]
    for c in range(3):
        force_out[c] = totals[:, c * BLK : (c + 1) * BLK] / mass


def deliver_kernel(dens_ref, force_ref, dens_out, accel_out):
    dens_out[...] = dens_ref[...]

    def put(b8, _):
        for k in range(8):
            b = b8 * 8 + k
            for c in range(3):
                accel_out[c : c + 1, pl.ds(pl.multiple_of(b * BLK, BLK), BLK)] = force_ref[c, pl.ds(b, 1), :]
        return 0

    lax.fori_loop(0, dens_ref.shape[0] // 8, put, 0)


def shards(
    particles, mig_count, mig_rows, active_ids, active_count, local_nbrs, ghost_slots, export_blocks
):
    count = particles.shape[1]
    blocks = count // BLK
    width = mig_rows.shape[2]
    peers, slots = export_blocks.shape[1:]
    near_count, far_count = local_nbrs.shape[3], ghost_slots.shape[3]
    limit = 60 * 1024 * 1024
    struct = jax.ShapeDtypeStruct
    ghost_count = peers * slots
    square = VMEM((BLK, BLK), F32)
    each = VMEM((ghost_count, BLK), F32)
    dens, force = pl.pallas_call(
        substep_kernel,
        name="substep",
        out_shape=(struct((blocks, BLK), F32), struct((3, blocks, BLK), F32)),
        in_specs=[spec(SMEM)] * 6 + [spec(VMEM)] * 2,
        out_specs=(spec(VMEM),) * 2,
        scratch_shapes=[
            VMEM((blocks, CHAN, BLK), F32),
            VMEM((LEVELS, CHAN, width), F32),
            VMEM((LEVELS, CHAN, width), F32),
            VMEM((6, width, width), jnp.bfloat16),
            VMEM((3, blocks, BLK), I32),
            VMEM((3, blocks, BLK), I32),
            VMEM((8, BLK), I32),
            SMEM((2 * TOTACT,), I32),
            SMEM((TOTACT * near_count,), I32),
            SMEM((TOTACT * far_count,), I32),
            VMEM((ghost_count * SENT, BLK), F32),
            each,
            each,
            each,
            VMEM((ghost_count, BLK), I32),
            VMEM((ghost_count * SENT, BLK), F32),
            each,
            each,
            VMEM((3, ghost_count, BLK), F32),
            VMEM((3, ghost_count, BLK), F32),
            square,
            square,
            VMEM((TOTACT, 6, BLK, BLK), F32),
            VMEM((TOTACT, BLK, BLK), F32),
            VMEM((TOTACT, 1 + near_count + far_count, BLK, BLK), F32),
            square,
            VMEM((blocks, BLK), F32),
            VMEM((3, ADDED, BLK), F32),
            VMEM((3, ADDED, BLK), F32),
            VMEM((3, TOTACT, BLK, BLK), F32),
            pltpu.SemaphoreType.DMA((LEVELS,)),
            pltpu.SemaphoreType.DMA((LEVELS,)),
            pltpu.SemaphoreType.DMA((6,)),
            pltpu.SemaphoreType.DMA((6,)),
        ],
        compiler_params=pltpu.CompilerParams(collective_id=0, has_side_effects=True, vmem_limit_bytes=limit),
    )(
        mig_count, active_ids, active_count,
        local_nbrs.transpose(0, 3, 1, 2), ghost_slots.transpose(0, 1, 3, 2), export_blocks.transpose(0, 2, 1),
        mig_rows, particles,
    )
    density, accel = pl.pallas_call(
        deliver_kernel,
        name="deliver",
        out_shape=(struct((blocks, BLK), F32), struct((3, count), F32)),
        in_specs=[spec(VMEM)] * 2,
        out_specs=(spec(VMEM),) * 2,
        compiler_params=pltpu.CompilerParams(vmem_limit_bytes=limit),
    )(dens, force)
    return density.reshape(-1), accel


def solution(mesh):
    placed = (
        P(None, ("gx", "gy")),
        P(("gx", "gy"), None),
        P(("gx", "gy"), None, None),
        P(("gx", "gy"), None, None),
        P(("gx", "gy"), None),
        P(("gx", "gy"), None, None, None),
        P(("gx", "gy"), None, None, None),
        P(("gx", "gy"), None, None),
    )
    return jax.shard_map(
        shards,
        mesh=mesh,
        in_specs=placed,
        out_specs=(P(("gx", "gy")), P(None, ("gx", "gy"))),
        check_vma=False,
    )
```

```python
import functools
import math

import jax
import jax.numpy as jnp
from jax import lax
from jax.experimental import pallas as pl
from jax.experimental.pallas import tpu as pltpu
from jax.sharding import PartitionSpec as P

BLK = 128
TOTACT = 12
LEVELS = 4
CHAN = 8
SENT = 4
SLOT_BITS = 3
ADDED = 64
WHICH_MAP = (0, 1, 1, 2)

KERNEL_NORM = 21.0 / (16.0 * math.pi)
GAMMA_LESS = 2.0 / 3.0
FORCE_NORM = GAMMA_LESS * 32.0 * 5.0 * KERNEL_NORM
TINY = 1e-37
PART = 32
MESH = pl.DeviceIdType.MESH
VMEM = pltpu.VMEM
SMEM = pltpu.SMEM
F32 = jnp.float32
I32 = jnp.int32


def lanes(shape):
    return lax.broadcasted_iota(I32, shape, len(shape) - 1)


def spec(space):
    return pl.BlockSpec(memory_space=space)


def flipped(index, bit):
    return index + bit - 2 * bit * (lax.div(index, bit) % 2)


def picked(chunk, lane_number):
    return jnp.take_along_axis(
        chunk, jnp.full(chunk.shape, lane_number, I32), axis=1, mode="promise_in_bounds"
    )


def gather(tiles, rows):
    parts = []
    for part in range(rows.shape[1] // BLK):
        here = rows[:, part * BLK : (part + 1) * BLK]
        block = jnp.broadcast_to(here >> 7, (CHAN, BLK))
        spot = jnp.broadcast_to(here & 127, (CHAN, BLK))

        def step(n, held):
            held = list(held)
            for k in range(64):
                b = n * 64 + k
                tile = tiles[b]
                turned = jnp.take_along_axis(tile, spot, axis=1, mode="promise_in_bounds")
                held[k % 4] = jnp.where(block == b, turned, held[k % 4])
            return tuple(held)

        zero = jnp.zeros((CHAN, BLK), F32)
        held = lax.fori_loop(0, tiles.shape[0] // 64, step, (zero,) * 4)
        parts.append((held[0] + held[1]) + (held[2] + held[3]))
    return jnp.concatenate(parts, axis=1)


def pieces(value):
    first = value.astype(jnp.bfloat16).astype(F32)
    rest = value - first
    second = rest.astype(jnp.bfloat16).astype(F32)
    return first, second, rest - second


def abreast(ref):
    return jnp.concatenate([ref[0], ref[1], ref[2]], axis=1)


def row_sums(value):
    return jnp.sum(jnp.transpose(value), axis=0, keepdims=True)


def placed_sum(ids, terms, count):
    depth = terms.shape[0]
    owner = lax.broadcasted_iota(I32, (count, depth), 0)
    chosen = jnp.where(owner == ids[:, 0:depth], 1.0, 0.0)
    chosen = jnp.concatenate([chosen] * 3, axis=1).astype(jnp.bfloat16)
    split = jnp.concatenate(pieces(terms), axis=0).astype(jnp.bfloat16)
    return jnp.dot(chosen, split, preferred_element_type=F32)


def substep_kernel(
    *refs,
):
    given, (dens_out, force_out), refs = refs[0:8], refs[8:10], refs[10:]
    (
    count_ref, ids_ref, live_ref, near_ref, far_ref, exp_ref, rows_ref, x_ref, in_sem,
    tiles, leaving, landed, match, map_lane, map_part, table, act, near, far,
    stage, stage_h, stage_p, energies, expcol, ghosts, ghost_h, ghost_p, back_stage, back_land,
    centres, cols, wide, sums, weights, rhos, pj, adds, fars, forces,
    mig_ssem, mig_rsem, ssem, rsem,
    ) = refs
    held = (count_ref, ids_ref, live_ref, near_ref, far_ref, exp_ref, rows_ref, x_ref)
    fetches = [pltpu.make_async_copy(a, b, in_sem.at[n]) for n, (a, b) in enumerate(zip(given, held))]
    for fetch in reversed(fetches):
        fetch.start()
    gx, me = lax.axis_index("gx"), lax.axis_index("gy")
    peers = lax.axis_size("gy")
    slots = exp_ref.shape[1]
    width = rows_ref.shape[2]
    parts = width // BLK
    blocks = x_ref.shape[1] // BLK
    near_count, far_count = near_ref.shape[1], far_ref.shape[2]
    partners = [(flipped(gx, 2), me), (flipped(gx, 1), me), (gx, flipped(me, 2)), (gx, flipped(me, 1))]
    low, high = lax.rem(me, 4), lax.div(me, 4)
    across = flipped(low, 2)
    column = (across, flipped(across, 1), flipped(low, 1), low)
    order = [lax.rem(high + apart, peers // 4) * 4 + z for z in column for apart in (2, 1, 3, 0)][: peers - 1]
    around = [(gx, peer) for peer in order]

    barrier = pltpu.get_barrier_semaphore()
    for other in partners[0:2] + around:
        pl.semaphore_signal(barrier, inc=1, device_id=other, device_id_type=MESH)

    for fetch in reversed(fetches):
        fetch.wait()

    def load(b8, _):
        for k in range(8):
            b = b8 * 8 + k
            tiles[b, 0:7, :] = x_ref[:, pl.ds(pl.multiple_of(b * BLK, BLK), BLK)]
            tiles[b, 7:8, :] = jnp.zeros((1, BLK), F32)
        return 0

    lax.fori_loop(0, blocks // 8, load, 0)
    rows = [rows_ref[0, level : level + 1, :] for level in range(LEVELS)]
    leaving[0] = gather(tiles, rows[0])

    def copy(level):
        return pltpu.make_async_remote_copy(
            src_ref=leaving.at[level],
            dst_ref=landed.at[level],
            send_sem=mig_ssem.at[level],
            recv_sem=mig_rsem.at[level],
            device_id=partners[level],
            device_id_type=MESH,
        )

    pair = {}
    for early in range(LEVELS - 1):
        for late in range(early + 1, LEVELS):
            pair[late, early] = len(pair)

    def relate(early):
        keys = jnp.where(lanes((1, width)) < count_ref[0, early], rows[early], -1)
        lane = lanes((BLK, BLK))
        slot = lax.broadcasted_iota(I32, (BLK, BLK), 0)
        owner = lax.broadcasted_iota(I32, (blocks, width), 0)
        spots = []
        for part in range(parts):
            down = jnp.transpose(jnp.broadcast_to(keys[:, part * BLK : (part + 1) * BLK], (BLK, BLK)))
            hit = (down & 127) == lane
            spots.append(
                jnp.concatenate(
                    [jnp.where(hit, (slot + 1).astype(F32), 0.0), jnp.where(hit, float(part), 0.0)], axis=1
                ).astype(jnp.bfloat16)
            )
            down = jnp.concatenate([down] * parts, axis=1)
            for late in range(early + 1, LEVELS):
                match[pair[late, early], part * BLK : (part + 1) * BLK, :] = jnp.where(
                    down == rows[late], 1.0, 0.0
                ).astype(jnp.bfloat16)
        held = jnp.where(owner == (keys >> 7), 1.0, 0.0).astype(jnp.bfloat16)
        found = jnp.dot(held, jnp.concatenate(spots, axis=0), preferred_element_type=F32).astype(I32)
        arriving = found[:, 0:BLK] > 0
        spot = found[:, 0:BLK] - 1
        part = found[:, BLK:] + early * parts
        which = WHICH_MAP[early]
        if early == 2:
            spot = jnp.where(arriving, spot, map_lane[which])
            part = jnp.where(arriving, part, map_part[which])
        else:
            spot = jnp.where(arriving, spot, 0)
            part = jnp.where(arriving, part, -1)
        map_lane[which] = spot
        map_part[which] = part

    def settle(which_map, levels):
        numbers = [level * parts + part for level in levels for part in range(parts)]
        arrived = {n: landed[n // parts, :, n % parts * BLK : (n % parts + 1) * BLK] for n in numbers}

        def step(b8, _):
            for k in range(8):
                b = b8 * 8 + k
                spot = jnp.broadcast_to(map_lane[which_map, pl.ds(b, 1), :], (CHAN, BLK))
                which = jnp.broadcast_to(map_part[which_map, pl.ds(b, 1), :], (CHAN, BLK))
                tile = tiles[b]
                for n in numbers:
                    turned = jnp.take_along_axis(arrived[n], spot, axis=1, mode="promise_in_bounds")
                    tile = jnp.where(which == n, turned, tile)
                tiles[b] = tile
            return 0

        lax.fori_loop(0, blocks // 8, step, 0)

    wide_lane = lanes((1, BLK))

    def compact():
        in_first = live_ref[0, 0]
        in_all = in_first + live_ref[0, 1]
        centre = jnp.full((1, BLK), -1, I32)
        distant = jnp.full((1, BLK), -1, I32)
        for p in range(TOTACT):
            n = jnp.where(p < in_first, 0, 1)
            i = jnp.minimum(jnp.where(p < in_first, p, p - in_first), ids_ref.shape[2] - 1)
            alive = p < in_all
            block = ids_ref[0, n, i]
            act[2 * p] = block
            act[2 * p + 1] = jnp.where(alive, block, -1)
            centre = jnp.where(wide_lane == p, jnp.where(alive, block, -1), centre)
            for k in range(near_count):
                other = near_ref[0, k, n, i]
                near[p * near_count + k] = other
                centre = jnp.where(
                    wide_lane == TOTACT + p * near_count + k, jnp.where(alive, other, -1), centre
                )
            for k in range(far_count):
                other = far_ref[0, n, k, i]
                far[p * far_count + k] = other
                distant = jnp.where(wide_lane == p * far_count + k, jnp.where(alive, other, -1), distant)
        table[0:1, :] = centre
        table[1:2, :] = distant
        table[3:8, :] = jnp.full((5, BLK), -1, I32)

    relate(0)
    pl.semaphore_wait(barrier, peers + 1)
    first = copy(0)
    first.start()
    kept = {1: gather(tiles, rows[1])}
    relate(1)
    relate(2)
    first.wait()
    factors = []
    for level in range(1, LEVELS):
        factors.append(
            jnp.concatenate([*pieces(landed[level - 1]), jnp.ones((8, width), F32)], axis=0).astype(jnp.bfloat16)
        )
        out = kept[level]
        for early in range(level):
            found = jnp.dot(factors[early], match[pair[level, early]], preferred_element_type=F32)
            value = (found[0:8] + found[8:16]) + found[16:24]
            out = jnp.where(found[24:32] > 0.5, value, out)
        leaving[level] = out
        moving = copy(level)
        moving.start()
        if level + 1 < LEVELS:
            kept[level + 1] = gather(tiles, rows[level + 1])
        if level == 2:
            relate(3)
        if level > 1:
            settle(level - 2, [[0], [1, 2]][level - 2])
        moving.wait()

    def send(phase, source, target, count, peer):
        pltpu.make_async_remote_copy(
            src_ref=source.at[pl.ds(peer * count, count), :],
            dst_ref=target.at[pl.ds(me * count, count), :],
            send_sem=ssem.at[phase],
            recv_sem=rsem.at[phase],
            device_id=(gx, peer),
            device_id_type=MESH,
        ).start()

    def exchange(phase, source, target, count):
        for peer in order:
            send(phase, source, target, count, peer)
        return phase

    def finish(phase, source, target, count):
        here = pl.ds(me * count, count)
        target[here, :] = source[here, :]
        whole = pl.ds(0, (peers - 1) * count)
        pltpu.make_async_remote_copy(
            src_ref=source.at[whole, :],
            dst_ref=target.at[whole, :],
            send_sem=ssem.at[phase],
            recv_sem=rsem.at[phase],
            device_id=(gx, order[0]),
            device_id_type=MESH,
        ).wait()

    last = LEVELS - 1
    arrived = [landed[last, :, part * BLK : (part + 1) * BLK] for part in range(parts)]
    for peer in order + [me]:
        for t in range(slots):
            block = exp_ref[0, t, peer]
            spot = jnp.broadcast_to(map_lane[2, pl.ds(block, 1), :], (CHAN, BLK))
            which = jnp.broadcast_to(map_part[2, pl.ds(block, 1), :], (CHAN, BLK))
            tile = tiles[block]
            for part in range(parts):
                turned = jnp.take_along_axis(arrived[part], spot, axis=1, mode="promise_in_bounds")
                tile = jnp.where(which == last * parts + part, turned, tile)
            stage[pl.ds(peer * (SENT * slots) + t, SENT, stride=slots), :] = tile[0:SENT]
        if peer is not me:
            send(0, stage, ghosts, SENT * slots, peer)
    sent_blocks = 0
    settle(2, [last])
    compact()

    def pack_rest(p, ids):
        for t in range(slots):
            block = exp_ref[0, t, p]
            tile = tiles[block]
            row = pl.ds(p * slots + t, 1)
            stage_h[row, :] = tile[4:5]
            energies[row, :] = tile[5:6]
            stage_p[row, :] = tile[6:7]
            expcol[row, :] = jnp.full((1, BLK), block, I32)
            ids = jnp.where(wide_lane == p * slots + t, block, ids)
        return ids

    table[2:3, :] = lax.fori_loop(0, peers, pack_rest, jnp.full((1, BLK), -1, I32))
    centres[...] = jnp.zeros_like(centres)
    for p in range(TOTACT):
        tile = tiles[act[2 * p]]
        centres[p * CHAN : p * CHAN + 7, :] = tile[0:7]
        centres[p * CHAN + 7 : p * CHAN + 8, :] = 0.5 / tile[4:5]
    cols[...] = jnp.transpose(centres[...])

    def sliced(q):
        return slice(q * PART, (q + 1) * PART)

    def local_row(block, channel):
        return tiles[block, channel : channel + 1, :]

    def ghost_base(ghost):
        return (ghost >> SLOT_BITS) * (SENT * slots) + (ghost & (slots - 1))

    def ghost_row(base, channel):
        return ghosts[pl.ds(base + channel * slots, 1), :]

    def separation(mine, theirs):
        dx, dy, dz = (a - b for a, b in zip(mine, theirs))
        square = dx * dx + dy * dy + dz * dz
        return square * lax.rsqrt(jnp.maximum(square, TINY))

    def density_term(r, inverse, mass5, mass4):
        fall = jnp.maximum(1.0 - r * inverse, 0.0)
        fall2 = fall * fall
        return (fall2 * fall2) * (mass5 - mass4 * fall)

    def pair_weight(r, smooth, mass, other_smooth, other_mass):
        inverse = 1.0 / (smooth + other_smooth)
        fall = jnp.maximum(1.0 - r * inverse, 0.0) * inverse
        return ((fall * fall) * fall * (inverse * inverse)) * (mass * other_mass)

    def local_first(p, _):
        others = [act[2 * p]] + [near[p * near_count + k] for k in range(near_count)]
        rows = [[local_row(b, c) for c in range(4)] for b in others]
        masses = [(5.0 * row[3], 4.0 * row[3]) for row in rows]
        for q in range(BLK // PART):
            here = sliced(q)
            chunk = cols[here, :]
            mine = [picked(chunk, p * CHAN + c) for c in (0, 1, 2, 3, 4, 7)]
            for c in range(6):
                wide[p, c, here, :] = mine[c]
            total = None
            for n, row in enumerate(rows):
                r = separation(mine[0:3], row[0:3])
                term = density_term(r, mine[5], *masses[n])
                total = term if total is None else total + term
                weights[p, n, here, :] = r
            sums[p, here, :] = total
        return 0

    lax.fori_loop(0, TOTACT, local_first, 0)
    finish(sent_blocks, stage, ghosts, SENT * slots)
    sent_h = exchange(1, stage_h, ghost_h, slots)

    def density_of(p):
        smooth = centres[pl.ds(p * CHAN + 4, 1), :]
        rhos[pl.ds(p, 1), :] = KERNEL_NORM / (smooth * smooth * smooth) * row_sums(sums[p])

    def ghost_first(p, _):
        others = [ghost_base(far[p * far_count + k]) for k in range(far_count)]
        rows = [[ghost_row(g, c) for c in range(4)] for g in others]
        masses = [(5.0 * row[3], 4.0 * row[3]) for row in rows]
        density_of(jnp.maximum(p - 1, 0))
        for q in range(BLK // PART):
            here = sliced(q)
            mine = [wide[p, c, here, :] for c in (0, 1, 2)]
            inverse = wide[p, 5, here, :]
            total = sums[p, here, :]
            for n, row in enumerate(rows):
                r = separation(mine, row[0:3])
                weights[p, 1 + near_count + n, here, :] = r
                total = total + density_term(r, inverse, *masses[n])
            sums[p, here, :] = total
        return 0

    lax.fori_loop(0, TOTACT, ghost_first, 0)
    density_of(TOTACT - 1)
    fresh = [rhos[p : p + 1, :] for p in range(TOTACT)]
    exported = stage_p[...]
    export_block = expcol[...]
    for p in range(TOTACT):
        exported = jnp.where(export_block == act[2 * p + 1], fresh[p], exported)
    stage_p[...] = FORCE_NORM * (energies[...] / exported)
    sent_p = exchange(2, stage_p, ghost_p, slots)

    block_number = lax.broadcasted_iota(I32, (blocks, BLK), 0)
    dens = tiles[:, 6, :]
    for p in range(TOTACT):
        dens = jnp.where(block_number == act[2 * p + 1], fresh[p], dens)
    dens_out[...] = dens
    pj[...] = FORCE_NORM * (tiles[:, 5, :] / dens)
    rhos[...] = jnp.zeros_like(rhos)
    for p in range(TOTACT):
        rhos[p : p + 1, :] = FORCE_NORM * (centres[p * CHAN + 5 : p * CHAN + 6, :] / fresh[p])
    cols[...] = jnp.transpose(rhos[...])
    adds[...] = jnp.zeros_like(adds)
    fars[...] = jnp.zeros_like(fars)

    def second(p, first, rows):
        for q in range(BLK // PART):
            here = sliced(q)
            mass, smooth = wide[p, 3, here, :], wide[p, 4, here, :]
            for n, row in enumerate(rows):
                r = weights[p, first + n, here, :]
                weights[p, first + n, here, :] = pair_weight(r, smooth, mass, row[1], row[0])

    def local_second(p, _):
        others = [act[2 * p]] + [near[p * near_count + k] for k in range(near_count)]
        second(p, 0, [[local_row(b, c) for c in (3, 4)] for b in others])
        for q in range(BLK // PART):
            here = sliced(q)
            wide[p, 5, here, :] = picked(cols[here, :], p)
        return 0

    def ghost_second(p, _):
        others = [far[p * far_count + k] for k in range(far_count)]
        second(p, 1 + near_count, [[ghost_row(ghost_base(g), 3), ghost_h[pl.ds(g, 1), :]] for g in others])
        return 0

    lax.fori_loop(0, TOTACT, local_second, 0)
    finish(sent_h, stage_h, ghost_h, slots)
    lax.fori_loop(0, TOTACT, ghost_second, 0)

    def force_phase(p, first, rows, skip, again):
        kept = len(rows) - skip
        carry = [None] * (3 * kept)
        for q in range(BLK // PART):
            here = sliced(q)
            mine = [wide[p, c, here, :] for c in (0, 1, 2)]
            pressure = wide[p, 5, here, :]
            total = [forces[c, p, here, :] for c in range(3)] if again else [None] * 3
            for n, row in enumerate(rows):
                weight = weights[p, first + n, here, :] * (pressure + row[3])
                for c in range(3):
                    push = weight * (mine[c] - row[c])
                    total[c] = push if total[c] is None else total[c] + push
                    if n >= skip:
                        at = (n - skip) * 3 + c
                        down = [push[8 * i : 8 * i + 8] for i in range(PART // 8)]
                        if carry[at] is not None:
                            down.append(carry[at])
                        while len(down) > 1:
                            down = down[2:] + [down[0] + down[1]]
                        carry[at] = down[0]
            for c in range(3):
                forces[c, p, here, :] = total[c]
        return [[-jnp.sum(carry[n * 3 + c], axis=0, keepdims=True) for c in range(3)] for n in range(kept)]

    finish(sent_p, stage_p, ghost_p, slots)

    def ghost_force(c):
        def body(p, _):
            others = [far[p * far_count + k] for k in range(far_count)]
            rows = [(ghost_row(ghost_base(g), c), ghost_p[pl.ds(g, 1), :] if c == 0 else None) for g in others]
            carry = [None] * far_count
            for q in range(BLK // PART):
                here = sliced(q)
                mine = wide[p, c, here, :]
                total = None
                for n, (row, pressure) in enumerate(rows):
                    weight = weights[p, 1 + near_count + n, here, :]
                    if c == 0:
                        weight = weight * (wide[p, 5, here, :] + pressure)
                        weights[p, 1 + near_count + n, here, :] = weight
                    push = weight * (mine - row)
                    total = push if total is None else total + push
                    down = [push[8 * i : 8 * i + 8] for i in range(PART // 8)]
                    if carry[n] is not None:
                        down.append(carry[n])
                    while len(down) > 1:
                        down = down[2:] + [down[0] + down[1]]
                    carry[n] = down[0]
                forces[c, p, here, :] = total
            for n in range(far_count):
                fars[c, pl.ds(p * far_count + n, 1), :] = -jnp.sum(carry[n], axis=0, keepdims=True)
            return 0

        lax.fori_loop(0, TOTACT, body, 0)

    for c in range(3):
        ghost_force(c)
        back_stage[c] = placed_sum(table[1:2, :], fars[c], peers * slots)
        exchange(3 + c, back_stage.at[c], back_land.at[c], slots)

    def centre_force(p):
        for c in range(3):
            adds[c, pl.ds(p, 1), :] = row_sums(forces[c, p])

    def local_force(p, _):
        others = [act[2 * p]] + [near[p * near_count + k] for k in range(near_count)]
        rows = [[local_row(b, c) for c in range(3)] + [pj[pl.ds(b, 1), :]] for b in others]
        centre_force(jnp.maximum(p - 1, 0))
        found = force_phase(p, 0, rows, 1, True)
        for n in range(near_count):
            for c in range(3):
                adds[c, pl.ds(TOTACT + p * near_count + n, 1), :] = found[n][c]
        return 0

    lax.fori_loop(0, TOTACT, local_force, 0)
    centre_force(TOTACT - 1)
    totals = placed_sum(table[0:1, :], abreast(adds), blocks)
    for c in range(3):
        finish(3 + c, back_stage.at[c], back_land.at[c], slots)
    totals = totals + placed_sum(table[2:3, :], abreast(back_land), blocks)
    mass = tiles[:, 3, :]
    for c in range(3):
        force_out[c] = totals[:, c * BLK : (c + 1) * BLK] / mass


def deliver_kernel(dens_ref, force_ref, dens_out, accel_out):
    dens_out[...] = dens_ref[...]

    def put(b8, _):
        for k in range(8):
            b = b8 * 8 + k
            for c in range(3):
                accel_out[c : c + 1, pl.ds(pl.multiple_of(b * BLK, BLK), BLK)] = force_ref[c, pl.ds(b, 1), :]
        return 0

    lax.fori_loop(0, dens_ref.shape[0] // 8, put, 0)


def shards(
    particles, mig_count, mig_rows, active_ids, active_count, local_nbrs, ghost_slots, export_blocks
):
    count = particles.shape[1]
    blocks = count // BLK
    width = mig_rows.shape[2]
    peers, slots = export_blocks.shape[1:]
    near_count, far_count = local_nbrs.shape[3], ghost_slots.shape[3]
    limit = 30 * 1024 * 1024
    struct = jax.ShapeDtypeStruct
    ghost_count = peers * slots
    square = VMEM((BLK, BLK), F32)
    each = VMEM((ghost_count, BLK), F32)
    tables = (
        mig_count, active_ids, active_count,
        local_nbrs.transpose(0, 3, 1, 2), ghost_slots.transpose(0, 1, 3, 2), export_blocks.transpose(0, 2, 1),
    )
    dens, force = pl.pallas_call(
        substep_kernel,
        name="substep",
        out_shape=(struct((blocks, BLK), F32), struct((3, blocks, BLK), F32)),
        in_specs=[spec(pltpu.HBM)] * 8,
        out_specs=(spec(VMEM),) * 2,
        scratch_shapes=[
            *(SMEM(given.shape, I32) for given in tables),
            VMEM(mig_rows.shape, I32),
            VMEM(particles.shape, F32),
            pltpu.SemaphoreType.DMA((8,)),
            VMEM((blocks, CHAN, BLK), F32),
            VMEM((LEVELS, CHAN, width), F32),
            VMEM((LEVELS, CHAN, width), F32),
            VMEM((6, width, width), jnp.bfloat16),
            VMEM((3, blocks, BLK), I32),
            VMEM((3, blocks, BLK), I32),
            VMEM((8, BLK), I32),
            SMEM((2 * TOTACT,), I32),
            SMEM((TOTACT * near_count,), I32),
            SMEM((TOTACT * far_count,), I32),
            VMEM((ghost_count * SENT, BLK), F32),
            each,
            each,
            each,
            VMEM((ghost_count, BLK), I32),
            VMEM((ghost_count * SENT, BLK), F32),
            each,
            each,
            VMEM((3, ghost_count, BLK), F32),
            VMEM((3, ghost_count, BLK), F32),
            square,
            square,
            VMEM((TOTACT, 6, BLK, BLK), F32),
            VMEM((TOTACT, BLK, BLK), F32),
            VMEM((TOTACT, 1 + near_count + far_count, BLK, BLK), F32),
            square,
            VMEM((blocks, BLK), F32),
            VMEM((3, ADDED, BLK), F32),
            VMEM((3, ADDED, BLK), F32),
            VMEM((3, TOTACT, BLK, BLK), F32),
            pltpu.SemaphoreType.DMA((LEVELS,)),
            pltpu.SemaphoreType.DMA((LEVELS,)),
            pltpu.SemaphoreType.DMA((6,)),
            pltpu.SemaphoreType.DMA((6,)),
        ],
        compiler_params=pltpu.CompilerParams(collective_id=0, has_side_effects=True, vmem_limit_bytes=limit),
    )(*(pltpu.with_memory_space_constraint(a, pltpu.HBM) for a in (*tables, mig_rows, particles)))
    density, accel = pl.pallas_call(
        deliver_kernel,
        name="deliver",
        out_shape=(struct((blocks, BLK), F32), struct((3, count), F32)),
        in_specs=[spec(VMEM)] * 2,
        out_specs=(spec(VMEM),) * 2,
        compiler_params=pltpu.CompilerParams(vmem_limit_bytes=limit),
    )(dens, force)
    return density.reshape(-1), accel


def solution(mesh):
    placed = (
        P(None, ("gx", "gy")),
        P(("gx", "gy"), None),
        P(("gx", "gy"), None, None),
        P(("gx", "gy"), None, None),
        P(("gx", "gy"), None),
        P(("gx", "gy"), None, None, None),
        P(("gx", "gy"), None, None, None),
        P(("gx", "gy"), None, None),
    )
    return jax.shard_map(
        shards,
        mesh=mesh,
        in_specs=placed,
        out_specs=(P(("gx", "gy")), P(None, ("gx", "gy"))),
        check_vma=False,
    )
```

```python
import functools
import math

import jax
import jax.numpy as jnp
from jax import lax
from jax.experimental import pallas as pl
from jax.experimental.pallas import tpu as pltpu
from jax.sharding import PartitionSpec as P

BLK = 128
TOTACT = 12
LEVELS = 4
CHAN = 8
SENT = 4
SLOT_BITS = 3
ADDED = 64
WHICH_MAP = (0, 0, 0, 1)

KERNEL_NORM = 21.0 / (16.0 * math.pi)
GAMMA_LESS = 2.0 / 3.0
FORCE_NORM = GAMMA_LESS * 32.0 * 5.0 * KERNEL_NORM
TINY = 1e-37
PART = 32
MESH = pl.DeviceIdType.MESH
VMEM = pltpu.VMEM
SMEM = pltpu.SMEM
F32 = jnp.float32
I32 = jnp.int32


def lanes(shape):
    return lax.broadcasted_iota(I32, shape, len(shape) - 1)


def spec(space):
    return pl.BlockSpec(memory_space=space)


def flipped(index, bit):
    return index + bit - 2 * bit * (lax.div(index, bit) % 2)


def picked(chunk, lane_number):
    return jnp.take_along_axis(
        chunk, jnp.full(chunk.shape, lane_number, I32), axis=1, mode="promise_in_bounds"
    )


def gather(tiles, rows):
    parts = []
    for part in range(rows.shape[1] // BLK):
        here = rows[:, part * BLK : (part + 1) * BLK]
        block = jnp.broadcast_to(here >> 7, (CHAN, BLK))
        spot = jnp.broadcast_to(here & 127, (CHAN, BLK))

        def step(n, held):
            held = list(held)
            for k in range(64):
                b = n * 64 + k
                tile = tiles[b]
                turned = jnp.take_along_axis(tile, spot, axis=1, mode="promise_in_bounds")
                held[k % 4] = jnp.where(block == b, turned, held[k % 4])
            return tuple(held)

        zero = jnp.zeros((CHAN, BLK), F32)
        held = lax.fori_loop(0, tiles.shape[0] // 64, step, (zero,) * 4)
        parts.append((held[0] + held[1]) + (held[2] + held[3]))
    return jnp.concatenate(parts, axis=1)


def pieces(value):
    first = value.astype(jnp.bfloat16).astype(F32)
    rest = value - first
    second = rest.astype(jnp.bfloat16).astype(F32)
    return first, second, rest - second


def abreast(ref):
    return jnp.concatenate([ref[0], ref[1], ref[2]], axis=1)


def row_sums(value):
    return jnp.sum(jnp.transpose(value), axis=0, keepdims=True)


def one_hot(ids, depth, count):
    owner = lax.broadcasted_iota(I32, (count, depth), 0)
    chosen = jnp.where(owner == ids[:, 0:depth], 1.0, 0.0)
    return jnp.concatenate([chosen] * 3, axis=1).astype(jnp.bfloat16)


def placed_sum(chosen, terms):
    split = jnp.concatenate(pieces(terms), axis=0).astype(jnp.bfloat16)
    return jnp.dot(chosen, split, preferred_element_type=F32)


def substep_kernel(
    *refs,
):
    given, (dens_out, force_out), refs = refs[0:8], refs[8:10], refs[10:]
    (
    count_ref, ids_ref, live_ref, near_ref, far_ref, exp_ref, rows_ref, x_ref, in_sem,
    tiles, leaving, landed, match, map_lane, map_part, table, act, near, far,
    stage, stage_h, stage_p, energies, expcol, ghosts, ghost_h, ghost_p, back_stage, back_land,
    centres, cols, wide, sums, weights, rhos, pj, adds, fars, forces,
    mig_ssem, mig_rsem, ssem, rsem,
    ) = refs
    held = (count_ref, ids_ref, live_ref, near_ref, far_ref, exp_ref, rows_ref, x_ref)
    fetches = [pltpu.make_async_copy(a, b, in_sem.at[n]) for n, (a, b) in enumerate(zip(given, held))]
    for fetch in reversed(fetches):
        fetch.start()
    gx, me = lax.axis_index("gx"), lax.axis_index("gy")
    peers = lax.axis_size("gy")
    slots = exp_ref.shape[1]
    width = rows_ref.shape[2]
    parts = width // BLK
    blocks = x_ref.shape[1] // BLK
    near_count, far_count = near_ref.shape[1], far_ref.shape[2]
    partners = [(flipped(gx, 2), me), (flipped(gx, 1), me), (gx, flipped(me, 2)), (gx, flipped(me, 1))]
    low, high = lax.rem(me, 4), lax.div(me, 4)
    across = flipped(low, 2)
    column = (across, flipped(across, 1), flipped(low, 1), low)
    order = [lax.rem(high + apart, peers // 4) * 4 + z for z in column for apart in (2, 1, 3, 0)][: peers - 1]
    around = [(gx, peer) for peer in order]

    barrier = pltpu.get_barrier_semaphore()
    for other in partners[0:2] + around:
        pl.semaphore_signal(barrier, inc=1, device_id=other, device_id_type=MESH)

    for fetch in reversed(fetches):
        fetch.wait()

    def load(b8, _):
        for k in range(8):
            b = b8 * 8 + k
            tiles[b, 0:7, :] = x_ref[:, pl.ds(pl.multiple_of(b * BLK, BLK), BLK)]
            tiles[b, 7:8, :] = jnp.zeros((1, BLK), F32)
        return 0

    lax.fori_loop(0, blocks // 8, load, 0)
    rows = [rows_ref[0, level : level + 1, :] for level in range(LEVELS)]
    leaving[0] = gather(tiles, rows[0])

    def copy(level):
        return pltpu.make_async_remote_copy(
            src_ref=leaving.at[level],
            dst_ref=landed.at[level],
            send_sem=mig_ssem.at[level],
            recv_sem=mig_rsem.at[level],
            device_id=partners[level],
            device_id_type=MESH,
        )

    pair = {}
    for early in range(LEVELS - 1):
        for late in range(early + 1, LEVELS):
            pair[late, early] = len(pair)

    def relate(early):
        keys = jnp.where(lanes((1, width)) < count_ref[0, early], rows[early], -1)
        lane = lanes((BLK, BLK))
        slot = lax.broadcasted_iota(I32, (BLK, BLK), 0)
        owner = lax.broadcasted_iota(I32, (blocks, width), 0)
        spots = []
        for part in range(parts):
            down = jnp.transpose(jnp.broadcast_to(keys[:, part * BLK : (part + 1) * BLK], (BLK, BLK)))
            hit = (down & 127) == lane
            spots.append(
                jnp.concatenate(
                    [jnp.where(hit, (slot + 1).astype(F32), 0.0), jnp.where(hit, float(part), 0.0)], axis=1
                ).astype(jnp.bfloat16)
            )
            down = jnp.concatenate([down] * parts, axis=1)
            for late in range(early + 1, LEVELS):
                match[pair[late, early], part * BLK : (part + 1) * BLK, :] = jnp.where(
                    down == rows[late], 1.0, 0.0
                ).astype(jnp.bfloat16)
        held = jnp.where(owner == (keys >> 7), 1.0, 0.0).astype(jnp.bfloat16)
        found = jnp.dot(held, jnp.concatenate(spots, axis=0), preferred_element_type=F32).astype(I32)
        arriving = found[:, 0:BLK] > 0
        spot = found[:, 0:BLK] - 1
        part = found[:, BLK:] + early * parts
        which = WHICH_MAP[early]
        if early in (1, 2):
            spot = jnp.where(arriving, spot, map_lane[which])
            part = jnp.where(arriving, part, map_part[which])
        else:
            spot = jnp.where(arriving, spot, 0)
            part = jnp.where(arriving, part, -1)
        map_lane[which] = spot
        map_part[which] = part

    def settle(which_map, levels):
        numbers = [level * parts + part for level in levels for part in range(parts)]
        arrived = {n: landed[n // parts, :, n % parts * BLK : (n % parts + 1) * BLK] for n in numbers}

        def step(b8, _):
            for k in range(8):
                b = b8 * 8 + k
                spot = jnp.broadcast_to(map_lane[which_map, pl.ds(b, 1), :], (CHAN, BLK))
                which = jnp.broadcast_to(map_part[which_map, pl.ds(b, 1), :], (CHAN, BLK))
                tile = tiles[b]
                for n in numbers:
                    turned = jnp.take_along_axis(arrived[n], spot, axis=1, mode="promise_in_bounds")
                    tile = jnp.where(which == n, turned, tile)
                tiles[b] = tile
            return 0

        lax.fori_loop(0, blocks // 8, step, 0)

    wide_lane = lanes((1, BLK))

    def compact():
        in_first = live_ref[0, 0]
        in_all = in_first + live_ref[0, 1]
        centre = jnp.full((1, BLK), -1, I32)
        distant = jnp.full((1, BLK), -1, I32)
        for p in range(TOTACT):
            n = jnp.where(p < in_first, 0, 1)
            i = jnp.minimum(jnp.where(p < in_first, p, p - in_first), ids_ref.shape[2] - 1)
            alive = p < in_all
            block = ids_ref[0, n, i]
            act[2 * p] = block
            act[2 * p + 1] = jnp.where(alive, block, -1)
            centre = jnp.where(wide_lane == p, jnp.where(alive, block, -1), centre)
            for k in range(near_count):
                other = near_ref[0, k, n, i]
                near[p * near_count + k] = other
                centre = jnp.where(
                    wide_lane == TOTACT + p * near_count + k, jnp.where(alive, other, -1), centre
                )
            for k in range(far_count):
                other = far_ref[0, n, k, i]
                far[p * far_count + k] = other
                distant = jnp.where(wide_lane == p * far_count + k, jnp.where(alive, other, -1), distant)
        table[0:1, :] = centre
        table[1:2, :] = distant
        table[3:8, :] = jnp.full((5, BLK), -1, I32)

    relate(0)
    pl.semaphore_wait(barrier, peers + 1)
    first = copy(0)
    first.start()
    kept = {1: gather(tiles, rows[1])}
    relate(1)
    first.wait()
    factors = []

    def corrected(out, level, early):
        found = jnp.dot(factors[early], match[pair[level, early]], preferred_element_type=F32)
        value = (found[0:8] + found[8:16]) + found[16:24]
        return jnp.where(found[24:32] > 0.5, value, out)

    for level in range(1, LEVELS):
        factors.append(
            jnp.concatenate([*pieces(landed[level - 1]), jnp.ones((8, width), F32)], axis=0).astype(jnp.bfloat16)
        )
        leaving[level] = corrected(kept[level], level, level - 1)
        moving = copy(level)
        moving.start()
        if level + 1 < LEVELS:
            out = gather(tiles, rows[level + 1])
            for early in range(level):
                out = corrected(out, level + 1, early)
            kept[level + 1] = out
        if level == 2:
            relate(2)
            relate(3)
        if level == 3:
            settle(0, [0, 1, 2])
        moving.wait()

    def send(phase, source, target, count, peer):
        pltpu.make_async_remote_copy(
            src_ref=source.at[pl.ds(peer * count, count), :],
            dst_ref=target.at[pl.ds(me * count, count), :],
            send_sem=ssem.at[phase],
            recv_sem=rsem.at[phase],
            device_id=(gx, peer),
            device_id_type=MESH,
        ).start()

    def exchange(phase, source, target, count):
        for peer in order:
            send(phase, source, target, count, peer)
        return phase

    def finish(phase, source, target, count):
        here = pl.ds(me * count, count)
        target[here, :] = source[here, :]
        whole = pl.ds(0, (peers - 1) * count)
        pltpu.make_async_remote_copy(
            src_ref=source.at[whole, :],
            dst_ref=target.at[whole, :],
            send_sem=ssem.at[phase],
            recv_sem=rsem.at[phase],
            device_id=(gx, order[0]),
            device_id_type=MESH,
        ).wait()

    last = LEVELS - 1
    arrived = [landed[last, :, part * BLK : (part + 1) * BLK] for part in range(parts)]
    export_ids = jnp.full((1, BLK), -1, I32)
    for peer in order + [me]:
        for t in range(slots):
            block = exp_ref[0, t, peer]
            spot = jnp.broadcast_to(map_lane[1, pl.ds(block, 1), :], (CHAN, BLK))
            which = jnp.broadcast_to(map_part[1, pl.ds(block, 1), :], (CHAN, BLK))
            tile = tiles[block]
            for part in range(parts):
                turned = jnp.take_along_axis(arrived[part], spot, axis=1, mode="promise_in_bounds")
                tile = jnp.where(which == last * parts + part, turned, tile)
            stage[pl.ds(peer * (SENT * slots) + t, SENT, stride=slots), :] = tile[0:SENT]
            row = pl.ds(peer * slots + t, 1)
            stage_h[row, :] = tile[4:5]
            energies[row, :] = tile[5:6]
            stage_p[row, :] = tile[6:7]
            expcol[row, :] = jnp.full((1, BLK), block, I32)
            export_ids = jnp.where(wide_lane == peer * slots + t, block, export_ids)
        if peer is not me:
            send(0, stage, ghosts, SENT * slots, peer)
    sent_blocks = 0
    table[2:3, :] = export_ids
    settle(1, [last])
    compact()

    centres[...] = jnp.zeros_like(centres)
    for p in range(TOTACT):
        tile = tiles[act[2 * p]]
        centres[p * CHAN : p * CHAN + 7, :] = tile[0:7]
        centres[p * CHAN + 7 : p * CHAN + 8, :] = 0.5 / tile[4:5]
    cols[...] = jnp.transpose(centres[...])

    def sliced(q):
        return slice(q * PART, (q + 1) * PART)

    def local_row(block, channel):
        return tiles[block, channel : channel + 1, :]

    def ghost_base(ghost):
        return (ghost >> SLOT_BITS) * (SENT * slots) + (ghost & (slots - 1))

    def ghost_row(base, channel):
        return ghosts[pl.ds(base + channel * slots, 1), :]

    def separation(mine, theirs):
        dx, dy, dz = (a - b for a, b in zip(mine, theirs))
        square = dx * dx + dy * dy + dz * dz
        return square * lax.rsqrt(jnp.maximum(square, TINY))

    def density_term(r, inverse, mass5, mass4):
        fall = jnp.maximum(1.0 - r * inverse, 0.0)
        fall2 = fall * fall
        return (fall2 * fall2) * (mass5 - mass4 * fall)

    def pair_weight(r, smooth, mass, other_smooth, other_mass):
        inverse = 1.0 / (smooth + other_smooth)
        fall = jnp.maximum(1.0 - r * inverse, 0.0) * inverse
        return ((fall * fall) * fall * (inverse * inverse)) * (mass * other_mass)

    def local_first(p, _):
        others = [act[2 * p]] + [near[p * near_count + k] for k in range(near_count)]
        rows = [[local_row(b, c) for c in range(4)] for b in others]
        masses = [(5.0 * row[3], 4.0 * row[3]) for row in rows]
        for q in range(BLK // PART):
            here = sliced(q)
            chunk = cols[here, :]
            mine = [picked(chunk, p * CHAN + c) for c in (0, 1, 2, 3, 4, 7)]
            for c in range(6):
                wide[p, c, here, :] = mine[c]
            total = None
            for n, row in enumerate(rows):
                r = separation(mine[0:3], row[0:3])
                term = density_term(r, mine[5], *masses[n])
                total = term if total is None else total + term
                weights[p, n, here, :] = r
            sums[p, here, :] = total
        return 0

    lax.fori_loop(0, TOTACT, local_first, 0)
    finish(sent_blocks, stage, ghosts, SENT * slots)
    sent_h = exchange(1, stage_h, ghost_h, slots)

    def density_of(p):
        smooth = centres[pl.ds(p * CHAN + 4, 1), :]
        rhos[pl.ds(p, 1), :] = KERNEL_NORM / (smooth * smooth * smooth) * row_sums(sums[p])

    def ghost_first(p, _):
        others = [ghost_base(far[p * far_count + k]) for k in range(far_count)]
        rows = [[ghost_row(g, c) for c in range(4)] for g in others]
        masses = [(5.0 * row[3], 4.0 * row[3]) for row in rows]
        density_of(jnp.maximum(p - 1, 0))
        for q in range(BLK // PART):
            here = sliced(q)
            mine = [wide[p, c, here, :] for c in (0, 1, 2)]
            inverse = wide[p, 5, here, :]
            total = sums[p, here, :]
            for n, row in enumerate(rows):
                r = separation(mine, row[0:3])
                weights[p, 1 + near_count + n, here, :] = r
                total = total + density_term(r, inverse, *masses[n])
            sums[p, here, :] = total
        return 0

    lax.fori_loop(0, TOTACT, ghost_first, 0)
    density_of(TOTACT - 1)
    fresh = [rhos[p : p + 1, :] for p in range(TOTACT)]
    exported = stage_p[...]
    export_block = expcol[...]
    for p in range(TOTACT):
        exported = jnp.where(export_block == act[2 * p + 1], fresh[p], exported)
    stage_p[...] = FORCE_NORM * (energies[...] / exported)
    sent_p = exchange(2, stage_p, ghost_p, slots)

    block_number = lax.broadcasted_iota(I32, (blocks, BLK), 0)
    dens = tiles[:, 6, :]
    for p in range(TOTACT):
        dens = jnp.where(block_number == act[2 * p + 1], fresh[p], dens)
    dens_out[...] = dens
    pj[...] = FORCE_NORM * (tiles[:, 5, :] / dens)
    rhos[...] = jnp.zeros_like(rhos)
    for p in range(TOTACT):
        rhos[p : p + 1, :] = FORCE_NORM * (centres[p * CHAN + 5 : p * CHAN + 6, :] / fresh[p])
    cols[...] = jnp.transpose(rhos[...])
    adds[...] = jnp.zeros_like(adds)
    fars[...] = jnp.zeros_like(fars)

    def second(p, first, rows):
        for q in range(BLK // PART):
            here = sliced(q)
            mass, smooth = wide[p, 3, here, :], wide[p, 4, here, :]
            for n, row in enumerate(rows):
                r = weights[p, first + n, here, :]
                weights[p, first + n, here, :] = pair_weight(r, smooth, mass, row[1], row[0])

    def local_second(p, _):
        others = [act[2 * p]] + [near[p * near_count + k] for k in range(near_count)]
        second(p, 0, [[local_row(b, c) for c in (3, 4)] for b in others])
        for q in range(BLK // PART):
            here = sliced(q)
            wide[p, 5, here, :] = picked(cols[here, :], p)
        return 0

    def ghost_second(p, _):
        others = [far[p * far_count + k] for k in range(far_count)]
        second(p, 1 + near_count, [[ghost_row(ghost_base(g), 3), ghost_h[pl.ds(g, 1), :]] for g in others])
        return 0

    lax.fori_loop(0, TOTACT, local_second, 0)
    finish(sent_h, stage_h, ghost_h, slots)
    lax.fori_loop(0, TOTACT, ghost_second, 0)

    def force_phase(p, first, rows, skip, again):
        kept = len(rows) - skip
        carry = [None] * (3 * kept)
        for q in range(BLK // PART):
            here = sliced(q)
            mine = [wide[p, c, here, :] for c in (0, 1, 2)]
            pressure = wide[p, 5, here, :]
            total = [forces[c, p, here, :] for c in range(3)] if again else [None] * 3
            for n, row in enumerate(rows):
                weight = weights[p, first + n, here, :] * (pressure + row[3])
                for c in range(3):
                    push = weight * (mine[c] - row[c])
                    total[c] = push if total[c] is None else total[c] + push
                    if n >= skip:
                        at = (n - skip) * 3 + c
                        down = [push[8 * i : 8 * i + 8] for i in range(PART // 8)]
                        if carry[at] is not None:
                            down.append(carry[at])
                        while len(down) > 1:
                            down = down[2:] + [down[0] + down[1]]
                        carry[at] = down[0]
            for c in range(3):
                forces[c, p, here, :] = total[c]
        return [[-jnp.sum(carry[n * 3 + c], axis=0, keepdims=True) for c in range(3)] for n in range(kept)]

    finish(sent_p, stage_p, ghost_p, slots)

    def ghost_force(c):
        def body(p, _):
            others = [far[p * far_count + k] for k in range(far_count)]
            rows = [(ghost_row(ghost_base(g), c), ghost_p[pl.ds(g, 1), :] if c == 0 else None) for g in others]
            carry = [None] * far_count
            for q in range(BLK // PART):
                here = sliced(q)
                mine = wide[p, c, here, :]
                total = None
                for n, (row, pressure) in enumerate(rows):
                    weight = weights[p, 1 + near_count + n, here, :]
                    if c == 0:
                        weight = weight * (wide[p, 5, here, :] + pressure)
                        weights[p, 1 + near_count + n, here, :] = weight
                    push = weight * (mine - row)
                    total = push if total is None else total + push
                    down = [push[8 * i : 8 * i + 8] for i in range(PART // 8)]
                    if carry[n] is not None:
                        down.append(carry[n])
                    while len(down) > 1:
                        down = down[2:] + [down[0] + down[1]]
                    carry[n] = down[0]
                forces[c, p, here, :] = total
            for n in range(far_count):
                fars[c, pl.ds(p * far_count + n, 1), :] = -jnp.sum(carry[n], axis=0, keepdims=True)
            return 0

        lax.fori_loop(0, TOTACT, body, 0)

    for_ghosts = one_hot(table[1:2, :], ADDED, peers * slots)
    for c in range(3):
        ghost_force(c)
        back_stage[c] = placed_sum(for_ghosts, fars[c])
        exchange(3 + c, back_stage.at[c], back_land.at[c], slots)

    def centre_force(p):
        for c in range(3):
            adds[c, pl.ds(p, 1), :] = row_sums(forces[c, p])

    def local_force(p, _):
        others = [act[2 * p]] + [near[p * near_count + k] for k in range(near_count)]
        rows = [[local_row(b, c) for c in range(3)] + [pj[pl.ds(b, 1), :]] for b in others]
        centre_force(jnp.maximum(p - 1, 0))
        found = force_phase(p, 0, rows, 1, True)
        for n in range(near_count):
            for c in range(3):
                adds[c, pl.ds(TOTACT + p * near_count + n, 1), :] = found[n][c]
        return 0

    lax.fori_loop(0, TOTACT, local_force, 0)
    centre_force(TOTACT - 1)
    totals = placed_sum(one_hot(table[0:1, :], ADDED, blocks), abreast(adds))
    for_owners = one_hot(table[2:3, :], peers * slots, blocks)
    mass = tiles[:, 3, :]
    for c in range(3):
        finish(3 + c, back_stage.at[c], back_land.at[c], slots)
        total = totals[:, c * BLK : (c + 1) * BLK] + placed_sum(for_owners, back_land[c])
        force_out[c] = total / mass


def deliver_kernel(dens_ref, force_ref, dens_out, accel_out):
    dens_out[...] = dens_ref[...]

    def put(b8, _):
        for k in range(8):
            b = b8 * 8 + k
            for c in range(3):
                accel_out[c : c + 1, pl.ds(pl.multiple_of(b * BLK, BLK), BLK)] = force_ref[c, pl.ds(b, 1), :]
        return 0

    lax.fori_loop(0, dens_ref.shape[0] // 8, put, 0)


def shards(
    particles, mig_count, mig_rows, active_ids, active_count, local_nbrs, ghost_slots, export_blocks
):
    count = particles.shape[1]
    blocks = count // BLK
    width = mig_rows.shape[2]
    peers, slots = export_blocks.shape[1:]
    near_count, far_count = local_nbrs.shape[3], ghost_slots.shape[3]
    limit = 30 * 1024 * 1024
    struct = jax.ShapeDtypeStruct
    ghost_count = peers * slots
    square = VMEM((BLK, BLK), F32)
    each = VMEM((ghost_count, BLK), F32)
    tables = (
        mig_count, active_ids, active_count,
        local_nbrs.transpose(0, 3, 1, 2), ghost_slots.transpose(0, 1, 3, 2), export_blocks.transpose(0, 2, 1),
    )
    dens, force = pl.pallas_call(
        substep_kernel,
        name="substep",
        out_shape=(struct((blocks, BLK), F32), struct((3, blocks, BLK), F32)),
        in_specs=[spec(pltpu.HBM)] * 8,
        out_specs=(spec(VMEM),) * 2,
        scratch_shapes=[
            *(SMEM(given.shape, I32) for given in tables),
            VMEM(mig_rows.shape, I32),
            VMEM(particles.shape, F32),
            pltpu.SemaphoreType.DMA((8,)),
            VMEM((blocks, CHAN, BLK), F32),
            VMEM((LEVELS, CHAN, width), F32),
            VMEM((LEVELS, CHAN, width), F32),
            VMEM((6, width, width), jnp.bfloat16),
            VMEM((2, blocks, BLK), I32),
            VMEM((2, blocks, BLK), I32),
            VMEM((8, BLK), I32),
            SMEM((2 * TOTACT,), I32),
            SMEM((TOTACT * near_count,), I32),
            SMEM((TOTACT * far_count,), I32),
            VMEM((ghost_count * SENT, BLK), F32),
            each,
            each,
            each,
            VMEM((ghost_count, BLK), I32),
            VMEM((ghost_count * SENT, BLK), F32),
            each,
            each,
            VMEM((3, ghost_count, BLK), F32),
            VMEM((3, ghost_count, BLK), F32),
            square,
            square,
            VMEM((TOTACT, 6, BLK, BLK), F32),
            VMEM((TOTACT, BLK, BLK), F32),
            VMEM((TOTACT, 1 + near_count + far_count, BLK, BLK), F32),
            square,
            VMEM((blocks, BLK), F32),
            VMEM((3, ADDED, BLK), F32),
            VMEM((3, ADDED, BLK), F32),
            VMEM((3, TOTACT, BLK, BLK), F32),
            pltpu.SemaphoreType.DMA((LEVELS,)),
            pltpu.SemaphoreType.DMA((LEVELS,)),
            pltpu.SemaphoreType.DMA((6,)),
            pltpu.SemaphoreType.DMA((6,)),
        ],
        compiler_params=pltpu.CompilerParams(collective_id=0, has_side_effects=True, vmem_limit_bytes=limit),
    )(*(pltpu.with_memory_space_constraint(a, pltpu.HBM) for a in (*tables, mig_rows, particles)))
    density, accel = pl.pallas_call(
        deliver_kernel,
        name="deliver",
        out_shape=(struct((blocks, BLK), F32), struct((3, count), F32)),
        in_specs=[spec(VMEM)] * 2,
        out_specs=(spec(VMEM),) * 2,
        compiler_params=pltpu.CompilerParams(vmem_limit_bytes=limit),
    )(dens, force)
    return density.reshape(-1), accel


def solution(mesh):
    placed = (
        P(None, ("gx", "gy")),
        P(("gx", "gy"), None),
        P(("gx", "gy"), None, None),
        P(("gx", "gy"), None, None),
        P(("gx", "gy"), None),
        P(("gx", "gy"), None, None, None),
        P(("gx", "gy"), None, None, None),
        P(("gx", "gy"), None, None),
    )
    return jax.shard_map(
        shards,
        mesh=mesh,
        in_specs=placed,
        out_specs=(P(("gx", "gy")), P(None, ("gx", "gy"))),
        check_vma=False,
    )
```

```python
import functools
import math

import jax
import jax.numpy as jnp
from jax import lax
from jax.experimental import pallas as pl
from jax.experimental.pallas import tpu as pltpu
from jax.sharding import PartitionSpec as P

BLK = 128
TOTACT = 12
LEVELS = 4
CHAN = 8
SENT = 4
SLOT_BITS = 3
ADDED = 64
WHICH_MAP = (0, 0, 0, 1)

KERNEL_NORM = 21.0 / (16.0 * math.pi)
GAMMA_LESS = 2.0 / 3.0
FORCE_NORM = GAMMA_LESS * 32.0 * 5.0 * KERNEL_NORM
TINY = 1e-37
PART = 64
MESH = pl.DeviceIdType.MESH
VMEM = pltpu.VMEM
SMEM = pltpu.SMEM
F32 = jnp.float32
I32 = jnp.int32


def lanes(shape):
    return lax.broadcasted_iota(I32, shape, len(shape) - 1)


def spec(space):
    return pl.BlockSpec(memory_space=space)


def flipped(index, bit):
    return index + bit - 2 * bit * (lax.div(index, bit) % 2)


def picked(chunk, lane_number):
    return jnp.take_along_axis(
        chunk, jnp.full(chunk.shape, lane_number, I32), axis=1, mode="promise_in_bounds"
    )


def gather(tiles, rows):
    parts = []
    for part in range(rows.shape[1] // BLK):
        here = rows[:, part * BLK : (part + 1) * BLK]
        block = jnp.broadcast_to(here >> 7, (CHAN, BLK))
        spot = jnp.broadcast_to(here & 127, (CHAN, BLK))

        def step(n, held):
            held = list(held)
            for k in range(64):
                b = n * 64 + k
                tile = tiles[b]
                turned = jnp.take_along_axis(tile, spot, axis=1, mode="promise_in_bounds")
                held[k % 4] = jnp.where(block == b, turned, held[k % 4])
            return tuple(held)

        zero = jnp.zeros((CHAN, BLK), F32)
        held = lax.fori_loop(0, tiles.shape[0] // 64, step, (zero,) * 4)
        parts.append((held[0] + held[1]) + (held[2] + held[3]))
    return jnp.concatenate(parts, axis=1)


def pieces(value):
    first = value.astype(jnp.bfloat16).astype(F32)
    rest = value - first
    second = rest.astype(jnp.bfloat16).astype(F32)
    return first, second, rest - second


def abreast(ref):
    return jnp.concatenate([ref[0], ref[1], ref[2]], axis=1)


def row_sums(value):
    return jnp.sum(jnp.transpose(value), axis=0, keepdims=True)


def one_hot(ids, depth, count):
    owner = lax.broadcasted_iota(I32, (count, depth), 0)
    chosen = jnp.where(owner == ids[:, 0:depth], 1.0, 0.0)
    return jnp.concatenate([chosen] * 3, axis=1).astype(jnp.bfloat16)


def placed_sum(chosen, terms):
    split = jnp.concatenate(pieces(terms), axis=0).astype(jnp.bfloat16)
    return jnp.dot(chosen, split, preferred_element_type=F32)


def substep_kernel(
    *refs,
):
    given, (dens_out, force_out), refs = refs[0:8], refs[8:10], refs[10:]
    (
    count_ref, ids_ref, live_ref, near_ref, far_ref, exp_ref, rows_ref, x_ref, in_sem,
    tiles, leaving, landed, match, map_lane, map_part, table, act, near, far,
    stage, stage_h, stage_p, energies, expcol, ghosts, ghost_h, ghost_p, back_stage, back_land,
    centres, cols, wide, sums, weights, rhos, pj, adds, fars, forces,
    mig_ssem, mig_rsem, ssem, rsem,
    ) = refs
    held = (count_ref, ids_ref, live_ref, near_ref, far_ref, exp_ref, rows_ref, x_ref)
    fetches = [pltpu.make_async_copy(a, b, in_sem.at[n]) for n, (a, b) in enumerate(zip(given, held))]
    for fetch in reversed(fetches):
        fetch.start()
    gx, me = lax.axis_index("gx"), lax.axis_index("gy")
    peers = lax.axis_size("gy")
    slots = exp_ref.shape[1]
    width = rows_ref.shape[2]
    parts = width // BLK
    blocks = x_ref.shape[1] // BLK
    near_count, far_count = near_ref.shape[1], far_ref.shape[2]
    partners = [(flipped(gx, 2), me), (flipped(gx, 1), me), (gx, flipped(me, 2)), (gx, flipped(me, 1))]
    low, high = lax.rem(me, 4), lax.div(me, 4)
    across = flipped(low, 2)
    column = (across, flipped(across, 1), flipped(low, 1), low)
    order = [lax.rem(high + apart, peers // 4) * 4 + z for z in column for apart in (2, 1, 3, 0)][: peers - 1]
    around = [(gx, peer) for peer in order]

    barrier = pltpu.get_barrier_semaphore()
    for other in partners[0:2] + around:
        pl.semaphore_signal(barrier, inc=1, device_id=other, device_id_type=MESH)

    for fetch in reversed(fetches):
        fetch.wait()

    def load(b8, _):
        for k in range(8):
            b = b8 * 8 + k
            tiles[b, 0:7, :] = x_ref[:, pl.ds(pl.multiple_of(b * BLK, BLK), BLK)]
            tiles[b, 7:8, :] = jnp.zeros((1, BLK), F32)
        return 0

    lax.fori_loop(0, blocks // 8, load, 0)
    rows = [rows_ref[0, level : level + 1, :] for level in range(LEVELS)]
    leaving[0] = gather(tiles, rows[0])

    def copy(level):
        return pltpu.make_async_remote_copy(
            src_ref=leaving.at[level],
            dst_ref=landed.at[level],
            send_sem=mig_ssem.at[level],
            recv_sem=mig_rsem.at[level],
            device_id=partners[level],
            device_id_type=MESH,
        )

    pair = {}
    for early in range(LEVELS - 1):
        for late in range(early + 1, LEVELS):
            pair[late, early] = len(pair)

    def relate(early):
        keys = jnp.where(lanes((1, width)) < count_ref[0, early], rows[early], -1)
        lane = lanes((BLK, BLK))
        slot = lax.broadcasted_iota(I32, (BLK, BLK), 0)
        owner = lax.broadcasted_iota(I32, (blocks, width), 0)
        spots = []
        for part in range(parts):
            down = jnp.transpose(jnp.broadcast_to(keys[:, part * BLK : (part + 1) * BLK], (BLK, BLK)))
            hit = (down & 127) == lane
            spots.append(
                jnp.concatenate(
                    [jnp.where(hit, (slot + 1).astype(F32), 0.0), jnp.where(hit, float(part), 0.0)], axis=1
                ).astype(jnp.bfloat16)
            )
            down = jnp.concatenate([down] * parts, axis=1)
            for late in range(early + 1, LEVELS):
                match[pair[late, early], part * BLK : (part + 1) * BLK, :] = jnp.where(
                    down == rows[late], 1.0, 0.0
                ).astype(jnp.bfloat16)
        held = jnp.where(owner == (keys >> 7), 1.0, 0.0).astype(jnp.bfloat16)
        found = jnp.dot(held, jnp.concatenate(spots, axis=0), preferred_element_type=F32).astype(I32)
        arriving = found[:, 0:BLK] > 0
        spot = found[:, 0:BLK] - 1
        part = found[:, BLK:] + early * parts
        which = WHICH_MAP[early]
        if early in (1, 2):
            spot = jnp.where(arriving, spot, map_lane[which])
            part = jnp.where(arriving, part, map_part[which])
        else:
            spot = jnp.where(arriving, spot, 0)
            part = jnp.where(arriving, part, -1)
        map_lane[which] = spot
        map_part[which] = part

    def settle(which_map, levels):
        numbers = [level * parts + part for level in levels for part in range(parts)]
        arrived = {n: landed[n // parts, :, n % parts * BLK : (n % parts + 1) * BLK] for n in numbers}

        def step(b8, _):
            for k in range(8):
                b = b8 * 8 + k
                spot = jnp.broadcast_to(map_lane[which_map, pl.ds(b, 1), :], (CHAN, BLK))
                which = jnp.broadcast_to(map_part[which_map, pl.ds(b, 1), :], (CHAN, BLK))
                tile = tiles[b]
                for n in numbers:
                    turned = jnp.take_along_axis(arrived[n], spot, axis=1, mode="promise_in_bounds")
                    tile = jnp.where(which == n, turned, tile)
                tiles[b] = tile
            return 0

        lax.fori_loop(0, blocks // 8, step, 0)

    wide_lane = lanes((1, BLK))

    def compact():
        in_first = live_ref[0, 0]
        in_all = in_first + live_ref[0, 1]
        centre = jnp.full((1, BLK), -1, I32)
        distant = jnp.full((1, BLK), -1, I32)
        for p in range(TOTACT):
            n = jnp.where(p < in_first, 0, 1)
            i = jnp.minimum(jnp.where(p < in_first, p, p - in_first), ids_ref.shape[2] - 1)
            alive = p < in_all
            block = ids_ref[0, n, i]
            act[2 * p] = block
            act[2 * p + 1] = jnp.where(alive, block, -1)
            centre = jnp.where(wide_lane == p, jnp.where(alive, block, -1), centre)
            for k in range(near_count):
                other = near_ref[0, k, n, i]
                near[p * near_count + k] = other
                centre = jnp.where(
                    wide_lane == TOTACT + p * near_count + k, jnp.where(alive, other, -1), centre
                )
            for k in range(far_count):
                other = far_ref[0, n, k, i]
                far[p * far_count + k] = other
                distant = jnp.where(wide_lane == p * far_count + k, jnp.where(alive, other, -1), distant)
        table[0:1, :] = centre
        table[1:2, :] = distant
        table[3:8, :] = jnp.full((5, BLK), -1, I32)

    relate(0)
    pl.semaphore_wait(barrier, peers + 1)
    first = copy(0)
    first.start()
    kept = {1: gather(tiles, rows[1])}
    relate(1)
    first.wait()
    factors = []

    def corrected(out, level, early):
        found = jnp.dot(factors[early], match[pair[level, early]], preferred_element_type=F32)
        value = (found[0:8] + found[8:16]) + found[16:24]
        return jnp.where(found[24:32] > 0.5, value, out)

    for level in range(1, LEVELS):
        factors.append(
            jnp.concatenate([*pieces(landed[level - 1]), jnp.ones((8, width), F32)], axis=0).astype(jnp.bfloat16)
        )
        leaving[level] = corrected(kept[level], level, level - 1)
        moving = copy(level)
        moving.start()
        if level + 1 < LEVELS:
            out = gather(tiles, rows[level + 1])
            for early in range(level):
                out = corrected(out, level + 1, early)
            kept[level + 1] = out
        if level == 2:
            relate(2)
            relate(3)
        if level == 3:
            settle(0, [0, 1, 2])
        moving.wait()

    def send(phase, source, target, count, peer):
        pltpu.make_async_remote_copy(
            src_ref=source.at[pl.ds(peer * count, count), :],
            dst_ref=target.at[pl.ds(me * count, count), :],
            send_sem=ssem.at[phase],
            recv_sem=rsem.at[phase],
            device_id=(gx, peer),
            device_id_type=MESH,
        ).start()

    def exchange(phase, source, target, count):
        for peer in order:
            send(phase, source, target, count, peer)
        return phase

    def finish(phase, source, target, count):
        here = pl.ds(me * count, count)
        target[here, :] = source[here, :]
        whole = pl.ds(0, (peers - 1) * count)
        pltpu.make_async_remote_copy(
            src_ref=source.at[whole, :],
            dst_ref=target.at[whole, :],
            send_sem=ssem.at[phase],
            recv_sem=rsem.at[phase],
            device_id=(gx, order[0]),
            device_id_type=MESH,
        ).wait()

    last = LEVELS - 1
    arrived = [landed[last, :, part * BLK : (part + 1) * BLK] for part in range(parts)]
    export_ids = jnp.full((1, BLK), -1, I32)
    for peer in order + [me]:
        for t in range(slots):
            block = exp_ref[0, t, peer]
            spot = jnp.broadcast_to(map_lane[1, pl.ds(block, 1), :], (CHAN, BLK))
            which = jnp.broadcast_to(map_part[1, pl.ds(block, 1), :], (CHAN, BLK))
            tile = tiles[block]
            for part in range(parts):
                turned = jnp.take_along_axis(arrived[part], spot, axis=1, mode="promise_in_bounds")
                tile = jnp.where(which == last * parts + part, turned, tile)
            stage[pl.ds(peer * (SENT * slots) + t, SENT, stride=slots), :] = tile[0:SENT]
            row = pl.ds(peer * slots + t, 1)
            stage_h[row, :] = tile[4:5]
            energies[row, :] = tile[5:6]
            stage_p[row, :] = tile[6:7]
            expcol[row, :] = jnp.full((1, BLK), block, I32)
            export_ids = jnp.where(wide_lane == peer * slots + t, block, export_ids)
        if peer is not me:
            send(0, stage, ghosts, SENT * slots, peer)
    sent_blocks = 0
    table[2:3, :] = export_ids
    settle(1, [last])
    compact()

    centres[...] = jnp.zeros_like(centres)
    for p in range(TOTACT):
        tile = tiles[act[2 * p]]
        centres[p * CHAN : p * CHAN + 7, :] = tile[0:7]
        centres[p * CHAN + 7 : p * CHAN + 8, :] = 0.5 / tile[4:5]
    cols[...] = jnp.transpose(centres[...])

    def sliced(q):
        return slice(q * PART, (q + 1) * PART)

    def local_row(block, channel):
        return tiles[block, channel : channel + 1, :]

    def ghost_base(ghost):
        return (ghost >> SLOT_BITS) * (SENT * slots) + (ghost & (slots - 1))

    def ghost_row(base, channel):
        return ghosts[pl.ds(base + channel * slots, 1), :]

    def separation(mine, theirs):
        dx, dy, dz = (a - b for a, b in zip(mine, theirs))
        square = dx * dx + dy * dy + dz * dz
        return square * lax.rsqrt(jnp.maximum(square, TINY))

    def density_term(r, inverse, mass5, mass4):
        fall = jnp.maximum(1.0 - r * inverse, 0.0)
        fall2 = fall * fall
        return (fall2 * fall2) * (mass5 - mass4 * fall)

    def pair_weight(r, smooth, mass, other_smooth, other_mass):
        inverse = 1.0 / (smooth + other_smooth)
        fall = jnp.maximum(1.0 - r * inverse, 0.0) * inverse
        return ((fall * fall) * fall * (inverse * inverse)) * (mass * other_mass)

    def local_first(p, _):
        others = [act[2 * p]] + [near[p * near_count + k] for k in range(near_count)]
        rows = [[local_row(b, c) for c in range(4)] for b in others]
        masses = [(5.0 * row[3], 4.0 * row[3]) for row in rows]
        for q in range(BLK // PART):
            here = sliced(q)
            chunk = cols[here, :]
            mine = [picked(chunk, p * CHAN + c) for c in (0, 1, 2, 3, 4, 7)]
            for c in range(6):
                wide[p, c, here, :] = mine[c]
            total = None
            for n, row in enumerate(rows):
                r = separation(mine[0:3], row[0:3])
                term = density_term(r, mine[5], *masses[n])
                total = term if total is None else total + term
                weights[p, n, here, :] = r
            sums[p, here, :] = total
        return 0

    lax.fori_loop(0, TOTACT, local_first, 0)
    finish(sent_blocks, stage, ghosts, SENT * slots)
    sent_h = exchange(1, stage_h, ghost_h, slots)

    def density_of(p):
        smooth = centres[pl.ds(p * CHAN + 4, 1), :]
        rhos[pl.ds(p, 1), :] = KERNEL_NORM / (smooth * smooth * smooth) * row_sums(sums[p])

    def ghost_first(p, _):
        others = [ghost_base(far[p * far_count + k]) for k in range(far_count)]
        rows = [[ghost_row(g, c) for c in range(4)] for g in others]
        masses = [(5.0 * row[3], 4.0 * row[3]) for row in rows]
        density_of(jnp.maximum(p - 1, 0))
        for q in range(BLK // PART):
            here = sliced(q)
            mine = [wide[p, c, here, :] for c in (0, 1, 2)]
            inverse = wide[p, 5, here, :]
            total = sums[p, here, :]
            for n, row in enumerate(rows):
                r = separation(mine, row[0:3])
                weights[p, 1 + near_count + n, here, :] = r
                total = total + density_term(r, inverse, *masses[n])
            sums[p, here, :] = total
        return 0

    lax.fori_loop(0, TOTACT, ghost_first, 0)
    density_of(TOTACT - 1)
    fresh = [rhos[p : p + 1, :] for p in range(TOTACT)]
    exported = stage_p[...]
    export_block = expcol[...]
    for p in range(TOTACT):
        exported = jnp.where(export_block == act[2 * p + 1], fresh[p], exported)
    stage_p[...] = FORCE_NORM * (energies[...] / exported)
    sent_p = exchange(2, stage_p, ghost_p, slots)

    block_number = lax.broadcasted_iota(I32, (blocks, BLK), 0)
    dens = tiles[:, 6, :]
    for p in range(TOTACT):
        dens = jnp.where(block_number == act[2 * p + 1], fresh[p], dens)
    dens_out[...] = dens
    pj[...] = FORCE_NORM * (tiles[:, 5, :] / dens)
    rhos[...] = jnp.zeros_like(rhos)
    for p in range(TOTACT):
        rhos[p : p + 1, :] = FORCE_NORM * (centres[p * CHAN + 5 : p * CHAN + 6, :] / fresh[p])
    cols[...] = jnp.transpose(rhos[...])
    adds[...] = jnp.zeros_like(adds)
    fars[...] = jnp.zeros_like(fars)

    def second(p, first, rows):
        for q in range(BLK // PART):
            here = sliced(q)
            mass, smooth = wide[p, 3, here, :], wide[p, 4, here, :]
            for n, row in enumerate(rows):
                r = weights[p, first + n, here, :]
                weights[p, first + n, here, :] = pair_weight(r, smooth, mass, row[1], row[0])

    def local_second(p, _):
        others = [act[2 * p]] + [near[p * near_count + k] for k in range(near_count)]
        second(p, 0, [[local_row(b, c) for c in (3, 4)] for b in others])
        for q in range(BLK // PART):
            here = sliced(q)
            wide[p, 5, here, :] = picked(cols[here, :], p)
        return 0

    def ghost_second(p, _):
        others = [far[p * far_count + k] for k in range(far_count)]
        second(p, 1 + near_count, [[ghost_row(ghost_base(g), 3), ghost_h[pl.ds(g, 1), :]] for g in others])
        return 0

    lax.fori_loop(0, TOTACT, local_second, 0)
    finish(sent_h, stage_h, ghost_h, slots)
    lax.fori_loop(0, TOTACT, ghost_second, 0)

    def force_phase(p, first, rows, skip, again):
        kept = len(rows) - skip
        carry = [None] * (3 * kept)
        for q in range(BLK // PART):
            here = sliced(q)
            mine = [wide[p, c, here, :] for c in (0, 1, 2)]
            pressure = wide[p, 5, here, :]
            total = [forces[c, p, here, :] for c in range(3)] if again else [None] * 3
            for n, row in enumerate(rows):
                weight = weights[p, first + n, here, :] * (pressure + row[3])
                for c in range(3):
                    push = weight * (mine[c] - row[c])
                    total[c] = push if total[c] is None else total[c] + push
                    if n >= skip:
                        at = (n - skip) * 3 + c
                        down = [push[8 * i : 8 * i + 8] for i in range(PART // 8)]
                        if carry[at] is not None:
                            down.append(carry[at])
                        while len(down) > 1:
                            down = down[2:] + [down[0] + down[1]]
                        carry[at] = down[0]
            for c in range(3):
                forces[c, p, here, :] = total[c]
        return [[-jnp.sum(carry[n * 3 + c], axis=0, keepdims=True) for c in range(3)] for n in range(kept)]

    finish(sent_p, stage_p, ghost_p, slots)

    def ghost_force(c):
        def body(p, _):
            others = [far[p * far_count + k] for k in range(far_count)]
            rows = [(ghost_row(ghost_base(g), c), ghost_p[pl.ds(g, 1), :] if c == 0 else None) for g in others]
            carry = [None] * far_count
            for q in range(BLK // PART):
                here = sliced(q)
                mine = wide[p, c, here, :]
                total = None
                for n, (row, pressure) in enumerate(rows):
                    weight = weights[p, 1 + near_count + n, here, :]
                    if c == 0:
                        weight = weight * (wide[p, 5, here, :] + pressure)
                        weights[p, 1 + near_count + n, here, :] = weight
                    push = weight * (mine - row)
                    total = push if total is None else total + push
                    down = [push[8 * i : 8 * i + 8] for i in range(PART // 8)]
                    if carry[n] is not None:
                        down.append(carry[n])
                    while len(down) > 1:
                        down = down[2:] + [down[0] + down[1]]
                    carry[n] = down[0]
                forces[c, p, here, :] = total
            for n in range(far_count):
                fars[c, pl.ds(p * far_count + n, 1), :] = -jnp.sum(carry[n], axis=0, keepdims=True)
            return 0

        lax.fori_loop(0, TOTACT, body, 0)

    for_ghosts = one_hot(table[1:2, :], ADDED, peers * slots)
    for c in range(3):
        ghost_force(c)
        back_stage[c] = placed_sum(for_ghosts, fars[c])
        exchange(3 + c, back_stage.at[c], back_land.at[c], slots)

    def centre_force(p):
        for c in range(3):
            adds[c, pl.ds(p, 1), :] = row_sums(forces[c, p])

    def local_force(p, _):
        others = [act[2 * p]] + [near[p * near_count + k] for k in range(near_count)]
        rows = [[local_row(b, c) for c in range(3)] + [pj[pl.ds(b, 1), :]] for b in others]
        centre_force(jnp.maximum(p - 1, 0))
        found = force_phase(p, 0, rows, 1, True)
        for n in range(near_count):
            for c in range(3):
                adds[c, pl.ds(TOTACT + p * near_count + n, 1), :] = found[n][c]
        return 0

    lax.fori_loop(0, TOTACT, local_force, 0)
    centre_force(TOTACT - 1)
    totals = placed_sum(one_hot(table[0:1, :], ADDED, blocks), abreast(adds))
    for_owners = one_hot(table[2:3, :], peers * slots, blocks)
    mass = tiles[:, 3, :]
    for c in range(3):
        finish(3 + c, back_stage.at[c], back_land.at[c], slots)
        total = totals[:, c * BLK : (c + 1) * BLK] + placed_sum(for_owners, back_land[c])
        force_out[c] = total / mass


def deliver_kernel(dens_ref, force_ref, dens_out, accel_out):
    dens_out[...] = dens_ref[...]

    def put(b8, _):
        for k in range(8):
            b = b8 * 8 + k
            for c in range(3):
                accel_out[c : c + 1, pl.ds(pl.multiple_of(b * BLK, BLK), BLK)] = force_ref[c, pl.ds(b, 1), :]
        return 0

    lax.fori_loop(0, dens_ref.shape[0] // 8, put, 0)


def shards(
    particles, mig_count, mig_rows, active_ids, active_count, local_nbrs, ghost_slots, export_blocks
):
    count = particles.shape[1]
    blocks = count // BLK
    width = mig_rows.shape[2]
    peers, slots = export_blocks.shape[1:]
    near_count, far_count = local_nbrs.shape[3], ghost_slots.shape[3]
    limit = 30 * 1024 * 1024
    struct = jax.ShapeDtypeStruct
    ghost_count = peers * slots
    square = VMEM((BLK, BLK), F32)
    each = VMEM((ghost_count, BLK), F32)
    tables = (
        mig_count, active_ids, active_count,
        local_nbrs.transpose(0, 3, 1, 2), ghost_slots.transpose(0, 1, 3, 2), export_blocks.transpose(0, 2, 1),
    )
    dens, force = pl.pallas_call(
        substep_kernel,
        name="substep",
        out_shape=(struct((blocks, BLK), F32), struct((3, blocks, BLK), F32)),
        in_specs=[spec(pltpu.HBM)] * 8,
        out_specs=(spec(VMEM),) * 2,
        scratch_shapes=[
            *(SMEM(given.shape, I32) for given in tables),
            VMEM(mig_rows.shape, I32),
            VMEM(particles.shape, F32),
            pltpu.SemaphoreType.DMA((8,)),
            VMEM((blocks, CHAN, BLK), F32),
            VMEM((LEVELS, CHAN, width), F32),
            VMEM((LEVELS, CHAN, width), F32),
            VMEM((6, width, width), jnp.bfloat16),
            VMEM((2, blocks, BLK), I32),
            VMEM((2, blocks, BLK), I32),
            VMEM((8, BLK), I32),
            SMEM((2 * TOTACT,), I32),
            SMEM((TOTACT * near_count,), I32),
            SMEM((TOTACT * far_count,), I32),
            VMEM((ghost_count * SENT, BLK), F32),
            each,
            each,
            each,
            VMEM((ghost_count, BLK), I32),
            VMEM((ghost_count * SENT, BLK), F32),
            each,
            each,
            VMEM((3, ghost_count, BLK), F32),
            VMEM((3, ghost_count, BLK), F32),
            square,
            square,
            VMEM((TOTACT, 6, BLK, BLK), F32),
            VMEM((TOTACT, BLK, BLK), F32),
            VMEM((TOTACT, 1 + near_count + far_count, BLK, BLK), F32),
            square,
            VMEM((blocks, BLK), F32),
            VMEM((3, ADDED, BLK), F32),
            VMEM((3, ADDED, BLK), F32),
            VMEM((3, TOTACT, BLK, BLK), F32),
            pltpu.SemaphoreType.DMA((LEVELS,)),
            pltpu.SemaphoreType.DMA((LEVELS,)),
            pltpu.SemaphoreType.DMA((6,)),
            pltpu.SemaphoreType.DMA((6,)),
        ],
        compiler_params=pltpu.CompilerParams(collective_id=0, has_side_effects=True, vmem_limit_bytes=limit),
    )(*(pltpu.with_memory_space_constraint(a, pltpu.HBM) for a in (*tables, mig_rows, particles)))
    density, accel = pl.pallas_call(
        deliver_kernel,
        name="deliver",
        out_shape=(struct((blocks, BLK), F32), struct((3, count), F32)),
        in_specs=[spec(VMEM)] * 2,
        out_specs=(spec(VMEM),) * 2,
        compiler_params=pltpu.CompilerParams(vmem_limit_bytes=limit),
    )(dens, force)
    return density.reshape(-1), accel


def solution(mesh):
    placed = (
        P(None, ("gx", "gy")),
        P(("gx", "gy"), None),
        P(("gx", "gy"), None, None),
        P(("gx", "gy"), None, None),
        P(("gx", "gy"), None),
        P(("gx", "gy"), None, None, None),
        P(("gx", "gy"), None, None, None),
        P(("gx", "gy"), None, None),
    )
    return jax.shard_map(
        shards,
        mesh=mesh,
        in_specs=placed,
        out_specs=(P(("gx", "gy")), P(None, ("gx", "gy"))),
        check_vma=False,
    )
```
